32 devices in a mesh: groups: 2 (over x), seq: 16 (over z, y, core).
Axes of the slice: x: 2, y: 2, z: 4, core: 2. Of those that a mesh axis runs over, the one named last changes fastest.
Arguments:
- hidden: bfloat16 [4096, 8192], P(('groups', 'seq')), parts along dimension 0, may hold values from -6 to 6
- q_base: bfloat16 [4096, 8192], P(('groups', 'seq')), parts along dimension 0, may hold values from -8 to 8
- base_key_weight: bfloat16 [4096, 1024], P(('groups', 'seq')), parts along dimension 0, may hold values from -8 to 8
- base_value_weight: bfloat16 [4096, 1024], P(('groups', 'seq')), parts along dimension 0, may hold values from -6 to 6
- shrink_a: bfloat16 [32, 8192, 192], P('groups', 'seq'), parts along dimension 0, may hold values from -0.0625 to 0.0625
- expand_q: bfloat16 [32, 64, 8192], P('groups', None, 'seq'), parts along dimension 0, may hold values from -0.375 to 0.375
- key_value_up_weight: bfloat16 [32, 64, 2048], P('groups'), parts along dimension 0, may hold values from -0.375 to 0.375
- block_request: int32 [64], P('groups'), parts along dimension 0, may hold values from 0 to 7, never falling along the last dimension, each value on 1 to 16 neighbouring positions
- request_adapter: int32 [16], P('groups'), parts along dimension 0, may hold values from 0 to 15
Outputs:
- attended: bfloat16 [4096, 8192], P(('groups', 'seq')), parts along dimension 0
The draws below stay inside these ranges and needn't reach their ends.
There are 2 independent parts, one for each index of `groups`. The reference program is written for one: setup_inputs(seed, part) draws one part's arguments, and reference() takes and returns one part's arrays. A program takes and returns all parts, laid end to end along the dimension named above; each array names one. Nothing has to cross between parts.
Inputs may be any that keep to these rules, and one draw needn't show every extreme that they name: `block_request`: each request holds 1 to 16 consecutive blocks, request numbers never fall along the blocks, and some request holds exactly 16 blocks.
All inputs are finite; a program needn't handle non-finite values.
Results may differ from the reference program's by a relative error of at most 0.012.
The reference program's roundings to bfloat16 on the way count: a program that leaves them out, or rounds other values in their place, can miss the bound.
Values may be sent and summed in bfloat16 or wider, within the bound.
No kernel may reach another device: no remote copies, remote signals or barrier semaphores. Data moves between devices by JAX's collectives and lax.ppermute only.
A program may use at most 128 MiB of HBM per device.

```python
import math
import jax
import jax.numpy as jnp
import numpy as np
from jax import lax

D = 8192
QUERY_HEADS = 64
KEY_VALUE_HEADS = 8
HEAD_SIZE = 128
ADAPTER_RANK = 64
ADAPTER_TOTAL = 16
BLK = 64
QBLK = 512
TOKEN_COUNT = 2048
NBLK = 32
MOSTB = 16
REQS = 8
KWIN = 1536


def draw_q_base(key, part):
    base_projection = jax.random.normal(jax.random.fold_in(key, 1), (TOKEN_COUNT, QUERY_HEADS * HEAD_SIZE), jnp.float32)
    base_projection = jnp.clip(base_projection, -8.0, 8.0)
    return base_projection.astype(jnp.bfloat16)


def draw_base_key_weight(key, part):
    base_projection = jax.random.normal(jax.random.fold_in(key, 2), (TOKEN_COUNT, KEY_VALUE_HEADS * HEAD_SIZE), jnp.float32)
    base_projection = jnp.clip(base_projection, -8.0, 8.0)
    return base_projection.astype(jnp.bfloat16)


def place_ends(array, own_key, smallest, high):
    longest = array.shape.index(max(array.shape))
    spots = []
    for shift in (0, 1):
        where = [jax.random.randint(jax.random.fold_in(own_key, axis), (), 0, length) for axis, length in enumerate(array.shape)]
        where[longest] = (where[longest] + shift) % array.shape[longest]
        spots.append(tuple(where))
    return array.at[spots[0]].set(smallest).at[spots[1]].set(high)


def steps_of(key, dims, pieces, smallest, high):
    def one(axis_at, blocks):
        steps = jax.random.uniform(jax.random.fold_in(jax.random.fold_in(key, 6), axis_at), (blocks,), jnp.float32, smallest / len(pieces), high / len(pieces))
        return jnp.repeat(jnp.exp(steps), dims[axis_at] // blocks).reshape((-1,) + (1,) * (len(dims) - axis_at - 1))

    gain = one(*pieces[0])
    for cut in pieces[1:]:
        gain = gain * one(*cut)
    return gain


def rank_bounds(number_of, slope):
    weights = [(1 << 20) // math.isqrt(standing ** slope) + 1 for standing in range(1, number_of + 1)]
    deviation = 1 + sum(weights) // (1 << 30)
    return np.cumsum(np.array([max(1, weight // deviation) for weight in weights]))


def ranked_ids(key, shape, number_of, lean):
    table = rank_bounds(number_of, lean)
    lot = jax.random.randint(jax.random.fold_in(key, 1), shape, 0, int(table[number_of - 1]))
    rank = jnp.searchsorted(jnp.asarray(table, jnp.int32), lot, side="right")
    return jax.random.permutation(jax.random.fold_in(key, 2), number_of)[rank].astype(jnp.int32)


def length_profile(amount, total, reach, slope):
    weights = [(1 << 20) // math.isqrt(standing ** slope) + 1 for standing in range(2, amount + 1)]
    spare, counts = total - reach - (amount - 1), [1] * (amount - 1)
    while spare > 0:
        free = [i for i in range(amount - 1) if counts[i] < reach]
        whole, budget = sum([weights[i] for i in free]), spare
        for i in free:
            extra = min(reach - counts[i], max(1, budget * weights[i] // whole), spare)
            counts[i] = counts[i] + extra
            spare = spare - extra
    return np.array([reach] + counts)


def ragged(key, count, total, most, lean):
    if count == 2:
        one = jax.random.randint(key, (), max(1, total - most), min(most, total - 1) + 1)
        return jnp.stack([one, total - one])
    tallies = jnp.asarray(length_profile(count, total, most, lean), jnp.int32)
    couples = (count - 1) // 2
    source_of, receiver = tallies[1:1 + 2 * couples:2], tallies[2:2 + 2 * couples:2]
    room = jnp.minimum(source_of - 1, most - receiver)
    passed = jax.random.randint(jax.random.fold_in(key, 1), (couples,), 0, 1 << 20) % (room + 1)
    tallies = tallies.at[1:1 + 2 * couples:2].set(source_of - passed).at[2:2 + 2 * couples:2].set(receiver + passed)
    return tallies[jax.random.permutation(jax.random.fold_in(key, 2), count)]


def noise(key, extent, spread, reach, split=(), kind=jnp.bfloat16):
    drawn = jax.random.normal(key, extent, jnp.float32) * spread
    if len(split) > 0:
        drawn = steps_of(key, extent, split, -0.22, 0.18) * drawn
    return jnp.clip(drawn, min=-reach, max=reach).astype(kind)


def setup_inputs(seed: int = 0, part: int = 0) -> dict:
    key_of = jax.random.split(jax.random.key(seed), 10)
    part_splits = jax.random.split(jax.random.fold_in(key_of[9], part), 10)
    return {
        "hidden": noise(part_splits[0], (TOKEN_COUNT, D), 1.0, 6.0, ((0, 16),)),
        "q_base": draw_q_base(jax.random.fold_in(jax.random.fold_in(key_of[9], part), 71), part),
        "base_key_weight": draw_base_key_weight(jax.random.fold_in(jax.random.fold_in(key_of[9], part), 71), part),
        "base_value_weight": noise(part_splits[3], (TOKEN_COUNT, KEY_VALUE_HEADS * HEAD_SIZE), 1.0, 6.0, ((0, 16),)),
        "shrink_a": noise(part_splits[4], (ADAPTER_TOTAL, D, 3 * ADAPTER_RANK), D ** -0.5, 0.0625, ((1, 16),)),
        "expand_q": noise(part_splits[5], (ADAPTER_TOTAL, ADAPTER_RANK, QUERY_HEADS * HEAD_SIZE), (4 * ADAPTER_RANK) ** -0.5, 0.375, ((2, 16),)),
        "key_value_up_weight": noise(part_splits[6], (ADAPTER_TOTAL, ADAPTER_RANK, 2 * KEY_VALUE_HEADS * HEAD_SIZE), (4 * ADAPTER_RANK) ** -0.5, 0.375),
        "block_request": jnp.searchsorted(jnp.cumsum(ragged(part_splits[7], REQS, NBLK, MOSTB, 2)), jnp.arange(NBLK), side="right").astype(jnp.int32),
        "request_adapter": place_ends(ranked_ids(part_splits[8], (REQS,), ADAPTER_TOTAL, 2), jax.random.fold_in(part_splits[8], 3), 0, ADAPTER_TOTAL - 1).astype(jnp.int32),
    }


def reference(hidden, q_base, base_key_weight, base_value_weight, shrink_a, expand_q, key_value_up_weight, block_request, request_adapter):
    adapter_of = request_adapter[block_request].astype(jnp.int32)
    hidden_blocks = hidden.reshape(NBLK, BLK, D)

    def shrink_block(pair_in):
        block_rows, adapter_id = pair_in
        return jnp.dot(block_rows, shrink_a[adapter_id], preferred_element_type=jnp.float32).astype(jnp.bfloat16)
    shrunk = lax.map(shrink_block, (hidden_blocks, adapter_of))
    key_value_width = KEY_VALUE_HEADS * HEAD_SIZE

    def expand_block(group_in):
        low_rows, adapter_id, q_rows, k_rows, v_rows = group_in
        kv_table = key_value_up_weight[adapter_id]
        q_delta = jnp.dot(low_rows[:, :ADAPTER_RANK], expand_q[adapter_id], preferred_element_type=jnp.float32)
        k_delta = jnp.dot(low_rows[:, ADAPTER_RANK:2 * ADAPTER_RANK], kv_table[:, :key_value_width], preferred_element_type=jnp.float32)
        v_delta = jnp.dot(low_rows[:, 2 * ADAPTER_RANK:], kv_table[:, key_value_width:], preferred_element_type=jnp.float32)
        q_new = (q_rows.astype(jnp.float32) + q_delta).astype(jnp.bfloat16)
        k_new = (k_rows.astype(jnp.float32) + k_delta).astype(jnp.bfloat16)
        v_new = (v_rows.astype(jnp.float32) + v_delta).astype(jnp.bfloat16)
        return (q_new, k_new, v_new)
    query_rows, key_rows, value_rows = lax.map(expand_block, (shrunk, adapter_of, q_base.reshape(NBLK, BLK, QUERY_HEADS * HEAD_SIZE), base_key_weight.reshape(NBLK, BLK, key_value_width), base_value_weight.reshape(NBLK, BLK, key_value_width)))
    query_group_width = QUERY_HEADS // KEY_VALUE_HEADS
    query_rows = query_rows.reshape(TOKEN_COUNT, KEY_VALUE_HEADS, query_group_width, HEAD_SIZE)
    key_rows = key_rows.reshape(TOKEN_COUNT, KEY_VALUE_HEADS, HEAD_SIZE)
    value_rows = value_rows.reshape(TOKEN_COUNT, KEY_VALUE_HEADS, HEAD_SIZE)
    request_of = jnp.repeat(block_request, BLK)
    score_scale = 1.0 / math.sqrt(HEAD_SIZE)

    def attend(block_index):
        q_start = (block_index * QBLK).astype(jnp.int32)
        k_start = jnp.clip(q_start + QBLK - KWIN, 0, TOKEN_COUNT - KWIN).astype(jnp.int32)
        q_rows = lax.dynamic_slice_in_dim(query_rows, q_start, QBLK, 0).astype(jnp.float32)
        k_rows = lax.dynamic_slice_in_dim(key_rows, k_start, KWIN, 0).astype(jnp.float32)
        v_rows = lax.dynamic_slice_in_dim(value_rows, k_start, KWIN, 0).astype(jnp.float32)
        q_request = lax.dynamic_slice_in_dim(request_of, q_start, QBLK, 0)
        k_request = lax.dynamic_slice_in_dim(request_of, k_start, KWIN, 0)
        q_pos = q_start + jnp.arange(QBLK, dtype=jnp.int32)
        k_pos = k_start + jnp.arange(KWIN, dtype=jnp.int32)
        allowed = (k_pos[None, :] <= q_pos[:, None]) & (k_request[None, :] == q_request[:, None])
        scores = jnp.einsum('qagd,kad->agqk', q_rows, k_rows) * score_scale
        scores = jnp.where(allowed[None, None], scores, -1e+30)
        row_max = lax.optimization_barrier(jnp.max(scores, axis=-1, keepdims=True))
        weights = jnp.exp(scores - row_max)
        probs = (weights / lax.optimization_barrier(jnp.sum(weights, axis=-1, keepdims=True))).astype(jnp.bfloat16)
        result = jnp.einsum('agqk,kad->qagd', probs.astype(jnp.float32), v_rows)
        return result.astype(jnp.bfloat16).reshape(QBLK, QUERY_HEADS * HEAD_SIZE)
    blocks_out = lax.map(attend, jnp.arange(TOKEN_COUNT // QBLK, dtype=jnp.int32))
    return blocks_out.reshape(TOKEN_COUNT, QUERY_HEADS * HEAD_SIZE)
```

```python
import functools
import math

import jax
import jax.numpy as jnp
from jax import lax
from jax.experimental import pallas as pl
from jax.experimental.pallas import tpu as pltpu
from jax.sharding import PartitionSpec as P

KEY_VALUE_HEADS = 8
HEAD_SIZE = 128
ADAPTER_RANK = 64
MOST_BLOCKS_CAP = 32
KEY_CHUNK = 256
NT = (((1,), (1,)), ((), ()))
TN = (((0,), (0,)), ((), ()))


def shrink_kernel(block_len, request_ref, adapter_ref, rows_ref, down_ref, out_ref):
    sources, tokens, _ = rows_ref.shape
    per_device = tokens // block_len
    first = pl.program_id(0) * (sources * per_device)
    for source in range(sources):
        for part in range(per_device):
            adapter = adapter_ref[request_ref[first + source * per_device + part]]
            span = pl.ds(part * block_len, block_len)
            out_ref[source, span, :] = lax.dot_general(
                rows_ref[source, span, :], down_ref[adapter], NT, preferred_element_type=jnp.float32
            ).astype(out_ref.dtype)


def shrink(rows, down, block_request, request_adapter, block_len):
    devices, tokens, features = rows.shape
    adapters, width, _ = down.shape
    steps = min(4, devices)
    sources = devices // steps
    return pl.pallas_call(
        functools.partial(shrink_kernel, block_len),
        out_shape=jax.ShapeDtypeStruct((devices, tokens, width), jnp.bfloat16),
        grid_spec=pltpu.PrefetchScalarGridSpec(
            num_scalar_prefetch=2,
            grid=(steps,),
            in_specs=[
                pl.BlockSpec((sources, tokens, features), lambda i, br, ra: (i, 0, 0)),
                pl.BlockSpec((adapters, width, features), lambda i, br, ra: (0, 0, 0)),
            ],
            out_specs=pl.BlockSpec((sources, tokens, width), lambda i, br, ra: (i, 0, 0)),
        ),
        name="shrink",
    )(block_request, request_adapter, rows, down)


def update_kernel(place_ref, request_ref, adapter_ref, part_ref, key_ref, value_ref, up_ref, kv_ref, low_ref):
    rank = ADAPTER_RANK
    width = key_ref.shape[1]
    low = jnp.sum(part_ref[...].astype(jnp.float32), axis=0).astype(jnp.bfloat16)
    low_ref[...] = low[:, :rank]
    key_delta = jnp.dot(low[:, rank : 2 * rank], up_ref[0, :, :width], preferred_element_type=jnp.float32)
    kv_ref[:, :width] = (key_ref[...].astype(jnp.float32) + key_delta).astype(kv_ref.dtype)
    value_delta = jnp.dot(low[:, 2 * rank :], up_ref[0, :, width:], preferred_element_type=jnp.float32)
    kv_ref[:, width:] = (value_ref[...].astype(jnp.float32) + value_delta).astype(kv_ref.dtype)


def update(partials, base_key, base_value, up_weight, place, block_request, request_adapter, block_len):
    devices, tokens, width = partials.shape
    kv_width = base_key.shape[1]
    per_device = tokens // block_len
    return pl.pallas_call(
        update_kernel,
        out_shape=(
            jax.ShapeDtypeStruct((tokens, 2 * kv_width), jnp.bfloat16),
            jax.ShapeDtypeStruct((tokens, ADAPTER_RANK), jnp.bfloat16),
        ),
        grid_spec=pltpu.PrefetchScalarGridSpec(
            num_scalar_prefetch=3,
            grid=(per_device,),
            in_specs=[
                pl.BlockSpec((devices, block_len, width), lambda i, me, br, ra: (0, i, 0)),
                pl.BlockSpec((block_len, kv_width), lambda i, me, br, ra: (i, 0)),
                pl.BlockSpec((block_len, kv_width), lambda i, me, br, ra: (i, 0)),
                pl.BlockSpec(
                    (1, ADAPTER_RANK, 2 * kv_width),
                    lambda i, me, br, ra: (ra[br[me[0] * per_device + i]], 0, 0),
                ),
            ],
            out_specs=(
                pl.BlockSpec((block_len, 2 * kv_width), lambda i, me, br, ra: (i, 0)),
                pl.BlockSpec((block_len, ADAPTER_RANK), lambda i, me, br, ra: (i, 0)),
            ),
        ),
        name="update",
    )(place, block_request, request_adapter, partials, base_key, base_value, up_weight)


def attend_kernel(
    block_len, most_blocks, planes, plane_devices, place_ref, request_ref, q_ref, low_ref, up_ref, *rest
):
    pieces = planes * plane_devices
    piece_refs = rest[:pieces]
    out_ref, kv_ref, query_ref, total_ref, top_ref, sum_ref, sems = rest[pieces:]
    part, head = pl.program_id(0), pl.program_id(1)
    per_device = pl.num_programs(0)
    tokens = piece_refs[0].shape[0]
    me = place_ref[0]
    within = lax.rem(me, plane_devices)
    copies = []
    for back in range(planes):
        for flip in range(plane_devices):
            slot = (planes - 1 - back) * plane_devices + (within ^ flip)
            index = back * plane_devices + flip
            copies.append(
                pltpu.make_async_copy(
                    piece_refs[index],
                    kv_ref.at[pl.ds(pl.multiple_of(slot * tokens, tokens), tokens), :],
                    sems.at[index],
                )
            )

    @pl.when((part == 0) & (head == 0))
    def _():
        for copy in copies:
            copy.start()

    group = q_ref.shape[1] // HEAD_SIZE
    sources = up_ref.shape[0]
    span = up_ref.shape[3]
    low = low_ref[...]
    for source in range(sources):
        columns = pl.ds(source * span, span)
        delta = jnp.dot(low, up_ref[source, 0], preferred_element_type=jnp.float32)
        query = (q_ref[:, columns].astype(jnp.float32) + delta).astype(jnp.bfloat16)
        for at in range(span // HEAD_SIZE):
            row = (source * (span // HEAD_SIZE) + at) * block_len
            query_ref[pl.ds(row, block_len), :] = query[:, at * HEAD_SIZE : (at + 1) * HEAD_SIZE]

    @pl.when((part == 0) & (head == 0))
    def _():
        for copy in copies:
            copy.wait()

    block = me * per_device + part
    request = request_ref[block]
    count = jnp.int32(1)
    for back in range(1, most_blocks):
        earlier = request_ref[jnp.maximum(block - back, 0)]
        same = (block >= back) & (earlier == request)
        count = count + same.astype(jnp.int32)
    window_block = (planes - 1) * plane_devices * per_device + within * per_device + part
    end = (window_block + 1) * block_len
    low_key = end - count * block_len
    chunks = lax.div(count * block_len + (KEY_CHUNK - 1), KEY_CHUNK)
    rows = group * block_len
    kv_width = kv_ref.shape[1] // 2
    key_columns = pl.ds(pl.multiple_of(head * HEAD_SIZE, HEAD_SIZE), HEAD_SIZE)
    value_columns = pl.ds(pl.multiple_of(kv_width + head * HEAD_SIZE, HEAD_SIZE), HEAD_SIZE)
    factor = math.log2(math.e) / math.sqrt(HEAD_SIZE)

    def chunk(step, first, masked):
        start = pl.multiple_of(end - (step + 1) * KEY_CHUNK, block_len)
        keys = kv_ref[pl.ds(start, KEY_CHUNK), key_columns]
        values = kv_ref[pl.ds(start, KEY_CHUNK), value_columns]
        scores = lax.dot_general(keys, query_ref[...], NT, preferred_element_type=jnp.float32)
        if masked:
            key_at = start + lax.broadcasted_iota(jnp.int32, scores.shape, 0)
            allowed = key_at >= low_key
            if first:
                query_at = end - block_len + lax.rem(
                    lax.broadcasted_iota(jnp.int32, scores.shape, 1), block_len
                )
                allowed = allowed & (key_at <= query_at)
            scores = jnp.where(allowed, scores, -1e30)
        top = jnp.max(scores, axis=0, keepdims=True)
        if not first:
            top = jnp.maximum(top, top_ref[...])
        weights = jnp.exp2((scores - top) * factor)
        sums = jnp.sum(weights, axis=0, keepdims=True)
        product = lax.dot_general(
            values, weights.astype(jnp.bfloat16), TN, preferred_element_type=jnp.float32
        )
        if not first:
            fade = jnp.exp2((top_ref[...] - top) * factor)
            sums = sums + sum_ref[...] * fade
            product = product + total_ref[...] * fade
        top_ref[...] = top
        sum_ref[...] = sums
        total_ref[...] = product

    chunk(0, True, True)

    @pl.loop(1, jnp.maximum(chunks - 1, 1))
    def _(step):
        chunk(step, False, False)

    @pl.when(chunks > 1)
    def _():
        chunk(chunks - 1, False, True)

    result = (total_ref[...] / sum_ref[...]).T.astype(out_ref.dtype)
    for at in range(group):
        out_ref[:, at * HEAD_SIZE : (at + 1) * HEAD_SIZE] = result[at * block_len : (at + 1) * block_len]


def attend(q_base, low, up_rows, pieces, place, block_request, block_len, most_blocks, planes, plane_devices):
    tokens, width = q_base.shape
    devices, per_device, rank, span = up_rows.shape
    kv_columns = pieces[0].shape[1]
    head_span = width // KEY_VALUE_HEADS
    sources = devices // KEY_VALUE_HEADS
    group = head_span // HEAD_SIZE
    window = planes * plane_devices * tokens
    flops = 4 * tokens * width * window // 2
    return pl.pallas_call(
        functools.partial(attend_kernel, block_len, most_blocks, planes, plane_devices),
        out_shape=jax.ShapeDtypeStruct((tokens, width), jnp.bfloat16),
        grid_spec=pltpu.PrefetchScalarGridSpec(
            num_scalar_prefetch=2,
            grid=(per_device, KEY_VALUE_HEADS),
            in_specs=[
                pl.BlockSpec((block_len, head_span), lambda i, m, me, br: (i, m)),
                pl.BlockSpec((block_len, rank), lambda i, m, me, br: (i, 0)),
                pl.BlockSpec((sources, 1, rank, span), lambda i, m, me, br: (m, i, 0, 0)),
            ]
            + [pl.BlockSpec(memory_space=pl.ANY)] * len(pieces),
            out_specs=pl.BlockSpec((block_len, head_span), lambda i, m, me, br: (i, m)),
            scratch_shapes=[
                pltpu.VMEM((window, kv_columns), jnp.bfloat16),
                pltpu.VMEM((group * block_len, HEAD_SIZE), jnp.bfloat16),
                pltpu.VMEM((HEAD_SIZE, group * block_len), jnp.float32),
                pltpu.VMEM((1, group * block_len), jnp.float32),
                pltpu.VMEM((1, group * block_len), jnp.float32),
                pltpu.SemaphoreType.DMA((len(pieces),)),
            ],
        ),
        cost_estimate=pl.CostEstimate(flops=flops, bytes_accessed=16 << 20, transcendentals=8 << 20),
        name="attend",
    )(place, block_request, q_base, low, up_rows, *pieces)


def body(
    hidden,
    q_base,
    base_key_weight,
    base_value_weight,
    shrink_a,
    expand_q,
    key_value_up_weight,
    block_request,
    request_adapter,
):
    tokens = hidden.shape[0]
    devices = lax.axis_size("seq")
    me = lax.axis_index("seq")
    place = me.astype(jnp.int32).reshape(1)
    block_count = block_request.shape[0]
    block_len = tokens * devices // block_count
    per_device = tokens // block_len
    most_blocks = min(MOST_BLOCKS_CAP, block_count // 2)
    plane_devices = 4
    plane_blocks = plane_devices * per_device
    hops = -(-(most_blocks - 1) // plane_blocks)

    features = hidden.shape[1] // devices
    sent = hidden.reshape(tokens, devices, features).transpose(1, 0, 2)
    rows = lax.all_to_all(sent, "seq", split_axis=0, concat_axis=0, tiled=True)
    down = jnp.swapaxes(shrink_a, 1, 2)
    partials = shrink(rows, down, block_request, request_adapter, block_len)
    received = lax.all_to_all(partials, "seq", split_axis=0, concat_axis=0, tiled=True)

    adapter_of = request_adapter[block_request]
    picked = expand_q[adapter_of].reshape(devices, per_device, ADAPTER_RANK, expand_q.shape[2])
    up_rows = lax.all_to_all(picked, "seq", split_axis=0, concat_axis=0, tiled=True)

    kv, low = update(
        received, base_key_weight, base_value_weight, key_value_up_weight,
        place, block_request, request_adapter, block_len,
    )
    forward = [(i, i + plane_devices) for i in range(devices - plane_devices)]
    swap_y = [(i, i ^ 2) for i in range(devices)]
    swap_core = [(i, i ^ 1) for i in range(devices)]
    pieces = []
    own = kv
    for back in range(hops + 1):
        if back > 0:
            own = lax.ppermute(own, "seq", forward)
        across = lax.ppermute(own, "seq", swap_y)
        pieces += [
            own,
            lax.ppermute(own, "seq", swap_core),
            across,
            lax.ppermute(across, "seq", swap_core),
        ]
    return attend(
        q_base, low, up_rows, pieces, place, block_request,
        block_len, most_blocks, hops + 1, plane_devices,
    )


def solution(mesh):
    return jax.shard_map(
        body,
        mesh=mesh,
        in_specs=(
            P(("groups", "seq"), None),
            P(("groups", "seq"), None),
            P(("groups", "seq"), None),
            P(("groups", "seq"), None),
            P("groups", "seq", None),
            P("groups", None, "seq"),
            P("groups", None, None),
            P("groups"),
            P("groups"),
        ),
        out_specs=P(("groups", "seq"), None),
        check_vma=False,
    )
```

```python
import functools
import math

import jax
import jax.numpy as jnp
from jax import lax
from jax.experimental import pallas as pl
from jax.experimental.pallas import tpu as pltpu
from jax.sharding import PartitionSpec as P

KEY_VALUE_HEADS = 8
HEAD_SIZE = 128
ADAPTER_RANK = 64
MOST_BLOCKS_CAP = 32
CORES = 2
PLANE = 4
KEY_CHUNK = 256
NT = (((1,), (1,)), ((), ()))
TN = (((0,), (0,)), ((), ()))


def split_kernel(hidden_ref, key_ref, value_ref, sent_ref, kv_ref):
    sent_ref[0] = hidden_ref[...]

    @pl.when(pl.program_id(0) == 0)
    def _():
        width = key_ref.shape[1]
        kv_ref[:, :width] = key_ref[...]
        kv_ref[:, width:] = value_ref[...]


def split(hidden, base_key, base_value, parts):
    tokens, width = hidden.shape
    span = width // parts
    kv_width = base_key.shape[1]
    return pl.pallas_call(
        split_kernel,
        out_shape=(
            jax.ShapeDtypeStruct((parts, tokens, span), hidden.dtype),
            jax.ShapeDtypeStruct((tokens, 2 * kv_width), hidden.dtype),
        ),
        grid=(parts,),
        in_specs=[
            pl.BlockSpec((tokens, span), lambda i: (0, i)),
            pl.BlockSpec((tokens, kv_width), lambda i: (0, 0)),
            pl.BlockSpec((tokens, kv_width), lambda i: (0, 0)),
        ],
        out_specs=(
            pl.BlockSpec((1, tokens, span), lambda i: (i, 0, 0)),
            pl.BlockSpec((tokens, 2 * kv_width), lambda i: (0, 0)),
        ),
        name="split",
    )(hidden, base_key, base_value)


def shrink_kernel(block_len, place_ref, request_ref, adapter_ref, rows_ref, own_ref, other_ref, out_ref):
    sources, tokens, features = rows_ref.shape
    per_device = tokens // block_len
    half = features // CORES
    core = lax.rem(place_ref[0], CORES)
    own_columns = pl.ds(pl.multiple_of(core * half, half), half)
    other_columns = pl.ds(pl.multiple_of((1 - core) * half, half), half)
    first = pl.program_id(0) * sources
    for source in range(sources):
        device = (first + source) * CORES + core
        for part in range(per_device):
            adapter = adapter_ref[request_ref[device * per_device + part]]
            span = pl.ds(part * block_len, block_len)
            total = lax.dot_general(
                own_ref[adapter], rows_ref[source, span, own_columns], NT, preferred_element_type=jnp.float32
            ) + lax.dot_general(
                other_ref[adapter], rows_ref[source, span, other_columns], NT, preferred_element_type=jnp.float32
            )
            out_ref[source, :, span] = total.astype(out_ref.dtype)


def shrink(rows, own, other, place, block_request, request_adapter, block_len):
    chips, tokens, features = rows.shape
    adapters, width, half = own.shape
    steps = min(2, chips)
    sources = chips // steps
    return pl.pallas_call(
        functools.partial(shrink_kernel, block_len),
        out_shape=jax.ShapeDtypeStruct((chips, width, tokens), jnp.bfloat16),
        grid_spec=pltpu.PrefetchScalarGridSpec(
            num_scalar_prefetch=3,
            grid=(steps,),
            in_specs=[
                pl.BlockSpec((sources, tokens, features), lambda i, me, br, ra: (i, 0, 0)),
                pl.BlockSpec((adapters, width, half), lambda i, me, br, ra: (0, 0, 0)),
                pl.BlockSpec((adapters, width, half), lambda i, me, br, ra: (0, 0, 0)),
            ],
            out_specs=pl.BlockSpec((sources, width, tokens), lambda i, me, br, ra: (i, 0, 0)),
        ),
        cost_estimate=pl.CostEstimate(
            flops=2 * chips * tokens * features * width,
            bytes_accessed=2 * (rows.size + own.size + other.size),
            transcendentals=0,
        ),
        name="shrink",
    )(place, block_request, request_adapter, rows, own, other)


def finish_kernel(block_len, planes, place_ref, request_ref, adapter_ref, low_ref, up_ref, *rest):
    pieces = planes * PLANE
    piece_refs = rest[:pieces]
    out_ref, base_ref, done_ref, in_sems, out_sems = rest[pieces:]
    tokens = piece_refs[0].shape[0]
    per_device = tokens // block_len
    rank = ADAPTER_RANK
    width = base_ref.shape[2] // 2
    me = place_ref[0]
    within = lax.rem(me, PLANE)
    for index in range(pieces):
        pltpu.make_async_copy(piece_refs[index], base_ref.at[index], in_sems.at[index]).start()
    for index in range(pieces):
        back, flip = index // PLANE, index % PLANE
        place = within ^ flip
        device = me - within - back * PLANE + place
        pltpu.make_async_copy(piece_refs[index], base_ref.at[index], in_sems.at[index]).wait()
        for part in range(per_device):
            adapter = adapter_ref[request_ref[jnp.maximum(device * per_device + part, 0)]]
            span = pl.ds(part * block_len, block_len)
            for which in range(2):
                columns = pl.ds(which * width, width)
                delta = lax.dot_general(
                    low_ref[index, pl.ds(which * rank, rank), span],
                    up_ref[adapter, :, columns],
                    TN,
                    preferred_element_type=jnp.float32,
                )
                done_ref[index, span, columns] = (
                    base_ref[index, span, columns].astype(jnp.float32) + delta
                ).astype(done_ref.dtype)
        slot = (planes - 1 - back) * PLANE + place
        pltpu.make_async_copy(
            done_ref.at[index], out_ref.at[pl.ds(pl.multiple_of(slot * tokens, tokens), tokens), :], out_sems.at[index]
        ).start()
    for index in range(pieces):
        pltpu.make_async_copy(done_ref.at[index], out_ref.at[pl.ds(0, tokens), :], out_sems.at[index]).wait()


def finish(pieces, lows, up_weight, place, block_request, request_adapter, block_len, planes):
    tokens, width = pieces[0].shape
    count = len(pieces)
    return pl.pallas_call(
        functools.partial(finish_kernel, block_len, planes),
        out_shape=jax.ShapeDtypeStruct((count * tokens, width), jnp.bfloat16),
        grid_spec=pltpu.PrefetchScalarGridSpec(
            num_scalar_prefetch=3,
            grid=(1,),
            in_specs=[
                pl.BlockSpec(lows.shape, lambda i, me, br, ra: (0, 0, 0)),
                pl.BlockSpec(up_weight.shape, lambda i, me, br, ra: (0, 0, 0)),
            ]
            + [pl.BlockSpec(memory_space=pl.ANY)] * count,
            out_specs=pl.BlockSpec(memory_space=pl.ANY),
            scratch_shapes=[
                pltpu.VMEM((count, tokens, width), jnp.bfloat16),
                pltpu.VMEM((count, tokens, width), jnp.bfloat16),
                pltpu.SemaphoreType.DMA((count,)),
                pltpu.SemaphoreType.DMA((count,)),
            ],
        ),
        cost_estimate=pl.CostEstimate(
            flops=2 * count * tokens * width * ADAPTER_RANK, bytes_accessed=4 * count * tokens * width, transcendentals=0
        ),
        name="finish",
    )(place, block_request, request_adapter, lows, up_weight, *pieces)


def attend_kernel(
    block_len, most_blocks, planes, place_ref, request_ref, q_ref, low_ref, up_ref, key_ref, value_ref,
    out_ref, query_ref, total_ref, top_ref, sum_ref,
):
    tokens = q_ref.shape[0]
    per_device = tokens // block_len
    me = place_ref[0]
    within = lax.rem(me, PLANE)
    group = q_ref.shape[1] // HEAD_SIZE
    rows = group * block_len
    sources = up_ref.shape[0]
    span = up_ref.shape[3]
    heads = span // HEAD_SIZE
    for part in range(per_device):
        own_rows = pl.ds(part * block_len, block_len)
        for source in range(sources):
            columns = pl.ds(source * span, span)
            delta = lax.dot_general(
                low_ref[:, own_rows], up_ref[source, part], TN, preferred_element_type=jnp.float32
            )
            query = (q_ref[own_rows, columns].astype(jnp.float32) + delta).astype(jnp.bfloat16)
            for at in range(heads):
                row = part * rows + (source * heads + at) * block_len
                query_ref[pl.ds(row, block_len), :] = query[:, at * HEAD_SIZE : (at + 1) * HEAD_SIZE]

    first_block = me * per_device
    request = request_ref[first_block]
    count = jnp.int32(1)
    for back in range(1, most_blocks):
        earlier = request_ref[jnp.maximum(first_block - back, 0)]
        count = count + ((first_block >= back) & (earlier == request)).astype(jnp.int32)
    window_first = ((planes - 1) * PLANE + within) * per_device
    end = (window_first + per_device) * block_len
    starts = [(window_first - count + 1) * block_len]
    for part in range(1, per_device):
        same = request_ref[first_block + part] == request_ref[first_block + part - 1]
        starts.append(jnp.where(same, starts[-1], (window_first + part) * block_len))
    all_same = request_ref[first_block + per_device - 1] == request
    chunks = lax.div(end - starts[0] + (KEY_CHUNK - 1), KEY_CHUNK)
    factor = math.log2(math.e) / math.sqrt(HEAD_SIZE)

    def chunk(step, parts, first, masked):
        stop = end - step * KEY_CHUNK
        start = stop - KEY_CHUNK
        if masked:
            start = jnp.maximum(start, 0)
        start = pl.multiple_of(start, block_len)
        keys = key_ref[pl.ds(start, KEY_CHUNK), :]
        values = value_ref[pl.ds(start, KEY_CHUNK), :]
        for part in parts:
            columns = pl.ds(part * rows, rows)
            scores = lax.dot_general(keys, query_ref[columns, :], NT, preferred_element_type=jnp.float32)
            if masked:
                key_at = start + lax.broadcasted_iota(jnp.int32, scores.shape, 0)
                allowed = (key_at >= starts[part]) & (key_at < stop)
                if first:
                    query_at = (window_first + part) * block_len + lax.rem(
                        lax.broadcasted_iota(jnp.int32, scores.shape, 1), block_len
                    )
                    allowed = allowed & (key_at <= query_at)
                scores = jnp.where(allowed, scores, -1e30)
            top = jnp.max(scores, axis=0, keepdims=True)
            if not first:
                top = jnp.maximum(top, top_ref[:, columns])
            weights = jnp.exp2((scores - top) * factor)
            sums = jnp.sum(weights, axis=0, keepdims=True)
            product = lax.dot_general(
                values, weights.astype(jnp.bfloat16), TN, preferred_element_type=jnp.float32
            )
            if not first:
                fade = jnp.exp2((top_ref[:, columns] - top) * factor)
                sums = sums + sum_ref[:, columns] * fade
                product = product + total_ref[:, columns] * fade
            top_ref[:, columns] = top
            sum_ref[:, columns] = sums
            total_ref[:, columns] = product

    every = list(range(per_device))
    leading = every[: max(1, per_device - 1)]
    chunk(0, every, True, True)

    @pl.when(all_same)
    def _():
        @pl.loop(1, jnp.maximum(chunks - 1, 1))
        def _(step):
            chunk(step, every, False, False)

        @pl.when(chunks > 1)
        def _():
            chunk(chunks - 1, every, False, True)

    @pl.when(jnp.logical_not(all_same))
    def _():
        @pl.loop(1, jnp.maximum(chunks, 1))
        def _(step):
            chunk(step, leading, False, True)

    for part in every:
        columns = pl.ds(part * rows, rows)
        result = (total_ref[:, columns] / sum_ref[:, columns]).T.astype(out_ref.dtype)
        for at in range(group):
            out_ref[pl.ds(part * block_len, block_len), at * HEAD_SIZE : (at + 1) * HEAD_SIZE] = result[
                at * block_len : (at + 1) * block_len
            ]


def attend(q_base, low, up_rows, kv, place, block_request, block_len, most_blocks, planes):
    tokens, width = q_base.shape
    devices, per_device, rank, span = up_rows.shape
    window = kv.shape[0]
    head_span = width // KEY_VALUE_HEADS
    sources = devices // KEY_VALUE_HEADS
    lanes = tokens * head_span // HEAD_SIZE
    return pl.pallas_call(
        functools.partial(attend_kernel, block_len, most_blocks, planes),
        out_shape=jax.ShapeDtypeStruct((tokens, width), jnp.bfloat16),
        grid_spec=pltpu.PrefetchScalarGridSpec(
            num_scalar_prefetch=2,
            grid=(KEY_VALUE_HEADS,),
            in_specs=[
                pl.BlockSpec((tokens, head_span), lambda m, me, br: (0, m)),
                pl.BlockSpec((rank, tokens), lambda m, me, br: (0, 0)),
                pl.BlockSpec((sources, per_device, rank, span), lambda m, me, br: (m, 0, 0, 0)),
                pl.BlockSpec((window, HEAD_SIZE), lambda m, me, br: (0, m)),
                pl.BlockSpec((window, HEAD_SIZE), lambda m, me, br: (0, KEY_VALUE_HEADS + m)),
            ],
            out_specs=pl.BlockSpec((tokens, head_span), lambda m, me, br: (0, m)),
            scratch_shapes=[
                pltpu.VMEM((lanes, HEAD_SIZE), jnp.bfloat16),
                pltpu.VMEM((HEAD_SIZE, lanes), jnp.float32),
                pltpu.VMEM((1, lanes), jnp.float32),
                pltpu.VMEM((1, lanes), jnp.float32),
            ],
        ),
        cost_estimate=pl.CostEstimate(
            flops=2 * tokens * width * window, bytes_accessed=16 << 20, transcendentals=8 << 20
        ),
        name="attend",
    )(place, block_request, q_base, low, up_rows, kv, kv)


def body(
    hidden,
    q_base,
    base_key_weight,
    base_value_weight,
    shrink_a,
    expand_q,
    key_value_up_weight,
    block_request,
    request_adapter,
):
    tokens = hidden.shape[0]
    devices = lax.axis_size("seq")
    me = lax.axis_index("seq")
    place = me.astype(jnp.int32).reshape(1)
    block_count = block_request.shape[0]
    block_len = tokens * devices // block_count
    per_device = tokens // block_len
    most_blocks = min(MOST_BLOCKS_CAP, block_count // 2)
    hops = -(-(most_blocks - 1) // (PLANE * per_device))
    planes = hops + 1
    chips = devices // CORES
    same_core = [[chip * CORES + core for chip in range(chips)] for core in range(CORES)]
    forward = [(i, i + PLANE) for i in range(devices - PLANE)]
    swap_row = [(i, i ^ CORES) for i in range(devices)]
    swap_core = [(i, i ^ 1) for i in range(devices)]

    sent, kv = split(hidden, base_key_weight, base_value_weight, chips)
    rows = lax.all_to_all(sent, "seq", split_axis=0, concat_axis=0, axis_index_groups=same_core, tiled=True)
    down = jnp.swapaxes(shrink_a, 1, 2)
    other_down = lax.ppermute(down, "seq", swap_core)

    pieces = []
    own = kv
    for back in range(planes):
        if back > 0:
            own = lax.ppermute(own, "seq", forward)
        across = lax.ppermute(own, "seq", swap_row)
        pieces += [
            own,
            lax.ppermute(own, "seq", swap_core),
            across,
            lax.ppermute(across, "seq", swap_core),
        ]

    partials = shrink(rows, down, other_down, place, block_request, request_adapter, block_len)
    received = lax.all_to_all(
        partials, "seq", split_axis=0, concat_axis=0, axis_index_groups=same_core, tiled=True
    )

    adapter_of = request_adapter[block_request]
    picked = expand_q[adapter_of].reshape(devices, per_device, ADAPTER_RANK, expand_q.shape[2])
    up_rows = lax.all_to_all(picked, "seq", split_axis=0, concat_axis=0, tiled=True)

    low = jnp.sum(received.astype(jnp.float32), axis=0).astype(jnp.bfloat16)
    steps = [low[ADAPTER_RANK:]]
    for _ in range(hops):
        steps.append(lax.ppermute(steps[-1], "seq", forward))
    column = jnp.stack(steps)
    both = jnp.concatenate([column, lax.ppermute(column, "seq", swap_row)])
    flipped = lax.ppermute(both, "seq", swap_core)
    lows = jnp.stack([both[:planes], flipped[:planes], both[planes:], flipped[planes:]], axis=1)
    lows = lows.reshape(planes * PLANE, 2 * ADAPTER_RANK, tokens)

    window = finish(
        pieces, lows, key_value_up_weight, place, block_request, request_adapter, block_len, planes
    )
    return attend(
        q_base, low[:ADAPTER_RANK], up_rows, window, place, block_request, block_len, most_blocks, planes
    )


def solution(mesh):
    return jax.shard_map(
        body,
        mesh=mesh,
        in_specs=(
            P(("groups", "seq"), None),
            P(("groups", "seq"), None),
            P(("groups", "seq"), None),
            P(("groups", "seq"), None),
            P("groups", "seq", None),
            P("groups", None, "seq"),
            P("groups", None, None),
            P("groups"),
            P("groups"),
        ),
        out_specs=P(("groups", "seq"), None),
        check_vma=False,
    )
```

```python
import functools
import math

import jax
import jax.numpy as jnp
from jax import lax
from jax.experimental import pallas as pl
from jax.experimental.pallas import tpu as pltpu
from jax.sharding import PartitionSpec as P

KEY_VALUE_HEADS = 8
HEAD_SIZE = 128
ADAPTER_RANK = 64
MOST_BLOCKS_CAP = 32
CORES = 2
PLANE = 4
KEY_CHUNK = 256
NT = (((1,), (1,)), ((), ()))
TN = (((0,), (0,)), ((), ()))


def split_kernel(hidden_ref, key_ref, value_ref, sent_ref, kv_ref):
    sent_ref[0] = hidden_ref[...]

    @pl.when(pl.program_id(0) == 0)
    def _():
        width = key_ref.shape[1]
        kv_ref[:, :width] = key_ref[...]
        kv_ref[:, width:] = value_ref[...]


def split(hidden, base_key, base_value, parts):
    tokens, width = hidden.shape
    span = width // parts
    kv_width = base_key.shape[1]
    return pl.pallas_call(
        split_kernel,
        out_shape=(
            jax.ShapeDtypeStruct((parts, tokens, span), hidden.dtype),
            jax.ShapeDtypeStruct((tokens, 2 * kv_width), hidden.dtype),
        ),
        grid=(parts,),
        in_specs=[
            pl.BlockSpec((tokens, span), lambda i: (0, i)),
            pl.BlockSpec((tokens, kv_width), lambda i: (0, 0)),
            pl.BlockSpec((tokens, kv_width), lambda i: (0, 0)),
        ],
        out_specs=(
            pl.BlockSpec((1, tokens, span), lambda i: (i, 0, 0)),
            pl.BlockSpec((tokens, 2 * kv_width), lambda i: (0, 0)),
        ),
        name="split",
    )(hidden, base_key, base_value)


def shrink_kernel(block_len, place_ref, request_ref, adapter_ref, rows_ref, own_ref, other_ref, out_ref):
    sources, tokens, features = rows_ref.shape
    per_device = tokens // block_len
    half = features // CORES
    core = lax.rem(place_ref[0], CORES)
    own_columns = pl.ds(pl.multiple_of(core * half, half), half)
    other_columns = pl.ds(pl.multiple_of((1 - core) * half, half), half)
    first = pl.program_id(0) * sources
    for source in range(sources):
        device = (first + source) * CORES + core
        for part in range(per_device):
            adapter = adapter_ref[request_ref[device * per_device + part]]
            span = pl.ds(part * block_len, block_len)
            total = lax.dot_general(
                own_ref[adapter], rows_ref[source, span, own_columns], NT, preferred_element_type=jnp.float32
            ) + lax.dot_general(
                other_ref[adapter], rows_ref[source, span, other_columns], NT, preferred_element_type=jnp.float32
            )
            out_ref[source, :, span] = total.astype(out_ref.dtype)


def shrink(rows, own, other, place, block_request, request_adapter, block_len):
    chips, tokens, features = rows.shape
    adapters, width, half = own.shape
    steps = min(2, chips)
    sources = chips // steps
    return pl.pallas_call(
        functools.partial(shrink_kernel, block_len),
        out_shape=jax.ShapeDtypeStruct((chips, width, tokens), jnp.bfloat16),
        grid_spec=pltpu.PrefetchScalarGridSpec(
            num_scalar_prefetch=3,
            grid=(steps,),
            in_specs=[
                pl.BlockSpec((sources, tokens, features), lambda i, me, br, ra: (i, 0, 0)),
                pl.BlockSpec((adapters, width, half), lambda i, me, br, ra: (0, 0, 0)),
                pl.BlockSpec((adapters, width, half), lambda i, me, br, ra: (0, 0, 0)),
            ],
            out_specs=pl.BlockSpec((sources, width, tokens), lambda i, me, br, ra: (i, 0, 0)),
        ),
        cost_estimate=pl.CostEstimate(
            flops=2 * chips * tokens * features * width,
            bytes_accessed=2 * (rows.size + own.size + other.size),
            transcendentals=0,
        ),
        name="shrink",
    )(place, block_request, request_adapter, rows, own, other)


def finish_kernel(block_len, planes, place_ref, request_ref, adapter_ref, low_ref, up_ref, *rest):
    pieces = planes * PLANE
    piece_refs = rest[:pieces]
    out_ref, base_ref, done_ref, in_sems, out_sems = rest[pieces:]
    tokens = piece_refs[0].shape[0]
    per_device = tokens // block_len
    rank = ADAPTER_RANK
    width = base_ref.shape[2] // 2
    me = place_ref[0]
    within = lax.rem(me, PLANE)
    for index in range(pieces):
        pltpu.make_async_copy(piece_refs[index], base_ref.at[index], in_sems.at[index]).start()
    for index in range(pieces):
        back, flip = index // PLANE, index % PLANE
        place = within ^ flip
        device = me - within - back * PLANE + place
        pltpu.make_async_copy(piece_refs[index], base_ref.at[index], in_sems.at[index]).wait()
        for part in range(per_device):
            adapter = adapter_ref[request_ref[jnp.maximum(device * per_device + part, 0)]]
            span = pl.ds(part * block_len, block_len)
            for which in range(2):
                columns = pl.ds(which * width, width)
                delta = lax.dot_general(
                    low_ref[index, pl.ds(which * rank, rank), span],
                    up_ref[adapter, :, columns],
                    TN,
                    preferred_element_type=jnp.float32,
                )
                done_ref[index, span, columns] = (
                    base_ref[index, span, columns].astype(jnp.float32) + delta
                ).astype(done_ref.dtype)
        slot = (planes - 1 - back) * PLANE + place
        pltpu.make_async_copy(
            done_ref.at[index], out_ref.at[pl.ds(pl.multiple_of(slot * tokens, tokens), tokens), :], out_sems.at[index]
        ).start()
    for index in range(pieces):
        pltpu.make_async_copy(done_ref.at[index], out_ref.at[pl.ds(0, tokens), :], out_sems.at[index]).wait()


def finish(pieces, lows, up_weight, place, block_request, request_adapter, block_len, planes):
    tokens, width = pieces[0].shape
    count = len(pieces)
    return pl.pallas_call(
        functools.partial(finish_kernel, block_len, planes),
        out_shape=jax.ShapeDtypeStruct((count * tokens, width), jnp.bfloat16),
        grid_spec=pltpu.PrefetchScalarGridSpec(
            num_scalar_prefetch=3,
            grid=(1,),
            in_specs=[
                pl.BlockSpec(lows.shape, lambda i, me, br, ra: (0, 0, 0)),
                pl.BlockSpec(up_weight.shape, lambda i, me, br, ra: (0, 0, 0)),
            ]
            + [pl.BlockSpec(memory_space=pl.ANY)] * count,
            out_specs=pl.BlockSpec(memory_space=pl.ANY),
            scratch_shapes=[
                pltpu.VMEM((count, tokens, width), jnp.bfloat16),
                pltpu.VMEM((count, tokens, width), jnp.bfloat16),
                pltpu.SemaphoreType.DMA((count,)),
                pltpu.SemaphoreType.DMA((count,)),
            ],
        ),
        cost_estimate=pl.CostEstimate(
            flops=2 * count * tokens * width * ADAPTER_RANK, bytes_accessed=4 * count * tokens * width, transcendentals=0
        ),
        name="finish",
    )(place, block_request, request_adapter, lows, up_weight, *pieces)


def attend_kernel(
    block_len, most_blocks, planes, place_ref, request_ref, q_ref, low_ref, up_ref, key_ref, value_ref,
    out_ref, query_ref, total_ref, top_ref, sum_ref,
):
    tokens = q_ref.shape[0]
    per_device = tokens // block_len
    me = place_ref[0]
    within = lax.rem(me, PLANE)
    group = q_ref.shape[1] // HEAD_SIZE
    rows = group * block_len
    sources = up_ref.shape[0]
    span = up_ref.shape[3]
    heads = span // HEAD_SIZE
    for part in range(per_device):
        own_rows = pl.ds(part * block_len, block_len)
        for source in range(sources):
            columns = pl.ds(source * span, span)
            delta = lax.dot_general(
                low_ref[:, own_rows], up_ref[source, part], TN, preferred_element_type=jnp.float32
            )
            query = (q_ref[own_rows, columns].astype(jnp.float32) + delta).astype(jnp.bfloat16)
            for at in range(heads):
                row = part * rows + (source * heads + at) * block_len
                query_ref[pl.ds(row, block_len), :] = query[:, at * HEAD_SIZE : (at + 1) * HEAD_SIZE]

    first_block = me * per_device
    request = request_ref[first_block]
    count = jnp.int32(1)
    for back in range(1, most_blocks):
        earlier = request_ref[jnp.maximum(first_block - back, 0)]
        count = count + ((first_block >= back) & (earlier == request)).astype(jnp.int32)
    window_first = ((planes - 1) * PLANE + within) * per_device
    end = (window_first + per_device) * block_len
    starts = [(window_first - count + 1) * block_len]
    for part in range(1, per_device):
        same = request_ref[first_block + part] == request_ref[first_block + part - 1]
        starts.append(jnp.where(same, starts[-1], (window_first + part) * block_len))
    all_same = request_ref[first_block + per_device - 1] == request
    chunks = lax.div(end - starts[0] + (KEY_CHUNK - 1), KEY_CHUNK)
    factor = math.log2(math.e) / math.sqrt(HEAD_SIZE)

    def chunk(step, parts, first, masked):
        stop = end - step * KEY_CHUNK
        start = stop - KEY_CHUNK
        if masked:
            start = jnp.maximum(start, 0)
        start = pl.multiple_of(start, block_len)
        keys = key_ref[pl.ds(start, KEY_CHUNK), :]
        values = value_ref[pl.ds(start, KEY_CHUNK), :]
        for part in parts:
            columns = pl.ds(part * rows, rows)
            scores = lax.dot_general(keys, query_ref[columns, :], NT, preferred_element_type=jnp.float32)
            if masked:
                key_at = start + lax.broadcasted_iota(jnp.int32, scores.shape, 0)
                allowed = (key_at >= starts[part]) & (key_at < stop)
                if first:
                    query_at = (window_first + part) * block_len + lax.rem(
                        lax.broadcasted_iota(jnp.int32, scores.shape, 1), block_len
                    )
                    allowed = allowed & (key_at <= query_at)
                scores = jnp.where(allowed, scores, -1e30)
            top = jnp.max(scores, axis=0, keepdims=True)
            if not first:
                top = jnp.maximum(top, top_ref[:, columns])
            weights = jnp.exp2((scores - top) * factor)
            sums = jnp.sum(weights, axis=0, keepdims=True)
            product = lax.dot_general(
                values, weights.astype(jnp.bfloat16), TN, preferred_element_type=jnp.float32
            )
            if not first:
                fade = jnp.exp2((top_ref[:, columns] - top) * factor)
                sums = sums + sum_ref[:, columns] * fade
                product = product + total_ref[:, columns] * fade
            top_ref[:, columns] = top
            sum_ref[:, columns] = sums
            total_ref[:, columns] = product

    every = list(range(per_device))
    leading = every[: max(1, per_device - 1)]
    chunk(0, every, True, True)

    @pl.when(all_same)
    def _():
        @pl.loop(1, jnp.maximum(chunks - 1, 1))
        def _(step):
            chunk(step, every, False, False)

        @pl.when(chunks > 1)
        def _():
            chunk(chunks - 1, every, False, True)

    @pl.when(jnp.logical_not(all_same))
    def _():
        @pl.loop(1, jnp.maximum(chunks, 1))
        def _(step):
            chunk(step, leading, False, True)

    for part in every:
        columns = pl.ds(part * rows, rows)
        result = (total_ref[:, columns] / sum_ref[:, columns]).T.astype(out_ref.dtype)
        for at in range(group):
            out_ref[pl.ds(part * block_len, block_len), at * HEAD_SIZE : (at + 1) * HEAD_SIZE] = result[
                at * block_len : (at + 1) * block_len
            ]


def attend(q_base, low, up_rows, kv, place, block_request, block_len, most_blocks, planes):
    tokens, width = q_base.shape
    devices, per_device, rank, span = up_rows.shape
    window = kv.shape[0]
    head_span = width // KEY_VALUE_HEADS
    sources = devices // KEY_VALUE_HEADS
    lanes = tokens * head_span // HEAD_SIZE
    return pl.pallas_call(
        functools.partial(attend_kernel, block_len, most_blocks, planes),
        out_shape=jax.ShapeDtypeStruct((tokens, width), jnp.bfloat16),
        grid_spec=pltpu.PrefetchScalarGridSpec(
            num_scalar_prefetch=2,
            grid=(KEY_VALUE_HEADS,),
            in_specs=[
                pl.BlockSpec((tokens, head_span), lambda m, me, br: (0, m)),
                pl.BlockSpec((rank, tokens), lambda m, me, br: (0, 0)),
                pl.BlockSpec((sources, per_device, rank, span), lambda m, me, br: (m, 0, 0, 0)),
                pl.BlockSpec((window, HEAD_SIZE), lambda m, me, br: (0, m)),
                pl.BlockSpec((window, HEAD_SIZE), lambda m, me, br: (0, KEY_VALUE_HEADS + m)),
            ],
            out_specs=pl.BlockSpec((tokens, head_span), lambda m, me, br: (0, m)),
            scratch_shapes=[
                pltpu.VMEM((lanes, HEAD_SIZE), jnp.bfloat16),
                pltpu.VMEM((HEAD_SIZE, lanes), jnp.float32),
                pltpu.VMEM((1, lanes), jnp.float32),
                pltpu.VMEM((1, lanes), jnp.float32),
            ],
        ),
        cost_estimate=pl.CostEstimate(
            flops=2 * tokens * width * window, bytes_accessed=16 << 20, transcendentals=8 << 20
        ),
        name="attend",
    )(place, block_request, q_base, low, up_rows, kv, kv)


def body(
    hidden,
    q_base,
    base_key_weight,
    base_value_weight,
    shrink_a,
    expand_q,
    key_value_up_weight,
    block_request,
    request_adapter,
):
    tokens = hidden.shape[0]
    devices = lax.axis_size("seq")
    me = lax.axis_index("seq")
    place = me.astype(jnp.int32).reshape(1)
    block_count = block_request.shape[0]
    block_len = tokens * devices // block_count
    per_device = tokens // block_len
    most_blocks = min(MOST_BLOCKS_CAP, block_count // 2)
    hops = -(-(most_blocks - 1) // (PLANE * per_device))
    planes = hops + 1
    chips = devices // CORES
    same_core = [[chip * CORES + core for chip in range(chips)] for core in range(CORES)]
    forward = [(i, i + PLANE) for i in range(devices - PLANE)]
    swap_row = [(i, i ^ CORES) for i in range(devices)]
    swap_core = [(i, i ^ 1) for i in range(devices)]

    sent, kv = split(hidden, base_key_weight, base_value_weight, chips)
    rows = lax.all_to_all(
        sent, "seq", split_axis=0, concat_axis=0, axis_index_groups=same_core, tiled=True
    )
    down = jnp.swapaxes(shrink_a, 1, 2)
    other_down = lax.ppermute(down, "seq", swap_core)

    pieces = []
    own = kv
    for back in range(planes):
        if back > 0:
            own = lax.ppermute(own, "seq", forward)
        across = lax.ppermute(own, "seq", swap_row)
        flipped = lax.ppermute(own, "seq", swap_core)
        both = lax.ppermute(across, "seq", swap_core)
        pieces += [own, flipped, across, both]

    partials = shrink(rows, down, other_down, place, block_request, request_adapter, block_len)
    received = lax.all_to_all(
        partials, "seq", split_axis=0, concat_axis=0, axis_index_groups=same_core, tiled=True
    )

    adapter_of = request_adapter[block_request]
    picked = expand_q[adapter_of].reshape(devices, per_device, ADAPTER_RANK, expand_q.shape[2])
    up_rows = lax.all_to_all(picked, "seq", split_axis=0, concat_axis=0, tiled=True)

    low = jnp.sum(received.astype(jnp.float32), axis=0).astype(jnp.bfloat16)
    steps = [low[ADAPTER_RANK:]]
    for _ in range(1, planes):
        steps.append(lax.ppermute(steps[-1], "seq", forward))
    column = jnp.stack(steps)
    both = jnp.concatenate([column, lax.ppermute(column, "seq", swap_row)])
    flipped = lax.ppermute(both, "seq", swap_core)
    lows = jnp.stack([both[:planes], flipped[:planes], both[planes:], flipped[planes:]], axis=1)
    lows = lows.reshape(planes * PLANE, 2 * ADAPTER_RANK, tokens)

    window = finish(
        pieces, lows, key_value_up_weight, place, block_request, request_adapter, block_len, planes
    )
    return attend(
        q_base, low[:ADAPTER_RANK], up_rows, window, place, block_request, block_len, most_blocks, planes
    )


def solution(mesh):
    return jax.shard_map(
        body,
        mesh=mesh,
        in_specs=(
            P(("groups", "seq"), None),
            P(("groups", "seq"), None),
            P(("groups", "seq"), None),
            P(("groups", "seq"), None),
            P("groups", "seq", None),
            P("groups", None, "seq"),
            P("groups", None, None),
            P("groups"),
            P("groups"),
        ),
        out_specs=P(("groups", "seq"), None),
        check_vma=False,
    )
```

```python
import functools
import math

import jax
import jax.numpy as jnp
from jax import lax
from jax.experimental import pallas as pl
from jax.experimental.pallas import tpu as pltpu
from jax.sharding import PartitionSpec as P

KEY_VALUE_HEADS = 8
HEAD_SIZE = 128
ADAPTER_RANK = 64
MOST_BLOCKS_CAP = 32
CORES = 2
PLANE = 4
KEY_CHUNK = 512
KEY_STEP = 512
NT = (((1,), (1,)), ((), ()))
TN = (((0,), (0,)), ((), ()))


def split_kernel(hidden_ref, key_ref, value_ref, sent_ref, kv_ref, rows_ref, both_ref, in_sems, out_sems):
    parts, _, span = rows_ref.shape
    width = key_ref.shape[1]
    fetches = [
        pltpu.make_async_copy(key_ref, both_ref.at[:, pl.ds(0, width)], in_sems.at[parts]),
        pltpu.make_async_copy(value_ref, both_ref.at[:, pl.ds(width, width)], in_sems.at[parts + 1]),
    ]
    fetches += [
        pltpu.make_async_copy(hidden_ref.at[:, pl.ds(i * span, span)], rows_ref.at[i], in_sems.at[i])
        for i in range(parts)
    ]
    for fetch in fetches:
        fetch.start()
    fetches[0].wait()
    fetches[1].wait()
    puts = [pltpu.make_async_copy(both_ref, kv_ref, out_sems.at[parts])]
    puts[0].start()
    for i in range(parts):
        fetches[2 + i].wait()
        put = pltpu.make_async_copy(rows_ref.at[i], sent_ref.at[i], out_sems.at[i])
        put.start()
        puts.append(put)
    for put in puts:
        put.wait()


def split(hidden, base_key, base_value, parts):
    tokens, width = hidden.shape
    span = width // parts
    kv_width = base_key.shape[1]
    return pl.pallas_call(
        split_kernel,
        out_shape=(
            jax.ShapeDtypeStruct((parts, tokens, span), hidden.dtype),
            jax.ShapeDtypeStruct((tokens, 2 * kv_width), hidden.dtype),
        ),
        in_specs=[pl.BlockSpec(memory_space=pl.ANY)] * 3,
        out_specs=(pl.BlockSpec(memory_space=pl.ANY),) * 2,
        scratch_shapes=[
            pltpu.VMEM((parts, tokens, span), hidden.dtype),
            pltpu.VMEM((tokens, 2 * kv_width), hidden.dtype),
            pltpu.SemaphoreType.DMA((parts + 2,)),
            pltpu.SemaphoreType.DMA((parts + 1,)),
        ],
        name="split",
    )(hidden, base_key, base_value)


def shrink_kernel(block_len, place_ref, request_ref, adapter_ref, rows_ref, own_ref, other_ref, out_ref):
    sources, tokens, features = rows_ref.shape
    per_device = tokens // block_len
    half = features // CORES
    core = lax.rem(place_ref[0], CORES)
    own_columns = pl.ds(pl.multiple_of(core * half, half), half)
    other_columns = pl.ds(pl.multiple_of((1 - core) * half, half), half)
    first = pl.program_id(0) * sources
    for source in range(sources):
        device = (first + source) * CORES + core
        for part in range(per_device):
            adapter = adapter_ref[request_ref[device * per_device + part]]
            span = pl.ds(part * block_len, block_len)
            total = lax.dot_general(
                own_ref[adapter], rows_ref[source, span, own_columns], NT, preferred_element_type=jnp.float32
            ) + lax.dot_general(
                other_ref[adapter], rows_ref[source, span, other_columns], NT, preferred_element_type=jnp.float32
            )
            out_ref[source, :, span] = total.astype(out_ref.dtype)


def shrink(rows, own, other, place, block_request, request_adapter, block_len):
    chips, tokens, features = rows.shape
    adapters, width, half = own.shape
    steps = min(2, chips)
    sources = chips // steps
    return pl.pallas_call(
        functools.partial(shrink_kernel, block_len),
        out_shape=jax.ShapeDtypeStruct((chips, width, tokens), jnp.bfloat16),
        grid_spec=pltpu.PrefetchScalarGridSpec(
            num_scalar_prefetch=3,
            grid=(steps,),
            in_specs=[
                pl.BlockSpec((sources, tokens, features), lambda i, me, br, ra: (i, 0, 0)),
                pl.BlockSpec((adapters, width, half), lambda i, me, br, ra: (0, 0, 0)),
                pl.BlockSpec((adapters, width, half), lambda i, me, br, ra: (0, 0, 0)),
            ],
            out_specs=pl.BlockSpec((sources, width, tokens), lambda i, me, br, ra: (i, 0, 0)),
        ),
        cost_estimate=pl.CostEstimate(
            flops=2 * chips * tokens * features * width,
            bytes_accessed=2 * (rows.size + own.size + other.size),
            transcendentals=0,
        ),
        name="shrink",
    )(place, block_request, request_adapter, rows, own, other)


def finish_kernel(block_len, planes, place_ref, request_ref, adapter_ref, near_ref, flipped_ref, up_ref, *rest):
    pieces = planes * PLANE
    piece_refs = rest[:pieces]
    out_ref, base_ref, done_ref, in_sems, out_sems = rest[pieces:]
    tokens = piece_refs[0].shape[0]
    per_device = tokens // block_len
    rank = ADAPTER_RANK
    width = base_ref.shape[2] // 2
    me = place_ref[0]
    within = lax.rem(me, PLANE)
    for index in range(pieces):
        pltpu.make_async_copy(piece_refs[index], base_ref.at[index], in_sems.at[index]).start()
    for index in range(pieces):
        back, flip = index // PLANE, index % PLANE
        low_ref = flipped_ref if flip % CORES else near_ref
        low_index = back * (PLANE // CORES) + flip // CORES
        place = within ^ flip
        device = me - within - back * PLANE + place
        pltpu.make_async_copy(piece_refs[index], base_ref.at[index], in_sems.at[index]).wait()
        for part in range(per_device):
            adapter = adapter_ref[request_ref[jnp.maximum(device * per_device + part, 0)]]
            span = pl.ds(part * block_len, block_len)
            for which in range(2):
                columns = pl.ds(which * width, width)
                delta = lax.dot_general(
                    low_ref[low_index, pl.ds(which * rank, rank), span],
                    up_ref[adapter, :, columns],
                    TN,
                    preferred_element_type=jnp.float32,
                )
                done_ref[index, span, columns] = (
                    base_ref[index, span, columns].astype(jnp.float32) + delta
                ).astype(done_ref.dtype)
        slot = (planes - 1 - back) * PLANE + place
        pltpu.make_async_copy(
            done_ref.at[index], out_ref.at[pl.ds(pl.multiple_of(slot * tokens, tokens), tokens), :], out_sems.at[index]
        ).start()
    for index in range(pieces):
        pltpu.make_async_copy(done_ref.at[index], out_ref.at[pl.ds(0, tokens), :], out_sems.at[index]).wait()


def finish(pieces, near, flipped, up_weight, place, block_request, request_adapter, block_len, planes):
    tokens, width = pieces[0].shape
    count = len(pieces)
    return pl.pallas_call(
        functools.partial(finish_kernel, block_len, planes),
        out_shape=jax.ShapeDtypeStruct((count * tokens, width), jnp.bfloat16),
        grid_spec=pltpu.PrefetchScalarGridSpec(
            num_scalar_prefetch=3,
            grid=(1,),
            in_specs=[
                pl.BlockSpec(near.shape, lambda i, me, br, ra: (0, 0, 0)),
                pl.BlockSpec(near.shape, lambda i, me, br, ra: (0, 0, 0)),
                pl.BlockSpec(up_weight.shape, lambda i, me, br, ra: (0, 0, 0)),
            ]
            + [pl.BlockSpec(memory_space=pl.ANY)] * count,
            out_specs=pl.BlockSpec(memory_space=pl.ANY),
            scratch_shapes=[
                pltpu.VMEM((count, tokens, width), jnp.bfloat16),
                pltpu.VMEM((count, tokens, width), jnp.bfloat16),
                pltpu.SemaphoreType.DMA((count,)),
                pltpu.SemaphoreType.DMA((count,)),
            ],
        ),
        cost_estimate=pl.CostEstimate(
            flops=2 * count * tokens * width * ADAPTER_RANK, bytes_accessed=4 * count * tokens * width, transcendentals=0
        ),
        name="finish",
    )(place, block_request, request_adapter, near, flipped, up_weight, *pieces)


def attend_kernel(
    block_len, most_blocks, planes, piece, piece_count,
    place_ref, request_ref, q_ref, low_ref, up_ref, key_ref, value_ref, *rest,
):
    done_ref = rest[0] if piece > 0 else None
    out_ref, query_ref, total_ref, score_ref, top_ref, sum_ref = rest[-6:]
    tokens = q_ref.shape[0]
    per_device = tokens // block_len
    me = place_ref[0]
    within = lax.rem(me, PLANE)
    sources = up_ref.shape[0]
    span = up_ref.shape[3]
    heads = span // HEAD_SIZE
    group = sources * heads
    rows = group * block_len
    offsets = [(source * piece_count + piece) * span for source in range(sources)]
    for part in range(per_device):
        own_rows = pl.ds(part * block_len, block_len)
        for source in range(sources):
            columns = pl.ds(offsets[source], span)
            delta = lax.dot_general(
                low_ref[:, own_rows], up_ref[source, part], TN, preferred_element_type=jnp.float32
            )
            query = (q_ref[own_rows, columns].astype(jnp.float32) + delta).astype(jnp.bfloat16)
            for at in range(heads):
                row = part * rows + (source * heads + at) * block_len
                query_ref[pl.ds(row, block_len), :] = query[:, at * HEAD_SIZE : (at + 1) * HEAD_SIZE]

    first_block = me * per_device
    request = request_ref[first_block]
    count = jnp.int32(1)
    for back in range(1, most_blocks):
        earlier = request_ref[jnp.maximum(first_block - back, 0)]
        count = count + ((first_block >= back) & (earlier == request)).astype(jnp.int32)
    window_first = ((planes - 1) * PLANE + within) * per_device
    end = (window_first + per_device) * block_len
    starts = [(window_first - count + 1) * block_len]
    for part in range(1, per_device):
        same = request_ref[first_block + part] == request_ref[first_block + part - 1]
        starts.append(jnp.where(same, starts[-1], (window_first + part) * block_len))
    all_same = request_ref[first_block + per_device - 1] == request
    chunks = lax.div(end - starts[0] + (KEY_CHUNK - 1), KEY_CHUNK)
    factor = math.log2(math.e) / math.sqrt(HEAD_SIZE)

    def score(step, slot, parts, first, masked):
        stop = end - step * KEY_CHUNK
        start = stop - KEY_CHUNK
        if masked:
            start = jnp.maximum(start, 0)
        start = pl.multiple_of(start, block_len)
        for part in parts:
            columns = pl.ds(part * rows, rows)
            top = None
            for at in range(0, KEY_CHUNK, KEY_STEP):
                keys = key_ref[pl.ds(start + at, KEY_STEP), :]
                scores = lax.dot_general(keys, query_ref[columns, :], NT, preferred_element_type=jnp.float32)
                if masked:
                    key_at = start + at + lax.broadcasted_iota(jnp.int32, (KEY_STEP, 1), 0)
                    allowed = (key_at >= starts[part]) & (key_at < stop)
                    if first and at >= KEY_CHUNK - tokens - KEY_STEP + 1:
                        key_at = start + at + lax.broadcasted_iota(jnp.int32, scores.shape, 0)
                        query_at = (window_first + part) * block_len + lax.rem(
                            lax.broadcasted_iota(jnp.int32, scores.shape, 1), block_len
                        )
                        allowed = allowed & (key_at <= query_at)
                    scores = jnp.where(allowed, scores, -1e30)
                score_ref[slot, pl.ds(at, KEY_STEP), columns] = scores
                high = jnp.max(scores, axis=0, keepdims=True)
                top = high if top is None else jnp.maximum(top, high)
            if first:
                top_ref[slot, :, columns] = top
            else:
                top_ref[slot, :, columns] = jnp.maximum(top, top_ref[1 - slot, :, columns])

    def gather(step, slot, parts, first, masked):
        stop = end - step * KEY_CHUNK
        start = stop - KEY_CHUNK
        if masked:
            start = jnp.maximum(start, 0)
        start = pl.multiple_of(start, block_len)
        for part in parts:
            columns = pl.ds(part * rows, rows)
            top = top_ref[slot, :, columns]
            sums = None
            product = None
            for at in range(0, KEY_CHUNK, KEY_STEP):
                weights = jnp.exp2((score_ref[slot, pl.ds(at, KEY_STEP), columns] - top) * factor)
                more = jnp.sum(weights, axis=0, keepdims=True)
                values = value_ref[pl.ds(start + at, KEY_STEP), :]
                extra = lax.dot_general(
                    values, weights.astype(jnp.bfloat16), TN, preferred_element_type=jnp.float32
                )
                sums = more if sums is None else sums + more
                product = extra if product is None else product + extra
            if not first:
                fade = jnp.exp2((top_ref[1 - slot, :, columns] - top) * factor)
                sums = sums + sum_ref[:, columns] * fade
                product = product + total_ref[:, columns] * fade
            sum_ref[:, columns] = sums
            total_ref[:, columns] = product

    every = list(range(per_device))
    leading = every[: max(1, per_device - 1)]
    score(0, 0, every, True, True)

    @pl.when(chunks == 1)
    def _():
        gather(0, 0, every, True, True)

    @pl.when((chunks > 1) & all_same)
    def _():
        @pl.when(chunks == 2)
        def _():
            for part in every:
                score(1, 1, [part], False, True)
                gather(0, 0, [part], True, True)

        @pl.when(chunks > 2)
        def _():
            for part in every:
                score(1, 1, [part], False, False)
                gather(0, 0, [part], True, True)

            @pl.loop(2, chunks)
            def _(step):
                slot = lax.rem(step, 2)
                for part in every:
                    score(step, slot, [part], False, True)
                    gather(step - 1, 1 - slot, [part], False, False)

        gather(chunks - 1, lax.rem(chunks - 1, 2), every, False, True)

    @pl.when((chunks > 1) & jnp.logical_not(all_same))
    def _():
        gather(0, 0, every, True, True)

        @pl.loop(1, chunks)
        def _(step):
            slot = lax.rem(step, 2)
            score(step, slot, leading, False, True)
            gather(step, slot, leading, False, True)

    for part in every:
        columns = pl.ds(part * rows, rows)
        span_rows = pl.ds(part * block_len, block_len)
        result = (total_ref[:, columns] / sum_ref[:, columns]).T.astype(out_ref.dtype)
        for source in range(sources):
            for at in range(heads):
                row = (source * heads + at) * block_len
                out_ref[span_rows, pl.ds(offsets[source] + at * HEAD_SIZE, HEAD_SIZE)] = result[
                    row : row + block_len
                ]
    for source in range(sources):
        for other in range(piece):
            columns = pl.ds((source * piece_count + other) * span, span)
            out_ref[:, columns] = done_ref[:, columns]


def attend(q_base, low, up_rows, kv, place, block_request, block_len, most_blocks, planes, piece, piece_count, done):
    tokens, width = q_base.shape
    devices, per_device, rank, span = up_rows.shape
    window = kv.shape[0]
    head_span = width // KEY_VALUE_HEADS
    sources = devices // KEY_VALUE_HEADS
    lanes = tokens * sources * span // HEAD_SIZE
    earlier = [] if done is None else [done]
    return pl.pallas_call(
        functools.partial(attend_kernel, block_len, most_blocks, planes, piece, piece_count),
        out_shape=jax.ShapeDtypeStruct((tokens, width), jnp.bfloat16),
        grid_spec=pltpu.PrefetchScalarGridSpec(
            num_scalar_prefetch=2,
            grid=(KEY_VALUE_HEADS,),
            in_specs=[
                pl.BlockSpec((tokens, head_span), lambda m, me, br: (0, m)),
                pl.BlockSpec((rank, tokens), lambda m, me, br: (0, 0)),
                pl.BlockSpec((sources, per_device, rank, span), lambda m, me, br: (m, 0, 0, 0)),
                pl.BlockSpec((window, HEAD_SIZE), lambda m, me, br: (0, m)),
                pl.BlockSpec((window, HEAD_SIZE), lambda m, me, br: (0, KEY_VALUE_HEADS + m)),
            ]
            + [pl.BlockSpec((tokens, head_span), lambda m, me, br: (0, m))] * len(earlier),
            out_specs=pl.BlockSpec((tokens, head_span), lambda m, me, br: (0, m)),
            scratch_shapes=[
                pltpu.VMEM((lanes, HEAD_SIZE), jnp.bfloat16),
                pltpu.VMEM((HEAD_SIZE, lanes), jnp.float32),
                pltpu.VMEM((2, KEY_CHUNK, lanes), jnp.float32),
                pltpu.VMEM((2, 1, lanes), jnp.float32),
                pltpu.VMEM((1, lanes), jnp.float32),
            ],
        ),
        input_output_aliases={7: 0} if earlier else {},
        cost_estimate=pl.CostEstimate(
            flops=2 * tokens * width * window // piece_count,
            bytes_accessed=(16 << 20) // piece_count,
            transcendentals=(8 << 20) // piece_count,
        ),
        name="attend",
    )(place, block_request, q_base, low, up_rows, kv, kv, *earlier)


def body(
    hidden,
    q_base,
    base_key_weight,
    base_value_weight,
    shrink_a,
    expand_q,
    key_value_up_weight,
    block_request,
    request_adapter,
):
    tokens = hidden.shape[0]
    devices = lax.axis_size("seq")
    me = lax.axis_index("seq")
    place = me.astype(jnp.int32).reshape(1)
    block_count = block_request.shape[0]
    block_len = tokens * devices // block_count
    per_device = tokens // block_len
    most_blocks = min(MOST_BLOCKS_CAP, block_count // 2)
    hops = -(-(most_blocks - 1) // (PLANE * per_device))
    planes = hops + 1
    chips = devices // CORES
    same_core = [[chip * CORES + core for chip in range(chips)] for core in range(CORES)]
    forward = [(i, i + PLANE) for i in range(devices - PLANE)]
    swap_row = [(i, i ^ CORES) for i in range(devices)]
    swap_core = [(i, i ^ 1) for i in range(devices)]

    sent, kv = split(hidden, base_key_weight, base_value_weight, chips)
    rows = lax.all_to_all(
        sent, "seq", split_axis=0, concat_axis=0, axis_index_groups=same_core, tiled=True
    )
    down = jnp.swapaxes(shrink_a, 1, 2)
    other_down = lax.ppermute(down, "seq", swap_core)

    pieces = []
    own = kv
    for back in range(planes):
        if back > 0:
            own = lax.ppermute(own, "seq", forward)
        across = lax.ppermute(own, "seq", swap_row)
        flipped = lax.ppermute(own, "seq", swap_core)
        both = lax.ppermute(across, "seq", swap_core)
        pieces += [own, flipped, across, both]

    partials = shrink(rows, down, other_down, place, block_request, request_adapter, block_len)
    received = lax.all_to_all(
        partials, "seq", split_axis=0, concat_axis=0, axis_index_groups=same_core, tiled=True
    )

    piece_count = 1
    span = expand_q.shape[2] // piece_count
    adapter_of = jnp.sum(
        jnp.where(
            block_request[:, None] == jnp.arange(request_adapter.shape[0], dtype=jnp.int32)[None, :],
            request_adapter[None, :],
            0,
        ),
        axis=1,
    )
    up_pieces = []
    for piece in range(piece_count):
        picked = expand_q[:, :, piece * span : (piece + 1) * span][adapter_of]
        picked = picked.reshape(devices, per_device, ADAPTER_RANK, span)
        up_pieces.append(lax.all_to_all(picked, "seq", split_axis=0, concat_axis=0, tiled=True))

    low = jnp.sum(received.astype(jnp.float32), axis=0).astype(jnp.bfloat16)
    low_kv = low[ADAPTER_RANK:]
    near = []
    for back in range(planes):
        for flip in (0, CORES):
            if back == 0 and flip == 0:
                near.append(low_kv)
                continue
            pairs = [(i, (i ^ flip) + back * PLANE) for i in range(devices - back * PLANE)]
            near.append(lax.ppermute(low_kv, "seq", pairs))
    near = jnp.stack(near)
    flipped = lax.ppermute(near, "seq", swap_core)

    window = finish(
        pieces, near, flipped, key_value_up_weight, place, block_request, request_adapter, block_len, planes
    )
    out = None
    for piece in range(piece_count):
        out = attend(
            q_base, low[:ADAPTER_RANK], up_pieces[piece], window, place, block_request,
            block_len, most_blocks, planes, piece, piece_count, out,
        )
    return out


def solution(mesh):
    return jax.shard_map(
        body,
        mesh=mesh,
        in_specs=(
            P(("groups", "seq"), None),
            P(("groups", "seq"), None),
            P(("groups", "seq"), None),
            P(("groups", "seq"), None),
            P("groups", "seq", None),
            P("groups", None, "seq"),
            P("groups", None, None),
            P("groups"),
            P("groups"),
        ),
        out_specs=P(("groups", "seq"), None),
        check_vma=False,
    )
```

```python
import functools
import math

import jax
import jax.numpy as jnp
from jax import lax
from jax.experimental import pallas as pl
from jax.experimental.pallas import tpu as pltpu
from jax.sharding import PartitionSpec as P

KEY_VALUE_HEADS = 8
HEAD_SIZE = 128
ADAPTER_RANK = 64
MOST_BLOCKS_CAP = 32
CORES = 2
PLANE = 4
KEY_CHUNK = 512
KEY_STEP = 512
NT = (((1,), (1,)), ((), ()))
TN = (((0,), (0,)), ((), ()))


def split_kernel(hidden_ref, key_ref, value_ref, sent_ref, kv_ref, rows_ref, both_ref, in_sems, out_sems):
    parts, _, span = rows_ref.shape
    width = key_ref.shape[1]
    fetches = [
        pltpu.make_async_copy(key_ref, both_ref.at[:, pl.ds(0, width)], in_sems.at[parts]),
        pltpu.make_async_copy(value_ref, both_ref.at[:, pl.ds(width, width)], in_sems.at[parts + 1]),
    ]
    fetches += [
        pltpu.make_async_copy(hidden_ref.at[:, pl.ds(i * span, span)], rows_ref.at[i], in_sems.at[i])
        for i in range(parts)
    ]
    for fetch in fetches:
        fetch.start()
    fetches[0].wait()
    fetches[1].wait()
    puts = [pltpu.make_async_copy(both_ref, kv_ref, out_sems.at[parts])]
    puts[0].start()
    for i in range(parts):
        fetches[2 + i].wait()
        put = pltpu.make_async_copy(rows_ref.at[i], sent_ref.at[i], out_sems.at[i])
        put.start()
        puts.append(put)
    for put in puts:
        put.wait()


def split(hidden, base_key, base_value, parts):
    tokens, width = hidden.shape
    span = width // parts
    kv_width = base_key.shape[1]
    return pl.pallas_call(
        split_kernel,
        out_shape=(
            jax.ShapeDtypeStruct((parts, tokens, span), hidden.dtype),
            jax.ShapeDtypeStruct((tokens, 2 * kv_width), hidden.dtype),
        ),
        in_specs=[pl.BlockSpec(memory_space=pl.ANY)] * 3,
        out_specs=(pl.BlockSpec(memory_space=pl.ANY),) * 2,
        scratch_shapes=[
            pltpu.VMEM((parts, tokens, span), hidden.dtype),
            pltpu.VMEM((tokens, 2 * kv_width), hidden.dtype),
            pltpu.SemaphoreType.DMA((parts + 2,)),
            pltpu.SemaphoreType.DMA((parts + 1,)),
        ],
        name="split",
    )(hidden, base_key, base_value)


def shrink_kernel(block_len, place_ref, request_ref, adapter_ref, rows_ref, own_ref, other_ref, out_ref):
    sources, tokens, features = rows_ref.shape
    per_device = tokens // block_len
    half = features // CORES
    core = lax.rem(place_ref[0], CORES)
    own_columns = pl.ds(pl.multiple_of(core * half, half), half)
    other_columns = pl.ds(pl.multiple_of((1 - core) * half, half), half)
    first = pl.program_id(0) * sources
    for source in range(sources):
        device = (first + source) * CORES + core
        for part in range(per_device):
            adapter = adapter_ref[request_ref[device * per_device + part]]
            span = pl.ds(part * block_len, block_len)
            total = lax.dot_general(
                own_ref[adapter], rows_ref[source, span, own_columns], NT, preferred_element_type=jnp.float32
            ) + lax.dot_general(
                other_ref[adapter], rows_ref[source, span, other_columns], NT, preferred_element_type=jnp.float32
            )
            out_ref[source, :, span] = total.astype(out_ref.dtype)


def shrink(rows, own, other, place, block_request, request_adapter, block_len):
    chips, tokens, features = rows.shape
    adapters, width, half = own.shape
    steps = min(2, chips)
    sources = chips // steps
    return pl.pallas_call(
        functools.partial(shrink_kernel, block_len),
        out_shape=jax.ShapeDtypeStruct((chips, width, tokens), jnp.bfloat16),
        grid_spec=pltpu.PrefetchScalarGridSpec(
            num_scalar_prefetch=3,
            grid=(steps,),
            in_specs=[
                pl.BlockSpec((sources, tokens, features), lambda i, me, br, ra: (i, 0, 0)),
                pl.BlockSpec((adapters, width, half), lambda i, me, br, ra: (0, 0, 0)),
                pl.BlockSpec((adapters, width, half), lambda i, me, br, ra: (0, 0, 0)),
            ],
            out_specs=pl.BlockSpec((sources, width, tokens), lambda i, me, br, ra: (i, 0, 0)),
        ),
        cost_estimate=pl.CostEstimate(
            flops=2 * chips * tokens * features * width,
            bytes_accessed=2 * (rows.size + own.size + other.size),
            transcendentals=0,
        ),
        name="shrink",
    )(place, block_request, request_adapter, rows, own, other)


def finish_kernel(block_len, planes, place_ref, request_ref, adapter_ref, near_ref, flipped_ref, up_ref, *rest):
    pieces = planes * PLANE
    piece_refs = rest[:pieces]
    out_ref, base_ref, done_ref, in_sems, out_sems = rest[pieces:]
    tokens = piece_refs[0].shape[0]
    per_device = tokens // block_len
    rank = ADAPTER_RANK
    width = base_ref.shape[2] // 2
    me = place_ref[0]
    within = lax.rem(me, PLANE)
    for index in range(pieces):
        pltpu.make_async_copy(piece_refs[index], base_ref.at[index], in_sems.at[index]).start()
    for index in range(pieces):
        back, flip = index // PLANE, index % PLANE
        low_ref = flipped_ref if flip % CORES else near_ref
        low_index = back * (PLANE // CORES) + flip // CORES
        place = within ^ flip
        device = me - within - back * PLANE + place
        pltpu.make_async_copy(piece_refs[index], base_ref.at[index], in_sems.at[index]).wait()
        for part in range(per_device):
            adapter = adapter_ref[request_ref[jnp.maximum(device * per_device + part, 0)]]
            span = pl.ds(part * block_len, block_len)
            for which in range(2):
                columns = pl.ds(which * width, width)
                delta = lax.dot_general(
                    low_ref[low_index, pl.ds(which * rank, rank), span],
                    up_ref[adapter, :, columns],
                    TN,
                    preferred_element_type=jnp.float32,
                )
                done_ref[index, span, columns] = (
                    base_ref[index, span, columns].astype(jnp.float32) + delta
                ).astype(done_ref.dtype)
        slot = (planes - 1 - back) * PLANE + place
        pltpu.make_async_copy(
            done_ref.at[index], out_ref.at[pl.ds(pl.multiple_of(slot * tokens, tokens), tokens), :], out_sems.at[index]
        ).start()
    for index in range(pieces):
        pltpu.make_async_copy(done_ref.at[index], out_ref.at[pl.ds(0, tokens), :], out_sems.at[index]).wait()


def finish(pieces, near, flipped, up_weight, place, block_request, request_adapter, block_len, planes):
    tokens, width = pieces[0].shape
    count = len(pieces)
    return pl.pallas_call(
        functools.partial(finish_kernel, block_len, planes),
        out_shape=jax.ShapeDtypeStruct((count * tokens, width), jnp.bfloat16),
        grid_spec=pltpu.PrefetchScalarGridSpec(
            num_scalar_prefetch=3,
            grid=(1,),
            in_specs=[
                pl.BlockSpec(near.shape, lambda i, me, br, ra: (0, 0, 0)),
                pl.BlockSpec(near.shape, lambda i, me, br, ra: (0, 0, 0)),
                pl.BlockSpec(up_weight.shape, lambda i, me, br, ra: (0, 0, 0)),
            ]
            + [pl.BlockSpec(memory_space=pl.ANY)] * count,
            out_specs=pl.BlockSpec(memory_space=pl.ANY),
            scratch_shapes=[
                pltpu.VMEM((count, tokens, width), jnp.bfloat16),
                pltpu.VMEM((count, tokens, width), jnp.bfloat16),
                pltpu.SemaphoreType.DMA((count,)),
                pltpu.SemaphoreType.DMA((count,)),
            ],
        ),
        cost_estimate=pl.CostEstimate(
            flops=2 * count * tokens * width * ADAPTER_RANK, bytes_accessed=4 * count * tokens * width, transcendentals=0
        ),
        name="finish",
    )(place, block_request, request_adapter, near, flipped, up_weight, *pieces)


def attend_kernel(
    block_len, most_blocks, planes,
    place_ref, request_ref, q_ref, low_ref, *rest,
):
    up_refs = rest[:-8]
    key_ref, value_ref, out_ref, query_ref, total_ref, score_ref, top_ref, sum_ref = rest[-8:]
    tokens = q_ref.shape[0]
    per_device = tokens // block_len
    me = place_ref[0]
    within = lax.rem(me, PLANE)
    sources = len(up_refs)
    span = up_refs[0].shape[4]
    heads = span // HEAD_SIZE
    group = sources * heads
    rows = group * block_len
    offsets = [source * span for source in range(sources)]
    for part in range(per_device):
        own_rows = pl.ds(part * block_len, block_len)
        for source in range(sources):
            columns = pl.ds(offsets[source], span)
            delta = lax.dot_general(
                low_ref[:, own_rows], up_refs[source][0, 0, part], TN, preferred_element_type=jnp.float32
            )
            query = (q_ref[own_rows, columns].astype(jnp.float32) + delta).astype(jnp.bfloat16)
            for at in range(heads):
                row = part * rows + (source * heads + at) * block_len
                query_ref[pl.ds(row, block_len), :] = query[:, at * HEAD_SIZE : (at + 1) * HEAD_SIZE]

    first_block = me * per_device
    request = request_ref[first_block]
    count = jnp.int32(1)
    for back in range(1, most_blocks):
        earlier = request_ref[jnp.maximum(first_block - back, 0)]
        count = count + ((first_block >= back) & (earlier == request)).astype(jnp.int32)
    window_first = ((planes - 1) * PLANE + within) * per_device
    end = (window_first + per_device) * block_len
    starts = [(window_first - count + 1) * block_len]
    for part in range(1, per_device):
        same = request_ref[first_block + part] == request_ref[first_block + part - 1]
        starts.append(jnp.where(same, starts[-1], (window_first + part) * block_len))
    all_same = request_ref[first_block + per_device - 1] == request
    chunks = lax.div(end - starts[0] + (KEY_CHUNK - 1), KEY_CHUNK)
    factor = math.log2(math.e) / math.sqrt(HEAD_SIZE)

    def score(step, slot, parts, first, masked):
        stop = end - step * KEY_CHUNK
        start = stop - KEY_CHUNK
        if masked:
            start = jnp.maximum(start, 0)
        start = pl.multiple_of(start, block_len)
        for part in parts:
            columns = pl.ds(part * rows, rows)
            top = None
            for at in range(0, KEY_CHUNK, KEY_STEP):
                keys = key_ref[pl.ds(start + at, KEY_STEP), :]
                scores = lax.dot_general(keys, query_ref[columns, :], NT, preferred_element_type=jnp.float32)
                if masked:
                    key_at = start + at + lax.broadcasted_iota(jnp.int32, (KEY_STEP, 1), 0)
                    allowed = (key_at >= starts[part]) & (key_at < stop)
                    if first and at >= KEY_CHUNK - tokens - KEY_STEP + 1:
                        key_at = start + at + lax.broadcasted_iota(jnp.int32, scores.shape, 0)
                        query_at = (window_first + part) * block_len + lax.rem(
                            lax.broadcasted_iota(jnp.int32, scores.shape, 1), block_len
                        )
                        allowed = allowed & (key_at <= query_at)
                    scores = jnp.where(allowed, scores, -1e30)
                score_ref[slot, pl.ds(at, KEY_STEP), columns] = scores
                high = jnp.max(scores, axis=0, keepdims=True)
                top = high if top is None else jnp.maximum(top, high)
            if first:
                top_ref[slot, :, columns] = top
            else:
                top_ref[slot, :, columns] = jnp.maximum(top, top_ref[1 - slot, :, columns])

    def gather(step, slot, parts, first, masked):
        stop = end - step * KEY_CHUNK
        start = stop - KEY_CHUNK
        if masked:
            start = jnp.maximum(start, 0)
        start = pl.multiple_of(start, block_len)
        for part in parts:
            columns = pl.ds(part * rows, rows)
            top = top_ref[slot, :, columns]
            sums = None
            product = None
            for at in range(0, KEY_CHUNK, KEY_STEP):
                weights = jnp.exp2((score_ref[slot, pl.ds(at, KEY_STEP), columns] - top) * factor)
                more = jnp.sum(weights, axis=0, keepdims=True)
                values = value_ref[pl.ds(start + at, KEY_STEP), :]
                extra = lax.dot_general(
                    values, weights.astype(jnp.bfloat16), TN, preferred_element_type=jnp.float32
                )
                sums = more if sums is None else sums + more
                product = extra if product is None else product + extra
            if not first:
                fade = jnp.exp2((top_ref[1 - slot, :, columns] - top) * factor)
                sums = sums + sum_ref[:, columns] * fade
                product = product + total_ref[:, columns] * fade
            sum_ref[:, columns] = sums
            total_ref[:, columns] = product

    every = list(range(per_device))
    leading = every[: max(1, per_device - 1)]
    score(0, 0, every, True, True)

    @pl.when(chunks == 1)
    def _():
        gather(0, 0, every, True, True)

    @pl.when((chunks > 1) & all_same)
    def _():
        @pl.when(chunks == 2)
        def _():
            for part in every:
                score(1, 1, [part], False, True)
                gather(0, 0, [part], True, True)

        @pl.when(chunks > 2)
        def _():
            for part in every:
                score(1, 1, [part], False, False)
                gather(0, 0, [part], True, True)

            @pl.loop(2, chunks)
            def _(step):
                slot = lax.rem(step, 2)
                for part in every:
                    score(step, slot, [part], False, True)
                    gather(step - 1, 1 - slot, [part], False, False)

        gather(chunks - 1, lax.rem(chunks - 1, 2), every, False, True)

    @pl.when((chunks > 1) & jnp.logical_not(all_same))
    def _():
        gather(0, 0, every, True, True)

        @pl.loop(1, chunks)
        def _(step):
            slot = lax.rem(step, 2)
            score(step, slot, leading, False, True)
            gather(step, slot, leading, False, True)

    for part in every:
        columns = pl.ds(part * rows, rows)
        span_rows = pl.ds(part * block_len, block_len)
        result = (total_ref[:, columns] / sum_ref[:, columns]).T.astype(out_ref.dtype)
        for source in range(sources):
            for at in range(heads):
                row = (source * heads + at) * block_len
                out_ref[span_rows, pl.ds(offsets[source] + at * HEAD_SIZE, HEAD_SIZE)] = result[
                    row : row + block_len
                ]


def attend(q_base, low, up_rows, kv, place, block_request, block_len, most_blocks, planes, devices):
    tokens, width = q_base.shape
    half, _, per_device, rank, span = up_rows.shape
    window = kv.shape[0]
    head_span = width // KEY_VALUE_HEADS
    sources = devices // KEY_VALUE_HEADS
    lanes = tokens * head_span // HEAD_SIZE

    def up_spec(source):
        def index(m, me, br):
            owner = m * sources + source
            far = lax.div(owner, half) ^ lax.div(me[0], half)
            return lax.rem(owner, half) ^ lax.rem(me[0], half), far, 0, 0, 0

        return pl.BlockSpec((1, 1, per_device, rank, span), index)

    return pl.pallas_call(
        functools.partial(attend_kernel, block_len, most_blocks, planes),
        out_shape=jax.ShapeDtypeStruct((tokens, width), jnp.bfloat16),
        grid_spec=pltpu.PrefetchScalarGridSpec(
            num_scalar_prefetch=2,
            grid=(KEY_VALUE_HEADS,),
            in_specs=[
                pl.BlockSpec((tokens, head_span), lambda m, me, br: (0, m)),
                pl.BlockSpec((rank, tokens), lambda m, me, br: (0, 0)),
            ]
            + [up_spec(source) for source in range(sources)]
            + [
                pl.BlockSpec((window, HEAD_SIZE), lambda m, me, br: (0, m)),
                pl.BlockSpec((window, HEAD_SIZE), lambda m, me, br: (0, KEY_VALUE_HEADS + m)),
            ],
            out_specs=pl.BlockSpec((tokens, head_span), lambda m, me, br: (0, m)),
            scratch_shapes=[
                pltpu.VMEM((lanes, HEAD_SIZE), jnp.bfloat16),
                pltpu.VMEM((HEAD_SIZE, lanes), jnp.float32),
                pltpu.VMEM((2, KEY_CHUNK, lanes), jnp.float32),
                pltpu.VMEM((2, 1, lanes), jnp.float32),
                pltpu.VMEM((1, lanes), jnp.float32),
            ],
        ),
        cost_estimate=pl.CostEstimate(
            flops=2 * tokens * width * window, bytes_accessed=16 << 20, transcendentals=8 << 20
        ),
        name="attend",
    )(place, block_request, q_base, low, *[up_rows] * sources, kv, kv)


def body(
    hidden,
    q_base,
    base_key_weight,
    base_value_weight,
    shrink_a,
    expand_q,
    key_value_up_weight,
    block_request,
    request_adapter,
):
    tokens = hidden.shape[0]
    devices = lax.axis_size("seq")
    me = lax.axis_index("seq")
    place = me.astype(jnp.int32).reshape(1)
    block_count = block_request.shape[0]
    block_len = tokens * devices // block_count
    per_device = tokens // block_len
    most_blocks = min(MOST_BLOCKS_CAP, block_count // 2)
    hops = -(-(most_blocks - 1) // (PLANE * per_device))
    planes = hops + 1
    chips = devices // CORES
    same_core = [[chip * CORES + core for chip in range(chips)] for core in range(CORES)]
    forward = [(i, i + PLANE) for i in range(devices - PLANE)]
    swap_row = [(i, i ^ CORES) for i in range(devices)]
    swap_core = [(i, i ^ 1) for i in range(devices)]

    sent, kv = split(hidden, base_key_weight, base_value_weight, chips)
    half = devices // 2
    near_up = expand_q[request_adapter]
    far_up = lax.ppermute(near_up, "seq", [(i, i ^ half) for i in range(devices)])
    targets = (me ^ jnp.arange(half, dtype=jnp.int32))[:, None] * per_device
    wanted = block_request[targets + jnp.arange(per_device, dtype=jnp.int32)[None, :]]
    picked = jnp.stack([near_up[wanted], far_up[wanted]], axis=1)
    spread = [picked[0]]
    for step in range(1, half):
        spread.append(lax.ppermute(picked[step], "seq", [(i, i ^ step) for i in range(devices)]))
    rows = lax.all_to_all(
        sent, "seq", split_axis=0, concat_axis=0, axis_index_groups=same_core, tiled=True
    )
    down = jnp.swapaxes(shrink_a, 1, 2)
    other_down = lax.ppermute(down, "seq", swap_core)

    pieces = []
    own = kv
    for back in range(planes):
        if back > 0:
            own = lax.ppermute(own, "seq", forward)
        across = lax.ppermute(own, "seq", swap_row)
        flipped = lax.ppermute(own, "seq", swap_core)
        both = lax.ppermute(across, "seq", swap_core)
        pieces += [own, flipped, across, both]

    partials = shrink(rows, down, other_down, place, block_request, request_adapter, block_len)
    received = lax.all_to_all(
        partials, "seq", split_axis=0, concat_axis=0, axis_index_groups=same_core, tiled=True
    )

    low = jnp.sum(received.astype(jnp.float32), axis=0).astype(jnp.bfloat16)
    low_kv = low[ADAPTER_RANK:]
    near = []
    for back in range(planes):
        for flip in (0, CORES):
            if back == 0 and flip == 0:
                near.append(low_kv)
                continue
            pairs = [(i, (i ^ flip) + back * PLANE) for i in range(devices - back * PLANE)]
            near.append(lax.ppermute(low_kv, "seq", pairs))
    near = jnp.stack(near)
    flipped = lax.ppermute(near, "seq", swap_core)

    window = finish(
        pieces, near, flipped, key_value_up_weight, place, block_request, request_adapter, block_len, planes
    )
    return attend(
        q_base, low[:ADAPTER_RANK], jnp.stack(spread), window, place, block_request,
        block_len, most_blocks, planes, devices,
    )


def solution(mesh):
    return jax.shard_map(
        body,
        mesh=mesh,
        in_specs=(
            P(("groups", "seq"), None),
            P(("groups", "seq"), None),
            P(("groups", "seq"), None),
            P(("groups", "seq"), None),
            P("groups", "seq", None),
            P("groups", None, "seq"),
            P("groups", None, None),
            P("groups"),
            P("groups"),
        ),
        out_specs=P(("groups", "seq"), None),
        check_vma=False,
    )
```

```python
import functools
import math

import jax
import jax.numpy as jnp
from jax import lax
from jax.experimental import pallas as pl
from jax.experimental.pallas import tpu as pltpu
from jax.sharding import PartitionSpec as P

KEY_VALUE_HEADS = 8
HEAD_SIZE = 128
ADAPTER_RANK = 64
MOST_BLOCKS_CAP = 32
CORES = 2
PLANE = 4
KEY_CHUNK = 512
KEY_STEP = 512
NT = (((1,), (1,)), ((), ()))
TN = (((0,), (0,)), ((), ()))


def split_kernel(hidden_ref, key_ref, value_ref, sent_ref, kv_ref, rows_ref, both_ref, in_sems, out_sems):
    parts, _, span = rows_ref.shape
    width = key_ref.shape[1]
    fetches = [
        pltpu.make_async_copy(key_ref, both_ref.at[:, pl.ds(0, width)], in_sems.at[parts]),
        pltpu.make_async_copy(value_ref, both_ref.at[:, pl.ds(width, width)], in_sems.at[parts + 1]),
    ]
    fetches += [
        pltpu.make_async_copy(hidden_ref.at[:, pl.ds(i * span, span)], rows_ref.at[i], in_sems.at[i])
        for i in range(parts)
    ]
    for fetch in fetches:
        fetch.start()
    fetches[0].wait()
    fetches[1].wait()
    puts = [pltpu.make_async_copy(both_ref, kv_ref, out_sems.at[parts])]
    puts[0].start()
    for i in range(parts):
        fetches[2 + i].wait()
        put = pltpu.make_async_copy(rows_ref.at[i], sent_ref.at[i], out_sems.at[i])
        put.start()
        puts.append(put)
    for put in puts:
        put.wait()


def split(hidden, base_key, base_value, parts):
    tokens, width = hidden.shape
    span = width // parts
    kv_width = base_key.shape[1]
    return pl.pallas_call(
        split_kernel,
        out_shape=(
            jax.ShapeDtypeStruct((parts, tokens, span), hidden.dtype),
            jax.ShapeDtypeStruct((tokens, 2 * kv_width), hidden.dtype),
        ),
        in_specs=[pl.BlockSpec(memory_space=pl.ANY)] * 3,
        out_specs=(pl.BlockSpec(memory_space=pl.ANY),) * 2,
        scratch_shapes=[
            pltpu.VMEM((parts, tokens, span), hidden.dtype),
            pltpu.VMEM((tokens, 2 * kv_width), hidden.dtype),
            pltpu.SemaphoreType.DMA((parts + 2,)),
            pltpu.SemaphoreType.DMA((parts + 1,)),
        ],
        name="split",
    )(hidden, base_key, base_value)


def shrink_kernel(block_len, place_ref, request_ref, adapter_ref, rows_ref, own_ref, other_ref, out_ref):
    sources, tokens, features = rows_ref.shape
    per_device = tokens // block_len
    half = features // CORES
    core = lax.rem(place_ref[0], CORES)
    own_columns = pl.ds(pl.multiple_of(core * half, half), half)
    other_columns = pl.ds(pl.multiple_of((1 - core) * half, half), half)
    first = pl.program_id(0) * sources
    for source in range(sources):
        device = (first + source) * CORES + core
        picks = [adapter_ref[request_ref[device * per_device + part]] for part in range(per_device)]
        shared = picks[0] == picks[-1]
        for pick in picks[1:-1]:
            shared = shared & (pick == picks[0])

        def put(adapter, span):
            total = lax.dot_general(
                own_ref[adapter], rows_ref[source, span, own_columns], NT, preferred_element_type=jnp.float32
            ) + lax.dot_general(
                other_ref[adapter], rows_ref[source, span, other_columns], NT, preferred_element_type=jnp.float32
            )
            out_ref[source, :, span] = total.astype(out_ref.dtype)

        @pl.when(shared)
        def _():
            put(picks[0], pl.ds(0, tokens))

        @pl.when(jnp.logical_not(shared))
        def _():
            for part in range(per_device):
                put(picks[part], pl.ds(part * block_len, block_len))


def shrink(rows, own, other, place, block_request, request_adapter, block_len):
    chips, tokens, features = rows.shape
    adapters, width, half = own.shape
    steps = min(2, chips)
    sources = chips // steps
    return pl.pallas_call(
        functools.partial(shrink_kernel, block_len),
        out_shape=jax.ShapeDtypeStruct((chips, width, tokens), jnp.bfloat16),
        grid_spec=pltpu.PrefetchScalarGridSpec(
            num_scalar_prefetch=3,
            grid=(steps,),
            in_specs=[
                pl.BlockSpec((sources, tokens, features), lambda i, me, br, ra: (i, 0, 0)),
                pl.BlockSpec((adapters, width, half), lambda i, me, br, ra: (0, 0, 0)),
                pl.BlockSpec((adapters, width, half), lambda i, me, br, ra: (0, 0, 0)),
            ],
            out_specs=pl.BlockSpec((sources, width, tokens), lambda i, me, br, ra: (i, 0, 0)),
        ),
        cost_estimate=pl.CostEstimate(
            flops=2 * chips * tokens * features * width,
            bytes_accessed=2 * (rows.size + own.size + other.size),
            transcendentals=0,
        ),
        name="shrink",
    )(place, block_request, request_adapter, rows, own, other)


def join_kernel(*refs):
    for index, ref in enumerate(refs[:-1]):
        refs[-1][index] = ref[...]


def join(parts):
    return pl.pallas_call(
        join_kernel,
        out_shape=jax.ShapeDtypeStruct((len(parts), *parts[0].shape), parts[0].dtype),
        name="join",
    )(*parts)


def finish_kernel(block_len, planes, place_ref, request_ref, adapter_ref, near_ref, flipped_ref, up_ref, *rest):
    pieces = planes * PLANE
    piece_refs = rest[:pieces]
    out_ref, base_ref, done_ref, in_sems, out_sems = rest[pieces:]
    tokens = piece_refs[0].shape[0]
    per_device = tokens // block_len
    rank = ADAPTER_RANK
    width = base_ref.shape[2] // 2
    me = place_ref[0]
    within = lax.rem(me, PLANE)
    for index in range(pieces):
        pltpu.make_async_copy(piece_refs[index], base_ref.at[index], in_sems.at[index]).start()
    for index in range(pieces):
        back, flip = index // PLANE, index % PLANE
        low_ref = flipped_ref if flip % CORES else near_ref
        low_index = back * (PLANE // CORES) + flip // CORES
        place = within ^ flip
        pltpu.make_async_copy(piece_refs[index], base_ref.at[index], in_sems.at[index]).wait()
        spans = [(0, tokens)] if index else [(part * block_len, block_len) for part in range(per_device)]
        for part, (at, length) in enumerate(spans):
            adapter = adapter_ref[request_ref[me * per_device + part]]
            span = pl.ds(at, length)
            for which in range(2):
                columns = pl.ds(which * width, width)
                delta = lax.dot_general(
                    low_ref[low_index, pl.ds(which * rank, rank), span],
                    up_ref[adapter, :, columns],
                    TN,
                    preferred_element_type=jnp.float32,
                )
                done_ref[index, span, columns] = (
                    base_ref[index, span, columns].astype(jnp.float32) + delta
                ).astype(done_ref.dtype)
        slot = (planes - 1 - back) * PLANE + place
        pltpu.make_async_copy(
            done_ref.at[index], out_ref.at[pl.ds(pl.multiple_of(slot * tokens, tokens), tokens), :], out_sems.at[index]
        ).start()
    for index in range(pieces):
        pltpu.make_async_copy(done_ref.at[index], out_ref.at[pl.ds(0, tokens), :], out_sems.at[index]).wait()


def finish(pieces, near, flipped, up_weight, place, block_request, request_adapter, block_len, planes):
    tokens, width = pieces[0].shape
    count = len(pieces)
    return pl.pallas_call(
        functools.partial(finish_kernel, block_len, planes),
        out_shape=jax.ShapeDtypeStruct((count * tokens, width), jnp.bfloat16),
        grid_spec=pltpu.PrefetchScalarGridSpec(
            num_scalar_prefetch=3,
            grid=(1,),
            in_specs=[
                pl.BlockSpec(near.shape, lambda i, me, br, ra: (0, 0, 0)),
                pl.BlockSpec(near.shape, lambda i, me, br, ra: (0, 0, 0)),
                pl.BlockSpec(up_weight.shape, lambda i, me, br, ra: (0, 0, 0)),
            ]
            + [pl.BlockSpec(memory_space=pl.ANY)] * count,
            out_specs=pl.BlockSpec(memory_space=pl.ANY),
            scratch_shapes=[
                pltpu.VMEM((count, tokens, width), jnp.bfloat16),
                pltpu.VMEM((count, tokens, width), jnp.bfloat16),
                pltpu.SemaphoreType.DMA((count,)),
                pltpu.SemaphoreType.DMA((count,)),
            ],
        ),
        cost_estimate=pl.CostEstimate(
            flops=2 * count * tokens * width * ADAPTER_RANK, bytes_accessed=4 * count * tokens * width, transcendentals=0
        ),
        name="finish",
    )(place, block_request, request_adapter, near, flipped, up_weight, *pieces)


def attend_kernel(
    block_len, most_blocks, planes,
    place_ref, request_ref, q_ref, low_ref, *rest,
):
    key_ref, value_ref = rest[:2]
    out_ref, up_ref, query_ref, total_ref, score_ref, top_ref, sum_ref, sems = rest[-8:]
    spread_refs = rest[2:-8]
    head = pl.program_id(0)
    half, _, _, _, span = up_ref.shape

    @pl.when(head == 0)
    def _():
        for step, ref in enumerate(spread_refs):
            pltpu.make_async_copy(ref, up_ref.at[step], sems.at[step]).start()
        for step, ref in enumerate(spread_refs):
            pltpu.make_async_copy(ref, up_ref.at[step], sems.at[step]).wait()

    tokens = q_ref.shape[0]
    per_device = tokens // block_len
    me = place_ref[0]
    within = lax.rem(me, PLANE)
    sources = q_ref.shape[1] // span
    heads = span // HEAD_SIZE
    group = sources * heads
    rows = group * block_len
    offsets = [source * span for source in range(sources)]
    for part in range(per_device):
        own_rows = pl.ds(part * block_len, block_len)
        for source in range(sources):
            columns = pl.ds(offsets[source], span)
            owner = head * sources + source
            far = lax.div(owner, half) ^ lax.div(me, half)
            step = lax.rem(owner, half) ^ lax.rem(me, half)
            delta = lax.dot_general(
                low_ref[:, own_rows], up_ref[step, far, part], TN, preferred_element_type=jnp.float32
            )
            query = (q_ref[own_rows, columns].astype(jnp.float32) + delta).astype(jnp.bfloat16)
            for at in range(heads):
                row = part * rows + (source * heads + at) * block_len
                query_ref[pl.ds(row, block_len), :] = query[:, at * HEAD_SIZE : (at + 1) * HEAD_SIZE]

    first_block = me * per_device
    request = request_ref[first_block]
    count = jnp.int32(1)
    for back in range(1, most_blocks):
        earlier = request_ref[jnp.maximum(first_block - back, 0)]
        count = count + ((first_block >= back) & (earlier == request)).astype(jnp.int32)
    window_first = ((planes - 1) * PLANE + within) * per_device
    end = (window_first + per_device) * block_len
    starts = [(window_first - count + 1) * block_len]
    for part in range(1, per_device):
        same = request_ref[first_block + part] == request_ref[first_block + part - 1]
        starts.append(jnp.where(same, starts[-1], (window_first + part) * block_len))
    all_same = request_ref[first_block + per_device - 1] == request
    chunks = lax.div(end - starts[0] + (KEY_CHUNK - 1), KEY_CHUNK)
    factor = math.log2(math.e) / math.sqrt(HEAD_SIZE)

    def score(step, slot, parts, first, masked):
        stop = end - step * KEY_CHUNK
        start = stop - KEY_CHUNK
        if masked:
            start = jnp.maximum(start, 0)
        start = pl.multiple_of(start, block_len)
        for part in parts:
            columns = pl.ds(part * rows, rows)
            top = None
            for at in range(0, KEY_CHUNK, KEY_STEP):
                keys = key_ref[pl.ds(start + at, KEY_STEP), :]
                scores = lax.dot_general(keys, query_ref[columns, :], NT, preferred_element_type=jnp.float32)
                if masked:
                    key_at = start + at + lax.broadcasted_iota(jnp.int32, (KEY_STEP, 1), 0)
                    allowed = (key_at >= starts[part]) & (key_at < stop)
                    if first and at >= KEY_CHUNK - tokens - KEY_STEP + 1:
                        key_at = start + at + lax.broadcasted_iota(jnp.int32, scores.shape, 0)
                        query_at = (window_first + part) * block_len + lax.rem(
                            lax.broadcasted_iota(jnp.int32, scores.shape, 1), block_len
                        )
                        allowed = allowed & (key_at <= query_at)
                    scores = jnp.where(allowed, scores, -1e30)
                score_ref[slot, pl.ds(at, KEY_STEP), columns] = scores
                high = jnp.max(scores, axis=0, keepdims=True)
                top = high if top is None else jnp.maximum(top, high)
            if first:
                top_ref[slot, :, columns] = top
            else:
                top_ref[slot, :, columns] = jnp.maximum(top, top_ref[1 - slot, :, columns])

    def gather(step, slot, parts, first, masked):
        stop = end - step * KEY_CHUNK
        start = stop - KEY_CHUNK
        if masked:
            start = jnp.maximum(start, 0)
        start = pl.multiple_of(start, block_len)
        for part in parts:
            columns = pl.ds(part * rows, rows)
            top = top_ref[slot, :, columns]
            sums = None
            product = None
            for at in range(0, KEY_CHUNK, KEY_STEP):
                weights = jnp.exp2((score_ref[slot, pl.ds(at, KEY_STEP), columns] - top) * factor)
                more = jnp.sum(weights, axis=0, keepdims=True)
                values = value_ref[pl.ds(start + at, KEY_STEP), :]
                extra = lax.dot_general(
                    values, weights.astype(jnp.bfloat16), TN, preferred_element_type=jnp.float32
                )
                sums = more if sums is None else sums + more
                product = extra if product is None else product + extra
            if not first:
                fade = jnp.exp2((top_ref[1 - slot, :, columns] - top) * factor)
                sums = sums + sum_ref[:, columns] * fade
                product = product + total_ref[:, columns] * fade
            sum_ref[:, columns] = sums
            total_ref[:, columns] = product

    every = list(range(per_device))
    leading = every[: max(1, per_device - 1)]
    score(0, 0, every, True, True)

    @pl.when(chunks == 1)
    def _():
        gather(0, 0, every, True, True)

    @pl.when((chunks > 1) & all_same)
    def _():
        @pl.when(chunks == 2)
        def _():
            for part in every:
                score(1, 1, [part], False, True)
                gather(0, 0, [part], True, True)

        @pl.when(chunks > 2)
        def _():
            for part in every:
                score(1, 1, [part], False, False)
                gather(0, 0, [part], True, True)

            @pl.loop(2, chunks)
            def _(step):
                slot = lax.rem(step, 2)
                for part in every:
                    score(step, slot, [part], False, True)
                    gather(step - 1, 1 - slot, [part], False, False)

        gather(chunks - 1, lax.rem(chunks - 1, 2), every, False, True)

    @pl.when((chunks > 1) & jnp.logical_not(all_same))
    def _():
        gather(0, 0, every, True, True)

        @pl.loop(1, chunks)
        def _(step):
            slot = lax.rem(step, 2)
            score(step, slot, leading, False, True)
            gather(step, slot, leading, False, True)

    for part in every:
        columns = pl.ds(part * rows, rows)
        span_rows = pl.ds(part * block_len, block_len)
        result = (total_ref[:, columns] / sum_ref[:, columns]).T.astype(out_ref.dtype)
        for source in range(sources):
            for at in range(heads):
                row = (source * heads + at) * block_len
                out_ref[span_rows, pl.ds(offsets[source] + at * HEAD_SIZE, HEAD_SIZE)] = result[
                    row : row + block_len
                ]


def attend(q_base, low, spread, kv, place, block_request, block_len, most_blocks, planes):
    tokens, width = q_base.shape
    _, _, rank, _ = spread[0].shape
    window = kv.shape[0]
    head_span = width // KEY_VALUE_HEADS
    lanes = tokens * head_span // HEAD_SIZE
    return pl.pallas_call(
        functools.partial(attend_kernel, block_len, most_blocks, planes),
        out_shape=jax.ShapeDtypeStruct((tokens, width), jnp.bfloat16),
        grid_spec=pltpu.PrefetchScalarGridSpec(
            num_scalar_prefetch=2,
            grid=(KEY_VALUE_HEADS,),
            in_specs=[
                pl.BlockSpec((tokens, head_span), lambda m, me, br: (0, m)),
                pl.BlockSpec((rank, tokens), lambda m, me, br: (0, 0)),
            ]
            + [
                pl.BlockSpec((window, HEAD_SIZE), lambda m, me, br: (0, m)),
                pl.BlockSpec((window, HEAD_SIZE), lambda m, me, br: (0, KEY_VALUE_HEADS + m)),
            ]
            + [pl.BlockSpec(memory_space=pl.ANY)] * len(spread),
            out_specs=pl.BlockSpec((tokens, head_span), lambda m, me, br: (0, m)),
            scratch_shapes=[
                pltpu.VMEM((len(spread), *spread[0].shape), jnp.bfloat16),
                pltpu.VMEM((lanes, HEAD_SIZE), jnp.bfloat16),
                pltpu.VMEM((HEAD_SIZE, lanes), jnp.float32),
                pltpu.VMEM((2, KEY_CHUNK, lanes), jnp.float32),
                pltpu.VMEM((2, 1, lanes), jnp.float32),
                pltpu.VMEM((1, lanes), jnp.float32),
                pltpu.SemaphoreType.DMA((len(spread),)),
            ],
        ),
        cost_estimate=pl.CostEstimate(
            flops=2 * tokens * width * window, bytes_accessed=16 << 20, transcendentals=8 << 20
        ),
        name="attend",
    )(place, block_request, q_base, low, kv, kv, *spread)


def body(
    hidden,
    q_base,
    base_key_weight,
    base_value_weight,
    shrink_a,
    expand_q,
    key_value_up_weight,
    block_request,
    request_adapter,
):
    tokens = hidden.shape[0]
    devices = lax.axis_size("seq")
    me = lax.axis_index("seq")
    place = me.astype(jnp.int32).reshape(1)
    block_count = block_request.shape[0]
    block_len = tokens * devices // block_count
    per_device = tokens // block_len
    most_blocks = min(MOST_BLOCKS_CAP, block_count // 2)
    hops = -(-(most_blocks - 1) // (PLANE * per_device))
    planes = hops + 1
    chips = devices // CORES
    same_core = [[chip * CORES + core for chip in range(chips)] for core in range(CORES)]
    forward = [(i, i + PLANE) for i in range(devices - PLANE)]
    swap_row = [(i, i ^ CORES) for i in range(devices)]
    swap_core = [(i, i ^ 1) for i in range(devices)]

    sent, kv = split(hidden, base_key_weight, base_value_weight, chips)
    half = devices // 2
    near_up = expand_q[request_adapter]
    far_up = lax.ppermute(near_up, "seq", [(i, i ^ half) for i in range(devices)])
    targets = (me ^ jnp.arange(half, dtype=jnp.int32))[:, None] * per_device
    wanted = block_request[targets + jnp.arange(per_device, dtype=jnp.int32)[None, :]]
    picked = jnp.stack([near_up[wanted], far_up[wanted]], axis=1)
    spread = [picked[0]]
    for step in range(1, half):
        spread.append(lax.ppermute(picked[step], "seq", [(i, i ^ step) for i in range(devices)]))
    rows = lax.all_to_all(
        sent, "seq", split_axis=0, concat_axis=0, axis_index_groups=same_core, tiled=True
    )
    down = jnp.swapaxes(shrink_a, 1, 2)
    other_down = lax.ppermute(down, "seq", swap_core)

    pieces = []
    own = kv
    for back in range(planes):
        if back > 0:
            own = lax.ppermute(own, "seq", forward)
        across = lax.ppermute(own, "seq", swap_row)
        flipped = lax.ppermute(own, "seq", swap_core)
        both = lax.ppermute(across, "seq", swap_core)
        pieces += [own, flipped, across, both]

    partials = shrink(rows, down, other_down, place, block_request, request_adapter, block_len)
    received = lax.all_to_all(
        partials, "seq", split_axis=0, concat_axis=0, axis_index_groups=same_core, tiled=True
    )

    low = jnp.sum(received.astype(jnp.float32), axis=0).astype(jnp.bfloat16)
    low_kv = low[ADAPTER_RANK:]
    near = []
    for back in range(planes):
        for flip in (0, CORES):
            if back == 0 and flip == 0:
                near.append(low_kv)
                continue
            pairs = [(i, (i ^ flip) + back * PLANE) for i in range(devices - back * PLANE)]
            near.append(lax.ppermute(low_kv, "seq", pairs))
    near = join(near)
    flipped = lax.ppermute(near, "seq", swap_core)

    window = finish(
        pieces, near, flipped, key_value_up_weight, place, block_request, request_adapter, block_len, planes
    )
    return attend(
        q_base, low[:ADAPTER_RANK], spread, window, place, block_request,
        block_len, most_blocks, planes,
    )


def solution(mesh):
    return jax.shard_map(
        body,
        mesh=mesh,
        in_specs=(
            P(("groups", "seq"), None),
            P(("groups", "seq"), None),
            P(("groups", "seq"), None),
            P(("groups", "seq"), None),
            P("groups", "seq", None),
            P("groups", None, "seq"),
            P("groups", None, None),
            P("groups"),
            P("groups"),
        ),
        out_specs=P(("groups", "seq"), None),
        check_vma=False,
    )
```

```python
import functools
import math

import jax
import jax.numpy as jnp
from jax import lax
from jax.experimental import pallas as pl
from jax.experimental.pallas import tpu as pltpu
from jax.sharding import PartitionSpec as P

KEY_VALUE_HEADS = 8
HEAD_SIZE = 128
ADAPTER_RANK = 64
MOST_BLOCKS_CAP = 32
CORES = 2
PLANE = 4
KEY_CHUNK = 512
KEY_STEP = 512
NT = (((1,), (1,)), ((), ()))
TN = (((0,), (0,)), ((), ()))


def split_kernel(hidden_ref, key_ref, value_ref, sent_ref, kv_ref, rows_ref, both_ref, in_sems, out_sems):
    parts, _, span = rows_ref.shape
    width = key_ref.shape[1]
    fetches = [
        pltpu.make_async_copy(key_ref, both_ref.at[:, pl.ds(0, width)], in_sems.at[parts]),
        pltpu.make_async_copy(value_ref, both_ref.at[:, pl.ds(width, width)], in_sems.at[parts + 1]),
    ]
    fetches += [
        pltpu.make_async_copy(hidden_ref.at[:, pl.ds(i * span, span)], rows_ref.at[i], in_sems.at[i])
        for i in range(parts)
    ]
    for fetch in fetches:
        fetch.start()
    fetches[0].wait()
    fetches[1].wait()
    puts = [pltpu.make_async_copy(both_ref, kv_ref, out_sems.at[parts])]
    puts[0].start()
    for i in range(parts):
        fetches[2 + i].wait()
        put = pltpu.make_async_copy(rows_ref.at[i], sent_ref.at[i], out_sems.at[i])
        put.start()
        puts.append(put)
    for put in puts:
        put.wait()


def split(hidden, base_key, base_value, parts):
    tokens, width = hidden.shape
    span = width // parts
    kv_width = base_key.shape[1]
    return pl.pallas_call(
        split_kernel,
        out_shape=(
            jax.ShapeDtypeStruct((parts, tokens, span), hidden.dtype),
            jax.ShapeDtypeStruct((tokens, 2 * kv_width), hidden.dtype),
        ),
        in_specs=[pl.BlockSpec(memory_space=pl.ANY)] * 3,
        out_specs=(pl.BlockSpec(memory_space=pl.ANY),) * 2,
        scratch_shapes=[
            pltpu.VMEM((parts, tokens, span), hidden.dtype),
            pltpu.VMEM((tokens, 2 * kv_width), hidden.dtype),
            pltpu.SemaphoreType.DMA((parts + 2,)),
            pltpu.SemaphoreType.DMA((parts + 1,)),
        ],
        name="split",
    )(hidden, base_key, base_value)


def shrink_kernel(
    block_len, place_ref, request_ref, adapter_ref, rows_hbm, own_hbm, other_hbm, out_ref,
    rows_ref, down_ref, row_sems, down_sems,
):
    chips, tokens, features = rows_ref.shape
    requests = down_ref.shape[1]
    per_device = tokens // block_len
    half = features // CORES
    core = lax.rem(place_ref[0], CORES)
    downs = []
    for request in range(requests):
        adapter = adapter_ref[request]
        for which, source in enumerate((own_hbm, other_hbm)):
            downs.append(
                pltpu.make_async_copy(
                    source.at[adapter], down_ref.at[which, request], down_sems.at[which, request]
                )
            )
    loads = [pltpu.make_async_copy(rows_hbm.at[i], rows_ref.at[i], row_sems.at[i]) for i in range(chips)]
    loads[0].start()
    for copy in downs:
        copy.start()
    for copy in loads[1:]:
        copy.start()
    for copy in downs:
        copy.wait()
    columns = [
        pl.ds(pl.multiple_of(core * half, half), half),
        pl.ds(pl.multiple_of((1 - core) * half, half), half),
    ]
    for chip in range(chips):
        loads[chip].wait()
        device = chip * CORES + core
        picks = [request_ref[device * per_device + part] for part in range(per_device)]

        def put(request, span):
            total = None
            for which in range(CORES):
                term = lax.dot_general(
                    down_ref[which, request], rows_ref[chip, span, columns[which]], NT,
                    preferred_element_type=jnp.float32,
                )
                total = term if total is None else total + term
            out_ref[chip, :, span] = total.astype(out_ref.dtype)

        shared = picks[0] == picks[-1]

        @pl.when(shared)
        def _():
            put(picks[0], pl.ds(0, tokens))

        @pl.when(jnp.logical_not(shared))
        def _():
            for part in range(per_device):
                put(picks[part], pl.ds(part * block_len, block_len))


def shrink(rows, own, other, place, block_request, request_adapter, block_len):
    chips, tokens, features = rows.shape
    _, width, half = own.shape
    requests = request_adapter.shape[0]
    return pl.pallas_call(
        functools.partial(shrink_kernel, block_len),
        out_shape=jax.ShapeDtypeStruct((chips, width, tokens), jnp.bfloat16),
        grid_spec=pltpu.PrefetchScalarGridSpec(
            num_scalar_prefetch=3,
            grid=(1,),
            in_specs=[pl.BlockSpec(memory_space=pl.ANY)] * 3,
            out_specs=pl.BlockSpec((chips, width, tokens), lambda i, me, br, ra: (0, 0, 0)),
            scratch_shapes=[
                pltpu.VMEM((chips, tokens, features), jnp.bfloat16),
                pltpu.VMEM((CORES, requests, width, half), jnp.bfloat16),
                pltpu.SemaphoreType.DMA((chips,)),
                pltpu.SemaphoreType.DMA((CORES, requests)),
            ],
        ),
        cost_estimate=pl.CostEstimate(
            flops=2 * chips * tokens * features * width,
            bytes_accessed=2 * (rows.size + own.size + other.size),
            transcendentals=0,
        ),
        name="shrink",
    )(place, block_request, request_adapter, rows, own, other)


def join_kernel(*refs):
    for index, ref in enumerate(refs[:-1]):
        refs[-1][index] = ref[...]


def join(parts):
    return pl.pallas_call(
        join_kernel,
        out_shape=jax.ShapeDtypeStruct((len(parts), *parts[0].shape), parts[0].dtype),
        name="join",
    )(*parts)


def finish_kernel(block_len, planes, place_ref, request_ref, adapter_ref, up_ref, *rest):
    pieces = planes * PLANE
    low_refs, rest = rest[:PLANE], rest[PLANE:]
    piece_refs = rest[:pieces]
    out_ref, base_ref, done_ref, in_sems, out_sems = rest[pieces:]
    tokens = piece_refs[0].shape[0]
    per_device = tokens // block_len
    rank = ADAPTER_RANK
    width = base_ref.shape[2] // 2
    me = place_ref[0]
    within = lax.rem(me, PLANE)
    for index in range(pieces):
        pltpu.make_async_copy(piece_refs[index], base_ref.at[index], in_sems.at[index]).start()
    for index in range(pieces):
        back, flip = index // PLANE, index % PLANE
        low_ref = low_refs[flip]
        place = within ^ flip
        pltpu.make_async_copy(piece_refs[index], base_ref.at[index], in_sems.at[index]).wait()
        spans = [(0, tokens)] if index else [(part * block_len, block_len) for part in range(per_device)]
        for part, (at, length) in enumerate(spans):
            adapter = adapter_ref[request_ref[me * per_device + part]]
            span = pl.ds(at, length)
            for which in range(2):
                columns = pl.ds(which * width, width)
                delta = lax.dot_general(
                    low_ref[back, pl.ds(which * rank, rank), span],
                    up_ref[adapter, :, columns],
                    TN,
                    preferred_element_type=jnp.float32,
                )
                done_ref[index, span, columns] = (
                    base_ref[index, span, columns].astype(jnp.float32) + delta
                ).astype(done_ref.dtype)
        slot = (planes - 1 - back) * PLANE + place
        pltpu.make_async_copy(
            done_ref.at[index], out_ref.at[pl.ds(pl.multiple_of(slot * tokens, tokens), tokens), :], out_sems.at[index]
        ).start()
    for index in range(pieces):
        pltpu.make_async_copy(done_ref.at[index], out_ref.at[pl.ds(0, tokens), :], out_sems.at[index]).wait()


def finish(pieces, lows, up_weight, place, block_request, request_adapter, block_len, planes):
    tokens, width = pieces[0].shape
    count = len(pieces)
    return pl.pallas_call(
        functools.partial(finish_kernel, block_len, planes),
        out_shape=jax.ShapeDtypeStruct((count * tokens, width), jnp.bfloat16),
        grid_spec=pltpu.PrefetchScalarGridSpec(
            num_scalar_prefetch=3,
            grid=(1,),
            in_specs=[
                pl.BlockSpec(up_weight.shape, lambda i, me, br, ra: (0, 0, 0)),
            ]
            + [pl.BlockSpec(lows[0].shape, lambda i, me, br, ra: (0, 0, 0))] * PLANE
            + [pl.BlockSpec(memory_space=pl.ANY)] * count,
            out_specs=pl.BlockSpec(memory_space=pl.ANY),
            scratch_shapes=[
                pltpu.VMEM((count, tokens, width), jnp.bfloat16),
                pltpu.VMEM((count, tokens, width), jnp.bfloat16),
                pltpu.SemaphoreType.DMA((count,)),
                pltpu.SemaphoreType.DMA((count,)),
            ],
        ),
        cost_estimate=pl.CostEstimate(
            flops=2 * count * tokens * width * ADAPTER_RANK, bytes_accessed=4 * count * tokens * width, transcendentals=0
        ),
        name="finish",
    )(place, block_request, request_adapter, up_weight, *lows, *pieces)


def attend_kernel(
    block_len, most_blocks, planes, piece, piece_count,
    place_ref, request_ref, q_ref, low_ref, up_ref, key_ref, value_ref, *rest,
):
    done_ref = rest[0] if piece > 0 else None
    out_ref, query_ref, total_ref, score_ref, bias_ref, top_ref, sum_ref = rest[-7:]
    tokens = q_ref.shape[0]
    per_device = tokens // block_len
    me = place_ref[0]
    within = lax.rem(me, PLANE)
    sources = up_ref.shape[0]
    span = up_ref.shape[3]
    heads = span // HEAD_SIZE
    group = sources * heads
    rows = group * block_len
    offsets = [(source * piece_count + piece) * span for source in range(sources)]
    for part in range(per_device):
        own_rows = pl.ds(part * block_len, block_len)
        for source in range(sources):
            columns = pl.ds(offsets[source], span)
            delta = lax.dot_general(
                low_ref[:, own_rows], up_ref[source, part], TN, preferred_element_type=jnp.float32
            )
            query = (q_ref[own_rows, columns].astype(jnp.float32) + delta).astype(jnp.bfloat16)
            for at in range(heads):
                row = part * rows + (source * heads + at) * block_len
                query_ref[pl.ds(row, block_len), :] = query[:, at * HEAD_SIZE : (at + 1) * HEAD_SIZE]

    first_block = me * per_device
    request = request_ref[first_block]
    count = jnp.int32(1)
    for back in range(1, most_blocks):
        earlier = request_ref[jnp.maximum(first_block - back, 0)]
        count = count + ((first_block >= back) & (earlier == request)).astype(jnp.int32)
    window_first = ((planes - 1) * PLANE + within) * per_device
    end = (window_first + per_device) * block_len
    starts = [(window_first - count + 1) * block_len]
    for part in range(1, per_device):
        same = request_ref[first_block + part] == request_ref[first_block + part - 1]
        starts.append(jnp.where(same, starts[-1], (window_first + part) * block_len))
    all_same = request_ref[first_block + per_device - 1] == request
    chunks = lax.div(end - starts[0] + (KEY_CHUNK - 1), KEY_CHUNK)
    factor = math.log2(math.e) / math.sqrt(HEAD_SIZE)

    @pl.when(pl.program_id(0) == 0)
    def _():
        key_at = lax.broadcasted_iota(jnp.int32, (tokens, rows), 0)
        offset = lax.rem(lax.broadcasted_iota(jnp.int32, (tokens, rows), 1), block_len)
        for part in range(per_device):
            bound = starts[part] - (end - tokens)
            allowed = (key_at >= bound) & (key_at <= offset + part * block_len)
            bias_ref[:, pl.ds(part * rows, rows)] = jnp.where(allowed, 0.0, -1e30)

    def score(step, slot, parts, first, masked):
        stop = end - step * KEY_CHUNK
        start = stop - KEY_CHUNK
        if masked:
            start = jnp.maximum(start, 0)
        start = pl.multiple_of(start, block_len)
        sections = [(0, KEY_CHUNK - tokens), (KEY_CHUNK - tokens, tokens)] if first else [(0, KEY_CHUNK)]
        for part in parts:
            columns = pl.ds(part * rows, rows)
            top = None
            for at, length in sections:
                keys = key_ref[pl.ds(start + at, length), :]
                scores = lax.dot_general(keys, query_ref[columns, :], NT, preferred_element_type=jnp.float32)
                if first and at > 0:
                    scores = scores + bias_ref[:, columns]
                elif masked:
                    key_at = start + at + lax.broadcasted_iota(jnp.int32, (length, 1), 0)
                    allowed = (key_at >= starts[part]) & (key_at < stop)
                    scores = jnp.where(allowed, scores, -1e30)
                score_ref[slot, pl.ds(at, length), columns] = scores
                high = jnp.max(scores, axis=0, keepdims=True)
                top = high if top is None else jnp.maximum(top, high)
            if first:
                top_ref[slot, :, columns] = top
            else:
                top_ref[slot, :, columns] = jnp.maximum(top, top_ref[1 - slot, :, columns])

    def gather(step, slot, parts, first, masked):
        stop = end - step * KEY_CHUNK
        start = stop - KEY_CHUNK
        if masked:
            start = jnp.maximum(start, 0)
        start = pl.multiple_of(start, block_len)
        for part in parts:
            columns = pl.ds(part * rows, rows)
            top = top_ref[slot, :, columns]
            sums = None
            product = None
            for at in range(0, KEY_CHUNK, KEY_STEP):
                weights = jnp.exp2((score_ref[slot, pl.ds(at, KEY_STEP), columns] - top) * factor)
                more = jnp.sum(weights, axis=0, keepdims=True)
                values = value_ref[pl.ds(start + at, KEY_STEP), :]
                extra = lax.dot_general(
                    values, weights.astype(jnp.bfloat16), TN, preferred_element_type=jnp.float32
                )
                sums = more if sums is None else sums + more
                product = extra if product is None else product + extra
            if not first:
                fade = jnp.exp2((top_ref[1 - slot, :, columns] - top) * factor)
                sums = sums + sum_ref[:, columns] * fade
                product = product + total_ref[:, columns] * fade
            sum_ref[:, columns] = sums
            total_ref[:, columns] = product

    every = list(range(per_device))
    leading = every[: max(1, per_device - 1)]
    score(0, 0, every, True, True)

    @pl.when(chunks == 1)
    def _():
        gather(0, 0, every, True, True)

    @pl.when((chunks > 1) & all_same)
    def _():
        @pl.when(chunks == 2)
        def _():
            for part in every:
                score(1, 1, [part], False, True)
                gather(0, 0, [part], True, True)

        @pl.when(chunks > 2)
        def _():
            for part in every:
                score(1, 1, [part], False, False)
                gather(0, 0, [part], True, True)

            @pl.loop(2, chunks)
            def _(step):
                slot = lax.rem(step, 2)
                for part in every:
                    score(step, slot, [part], False, True)
                    gather(step - 1, 1 - slot, [part], False, False)

        gather(chunks - 1, lax.rem(chunks - 1, 2), every, False, True)

    @pl.when((chunks > 1) & jnp.logical_not(all_same))
    def _():
        gather(0, 0, every, True, True)

        @pl.loop(1, chunks)
        def _(step):
            slot = lax.rem(step, 2)
            score(step, slot, leading, False, True)
            gather(step, slot, leading, False, True)

    for part in every:
        columns = pl.ds(part * rows, rows)
        span_rows = pl.ds(part * block_len, block_len)
        result = (total_ref[:, columns] / sum_ref[:, columns]).T.astype(out_ref.dtype)
        for source in range(sources):
            for at in range(heads):
                row = (source * heads + at) * block_len
                out_ref[span_rows, pl.ds(offsets[source] + at * HEAD_SIZE, HEAD_SIZE)] = result[
                    row : row + block_len
                ]
    for source in range(sources):
        for other in range(piece):
            columns = pl.ds((source * piece_count + other) * span, span)
            out_ref[:, columns] = done_ref[:, columns]


def attend(q_base, low, up_rows, kv, place, block_request, block_len, most_blocks, planes, piece, piece_count, done):
    tokens, width = q_base.shape
    devices, per_device, rank, span = up_rows.shape
    window = kv.shape[0]
    head_span = width // KEY_VALUE_HEADS
    sources = devices // KEY_VALUE_HEADS
    lanes = tokens * sources * span // HEAD_SIZE
    earlier = [] if done is None else [done]
    return pl.pallas_call(
        functools.partial(attend_kernel, block_len, most_blocks, planes, piece, piece_count),
        out_shape=jax.ShapeDtypeStruct((tokens, width), jnp.bfloat16),
        grid_spec=pltpu.PrefetchScalarGridSpec(
            num_scalar_prefetch=2,
            grid=(KEY_VALUE_HEADS,),
            in_specs=[
                pl.BlockSpec((tokens, head_span), lambda m, me, br: (0, m)),
                pl.BlockSpec((rank, tokens), lambda m, me, br: (0, 0)),
                pl.BlockSpec((sources, per_device, rank, span), lambda m, me, br: (m, 0, 0, 0)),
                pl.BlockSpec((window, HEAD_SIZE), lambda m, me, br: (0, m)),
                pl.BlockSpec((window, HEAD_SIZE), lambda m, me, br: (0, KEY_VALUE_HEADS + m)),
            ]
            + [pl.BlockSpec((tokens, head_span), lambda m, me, br: (0, m))] * len(earlier),
            out_specs=pl.BlockSpec((tokens, head_span), lambda m, me, br: (0, m)),
            scratch_shapes=[
                pltpu.VMEM((lanes, HEAD_SIZE), jnp.bfloat16),
                pltpu.VMEM((HEAD_SIZE, lanes), jnp.float32),
                pltpu.VMEM((2, KEY_CHUNK, lanes), jnp.float32),
                pltpu.VMEM((tokens, lanes), jnp.float32),
                pltpu.VMEM((2, 1, lanes), jnp.float32),
                pltpu.VMEM((1, lanes), jnp.float32),
            ],
        ),
        input_output_aliases={7: 0} if earlier else {},
        cost_estimate=pl.CostEstimate(
            flops=2 * tokens * width * window // piece_count,
            bytes_accessed=(16 << 20) // piece_count,
            transcendentals=(8 << 20) // piece_count,
        ),
        name="attend",
    )(place, block_request, q_base, low, up_rows, kv, kv, *earlier)


def body(
    hidden,
    q_base,
    base_key_weight,
    base_value_weight,
    shrink_a,
    expand_q,
    key_value_up_weight,
    block_request,
    request_adapter,
):
    tokens = hidden.shape[0]
    devices = lax.axis_size("seq")
    me = lax.axis_index("seq")
    place = me.astype(jnp.int32).reshape(1)
    block_count = block_request.shape[0]
    block_len = tokens * devices // block_count
    per_device = tokens // block_len
    most_blocks = min(MOST_BLOCKS_CAP, block_count // 2)
    hops = -(-(most_blocks - 1) // (PLANE * per_device))
    planes = hops + 1
    chips = devices // CORES
    same_core = [[chip * CORES + core for chip in range(chips)] for core in range(CORES)]
    forward = [(i, i + PLANE) for i in range(devices - PLANE)]
    swap_row = [(i, i ^ CORES) for i in range(devices)]
    swap_core = [(i, i ^ 1) for i in range(devices)]

    sent, kv = split(hidden, base_key_weight, base_value_weight, chips)
    rows = lax.all_to_all(
        sent, "seq", split_axis=0, concat_axis=0, axis_index_groups=same_core, tiled=True
    )
    down = jnp.swapaxes(shrink_a, 1, 2)
    other_down = lax.ppermute(down, "seq", swap_core)

    pieces = []
    own = kv
    for back in range(planes):
        if back > 0:
            own = lax.ppermute(own, "seq", forward)
        across = lax.ppermute(own, "seq", swap_row)
        flipped = lax.ppermute(own, "seq", swap_core)
        both = lax.ppermute(across, "seq", swap_core)
        pieces += [own, flipped, across, both]

    partials = shrink(rows, down, other_down, place, block_request, request_adapter, block_len)
    received = lax.all_to_all(
        partials, "seq", split_axis=0, concat_axis=0, axis_index_groups=same_core, tiled=True
    )

    piece_count = 1
    span = expand_q.shape[2] // piece_count
    adapter_of = jnp.sum(
        jnp.where(
            block_request[:, None] == jnp.arange(request_adapter.shape[0], dtype=jnp.int32)[None, :],
            request_adapter[None, :],
            0,
        ),
        axis=1,
    )
    up_pieces = []
    for piece in range(piece_count):
        picked = expand_q[:, :, piece * span : (piece + 1) * span][adapter_of]
        picked = picked.reshape(devices, per_device, ADAPTER_RANK, span)
        up_pieces.append(lax.all_to_all(picked, "seq", split_axis=0, concat_axis=0, tiled=True))

    low = jnp.sum(received.astype(jnp.float32), axis=0).astype(jnp.bfloat16)
    column = [low[ADAPTER_RANK:]]
    for back in range(1, planes):
        pairs = [(i, i + back * PLANE) for i in range(devices - back * PLANE)]
        column.append(lax.ppermute(column[0], "seq", pairs))
    column = join(column)
    across = lax.ppermute(column, "seq", swap_row)
    column_flipped = lax.ppermute(column, "seq", swap_core)
    across_flipped = lax.ppermute(across, "seq", swap_core)
    lows = [column, column_flipped, across, across_flipped]

    window = finish(
        pieces, lows, key_value_up_weight, place, block_request, request_adapter, block_len, planes
    )
    out = None
    for piece in range(piece_count):
        out = attend(
            q_base, low[:ADAPTER_RANK], up_pieces[piece], window, place, block_request,
            block_len, most_blocks, planes, piece, piece_count, out,
        )
    return out


def solution(mesh):
    return jax.shard_map(
        body,
        mesh=mesh,
        in_specs=(
            P(("groups", "seq"), None),
            P(("groups", "seq"), None),
            P(("groups", "seq"), None),
            P(("groups", "seq"), None),
            P("groups", "seq", None),
            P("groups", None, "seq"),
            P("groups", None, None),
            P("groups"),
            P("groups"),
        ),
        out_specs=P(("groups", "seq"), None),
        check_vma=False,
    )
```

```python
import functools
import math

import jax
import jax.numpy as jnp
from jax import lax
from jax.experimental import pallas as pl
from jax.experimental.pallas import tpu as pltpu
from jax.sharding import PartitionSpec as P

KEY_VALUE_HEADS = 8
HEAD_SIZE = 128
ADAPTER_RANK = 64
MOST_BLOCKS_CAP = 32
CORES = 2
PLANE = 4
KEY_CHUNK = 512
KEY_STEP = 512
NT = (((1,), (1,)), ((), ()))
TN = (((0,), (0,)), ((), ()))


def split_kernel(hidden_ref, key_ref, value_ref, sent_ref, kv_ref, rows_ref, both_ref, in_sems, out_sems):
    parts, _, span = rows_ref.shape
    width = key_ref.shape[1]
    fetches = [
        pltpu.make_async_copy(key_ref, both_ref.at[:, pl.ds(0, width)], in_sems.at[parts]),
        pltpu.make_async_copy(value_ref, both_ref.at[:, pl.ds(width, width)], in_sems.at[parts + 1]),
    ]
    fetches += [
        pltpu.make_async_copy(hidden_ref.at[:, pl.ds(i * span, span)], rows_ref.at[i], in_sems.at[i])
        for i in range(parts)
    ]
    for fetch in fetches:
        fetch.start()
    fetches[0].wait()
    fetches[1].wait()
    puts = [pltpu.make_async_copy(both_ref, kv_ref, out_sems.at[parts])]
    puts[0].start()
    for i in range(parts):
        fetches[2 + i].wait()
        put = pltpu.make_async_copy(rows_ref.at[i], sent_ref.at[i], out_sems.at[i])
        put.start()
        puts.append(put)
    for put in puts:
        put.wait()


def split(hidden, base_key, base_value, parts):
    tokens, width = hidden.shape
    span = width // parts
    kv_width = base_key.shape[1]
    return pl.pallas_call(
        split_kernel,
        out_shape=(
            jax.ShapeDtypeStruct((parts, tokens, span), hidden.dtype),
            jax.ShapeDtypeStruct((tokens, 2 * kv_width), hidden.dtype),
        ),
        in_specs=[pl.BlockSpec(memory_space=pl.ANY)] * 3,
        out_specs=(pl.BlockSpec(memory_space=pl.ANY),) * 2,
        scratch_shapes=[
            pltpu.VMEM((parts, tokens, span), hidden.dtype),
            pltpu.VMEM((tokens, 2 * kv_width), hidden.dtype),
            pltpu.SemaphoreType.DMA((parts + 2,)),
            pltpu.SemaphoreType.DMA((parts + 1,)),
        ],
        name="split",
    )(hidden, base_key, base_value)


def shrink_kernel(
    block_len, place_ref, request_ref, adapter_ref, rows_hbm, own_hbm, other_hbm, out_ref,
    rows_ref, down_ref, row_sems, down_sems,
):
    chips, tokens, features = rows_ref.shape
    requests = down_ref.shape[1]
    per_device = tokens // block_len
    half = features // CORES
    core = lax.rem(place_ref[0], CORES)
    downs = []
    for request in range(requests):
        adapter = adapter_ref[request]
        for which, source in enumerate((own_hbm, other_hbm)):
            downs.append(
                pltpu.make_async_copy(
                    source.at[adapter], down_ref.at[which, request], down_sems.at[which, request]
                )
            )
    loads = [pltpu.make_async_copy(rows_hbm.at[i], rows_ref.at[i], row_sems.at[i]) for i in range(chips)]
    loads[0].start()
    for copy in downs:
        copy.start()
    for copy in loads[1:]:
        copy.start()
    for copy in downs:
        copy.wait()
    columns = [
        pl.ds(pl.multiple_of(core * half, half), half),
        pl.ds(pl.multiple_of((1 - core) * half, half), half),
    ]
    for chip in range(chips):
        loads[chip].wait()
        device = chip * CORES + core
        picks = [request_ref[device * per_device + part] for part in range(per_device)]

        def put(request, span):
            total = None
            for which in range(CORES):
                term = lax.dot_general(
                    down_ref[which, request], rows_ref[chip, span, columns[which]], NT,
                    preferred_element_type=jnp.float32,
                )
                total = term if total is None else total + term
            out_ref[chip, :, span] = total.astype(out_ref.dtype)

        shared = picks[0] == picks[-1]

        @pl.when(shared)
        def _():
            put(picks[0], pl.ds(0, tokens))

        @pl.when(jnp.logical_not(shared))
        def _():
            for part in range(per_device):
                put(picks[part], pl.ds(part * block_len, block_len))


def shrink(rows, own, other, place, block_request, request_adapter, block_len):
    chips, tokens, features = rows.shape
    _, width, half = own.shape
    requests = request_adapter.shape[0]
    return pl.pallas_call(
        functools.partial(shrink_kernel, block_len),
        out_shape=jax.ShapeDtypeStruct((chips, width, tokens), jnp.bfloat16),
        grid_spec=pltpu.PrefetchScalarGridSpec(
            num_scalar_prefetch=3,
            grid=(1,),
            in_specs=[pl.BlockSpec(memory_space=pl.ANY)] * 3,
            out_specs=pl.BlockSpec((chips, width, tokens), lambda i, me, br, ra: (0, 0, 0)),
            scratch_shapes=[
                pltpu.VMEM((chips, tokens, features), jnp.bfloat16),
                pltpu.VMEM((CORES, requests, width, half), jnp.bfloat16),
                pltpu.SemaphoreType.DMA((chips,)),
                pltpu.SemaphoreType.DMA((CORES, requests)),
            ],
        ),
        cost_estimate=pl.CostEstimate(
            flops=2 * chips * tokens * features * width,
            bytes_accessed=2 * (rows.size + own.size + other.size),
            transcendentals=0,
        ),
        name="shrink",
    )(place, block_request, request_adapter, rows, own, other)


def join_kernel(*refs):
    for index, ref in enumerate(refs[:-1]):
        refs[-1][index] = ref[...]


def join(parts):
    return pl.pallas_call(
        join_kernel,
        out_shape=jax.ShapeDtypeStruct((len(parts), *parts[0].shape), parts[0].dtype),
        name="join",
    )(*parts)


def finish_kernel(block_len, planes, place_ref, request_ref, adapter_ref, up_ref, *rest):
    pieces = planes * PLANE
    low_refs, rest = rest[:PLANE], rest[PLANE:]
    piece_refs = rest[:pieces]
    out_ref, base_ref, done_ref, in_sems, out_sems = rest[pieces:]
    tokens = piece_refs[0].shape[0]
    per_device = tokens // block_len
    rank = ADAPTER_RANK
    width = base_ref.shape[2] // 2
    me = place_ref[0]
    within = lax.rem(me, PLANE)
    for index in range(pieces):
        pltpu.make_async_copy(piece_refs[index], base_ref.at[index], in_sems.at[index]).start()
    for index in range(pieces):
        back, flip = index // PLANE, index % PLANE
        low_ref = low_refs[flip]
        place = within ^ flip
        pltpu.make_async_copy(piece_refs[index], base_ref.at[index], in_sems.at[index]).wait()
        spans = [(0, tokens)] if index else [(part * block_len, block_len) for part in range(per_device)]
        for part, (at, length) in enumerate(spans):
            adapter = adapter_ref[request_ref[me * per_device + part]]
            span = pl.ds(at, length)
            for which in range(2):
                columns = pl.ds(which * width, width)
                delta = lax.dot_general(
                    low_ref[back, pl.ds(which * rank, rank), span],
                    up_ref[adapter, :, columns],
                    TN,
                    preferred_element_type=jnp.float32,
                )
                done_ref[index, span, columns] = (
                    base_ref[index, span, columns].astype(jnp.float32) + delta
                ).astype(done_ref.dtype)
        slot = (planes - 1 - back) * PLANE + place
        pltpu.make_async_copy(
            done_ref.at[index], out_ref.at[pl.ds(pl.multiple_of(slot * tokens, tokens), tokens), :], out_sems.at[index]
        ).start()
    for index in range(pieces):
        pltpu.make_async_copy(done_ref.at[index], out_ref.at[pl.ds(0, tokens), :], out_sems.at[index]).wait()


def finish(pieces, lows, up_weight, place, block_request, request_adapter, block_len, planes):
    tokens, width = pieces[0].shape
    count = len(pieces)
    return pl.pallas_call(
        functools.partial(finish_kernel, block_len, planes),
        out_shape=jax.ShapeDtypeStruct((count * tokens, width), jnp.bfloat16),
        grid_spec=pltpu.PrefetchScalarGridSpec(
            num_scalar_prefetch=3,
            grid=(1,),
            in_specs=[
                pl.BlockSpec(up_weight.shape, lambda i, me, br, ra: (0, 0, 0)),
            ]
            + [pl.BlockSpec(lows[0].shape, lambda i, me, br, ra: (0, 0, 0))] * PLANE
            + [pl.BlockSpec(memory_space=pl.ANY)] * count,
            out_specs=pl.BlockSpec(memory_space=pl.ANY),
            scratch_shapes=[
                pltpu.VMEM((count, tokens, width), jnp.bfloat16),
                pltpu.VMEM((count, tokens, width), jnp.bfloat16),
                pltpu.SemaphoreType.DMA((count,)),
                pltpu.SemaphoreType.DMA((count,)),
            ],
        ),
        cost_estimate=pl.CostEstimate(
            flops=2 * count * tokens * width * ADAPTER_RANK, bytes_accessed=4 * count * tokens * width, transcendentals=0
        ),
        name="finish",
    )(place, block_request, request_adapter, up_weight, *lows, *pieces)


def attend_kernel(
    block_len, most_blocks, planes, piece, piece_count,
    place_ref, request_ref, q_ref, low_ref, up_ref, key_ref, value_ref, *rest,
):
    done_ref = rest[0] if piece > 0 else None
    out_ref, query_ref, total_ref, score_ref, bias_ref, top_ref, fade_ref, sum_ref = rest[-8:]
    tokens = q_ref.shape[0]
    per_device = tokens // block_len
    me = place_ref[0]
    within = lax.rem(me, PLANE)
    sources = up_ref.shape[0]
    span = up_ref.shape[3]
    heads = span // HEAD_SIZE
    group = sources * heads
    rows = group * block_len
    offsets = [(source * piece_count + piece) * span for source in range(sources)]
    for part in range(per_device):
        own_rows = pl.ds(part * block_len, block_len)
        for source in range(sources):
            columns = pl.ds(offsets[source], span)
            delta = lax.dot_general(
                low_ref[:, own_rows], up_ref[source, part], TN, preferred_element_type=jnp.float32
            )
            query = (q_ref[own_rows, columns].astype(jnp.float32) + delta).astype(jnp.bfloat16)
            for at in range(heads):
                row = part * rows + (source * heads + at) * block_len
                query_ref[pl.ds(row, block_len), :] = query[:, at * HEAD_SIZE : (at + 1) * HEAD_SIZE]

    first_block = me * per_device
    request = request_ref[first_block]
    count = jnp.int32(1)
    for back in range(1, most_blocks):
        earlier = request_ref[jnp.maximum(first_block - back, 0)]
        count = count + ((first_block >= back) & (earlier == request)).astype(jnp.int32)
    window_first = ((planes - 1) * PLANE + within) * per_device
    end = (window_first + per_device) * block_len
    starts = [(window_first - count + 1) * block_len]
    for part in range(1, per_device):
        same = request_ref[first_block + part] == request_ref[first_block + part - 1]
        starts.append(jnp.where(same, starts[-1], (window_first + part) * block_len))
    all_same = request_ref[first_block + per_device - 1] == request
    chunks = lax.div(end - starts[0] + (KEY_CHUNK - 1), KEY_CHUNK)
    factor = math.log2(math.e) / math.sqrt(HEAD_SIZE)

    @pl.when(pl.program_id(0) == 0)
    def _():
        key_at = lax.broadcasted_iota(jnp.int32, (tokens, rows), 0)
        offset = lax.rem(lax.broadcasted_iota(jnp.int32, (tokens, rows), 1), block_len)
        for part in range(per_device):
            bound = starts[part] - (end - tokens)
            allowed = (key_at >= bound) & (key_at <= offset + part * block_len)
            bias_ref[:, pl.ds(part * rows, rows)] = jnp.where(allowed, 0.0, -1e30)

    def score(step, slot, parts, first, masked):
        stop = end - step * KEY_CHUNK
        start = stop - KEY_CHUNK
        if masked:
            start = jnp.maximum(start, 0)
        start = pl.multiple_of(start, block_len)
        sections = [(0, KEY_CHUNK - tokens), (KEY_CHUNK - tokens, tokens)] if first else [(0, KEY_CHUNK)]
        for part in parts:
            columns = pl.ds(part * rows, rows)
            top = None
            for at, length in sections:
                keys = key_ref[pl.ds(start + at, length), :]
                scores = lax.dot_general(keys, query_ref[columns, :], NT, preferred_element_type=jnp.float32)
                if first and at > 0:
                    scores = scores + bias_ref[:, columns]
                elif masked:
                    key_at = start + at + lax.broadcasted_iota(jnp.int32, (length, 1), 0)
                    allowed = (key_at >= starts[part]) & (key_at < stop)
                    scores = jnp.where(allowed, scores, -1e30)
                score_ref[slot, pl.ds(at, length), columns] = scores
                high = jnp.max(scores, axis=0, keepdims=True)
                top = high if top is None else jnp.maximum(top, high)
            if first:
                top_ref[slot, :, columns] = top
            else:
                before = top_ref[1 - slot, :, columns]
                top = jnp.maximum(top, before)
                top_ref[slot, :, columns] = top
                fade_ref[slot, :, columns] = jnp.exp2((before - top) * factor)

    def gather(step, slot, parts, first, masked):
        stop = end - step * KEY_CHUNK
        start = stop - KEY_CHUNK
        if masked:
            start = jnp.maximum(start, 0)
        start = pl.multiple_of(start, block_len)
        for part in parts:
            columns = pl.ds(part * rows, rows)
            top = top_ref[slot, :, columns]
            sums = None
            product = None
            for at in range(0, KEY_CHUNK, KEY_STEP):
                weights = jnp.exp2((score_ref[slot, pl.ds(at, KEY_STEP), columns] - top) * factor)
                more = jnp.sum(weights, axis=0, keepdims=True)
                values = value_ref[pl.ds(start + at, KEY_STEP), :]
                extra = lax.dot_general(
                    values, weights.astype(jnp.bfloat16), TN, preferred_element_type=jnp.float32
                )
                sums = more if sums is None else sums + more
                product = extra if product is None else product + extra
            if not first:
                fade = fade_ref[slot, :, columns]
                sums = sums + sum_ref[:, columns] * fade
                product = product + total_ref[:, columns] * fade
            sum_ref[:, columns] = sums
            total_ref[:, columns] = product

    every = list(range(per_device))
    leading = every[: max(1, per_device - 1)]
    score(0, 0, every, True, True)

    @pl.when(chunks == 1)
    def _():
        gather(0, 0, every, True, True)

    @pl.when((chunks > 1) & all_same)
    def _():
        @pl.when(chunks == 2)
        def _():
            for part in every:
                score(1, 1, [part], False, True)
                gather(0, 0, [part], True, True)

        @pl.when(chunks > 2)
        def _():
            for part in every:
                score(1, 1, [part], False, False)
                gather(0, 0, [part], True, True)

            @pl.loop(2, chunks)
            def _(step):
                slot = lax.rem(step, 2)
                for part in every:
                    score(step, slot, [part], False, True)
                    gather(step - 1, 1 - slot, [part], False, False)

        gather(chunks - 1, lax.rem(chunks - 1, 2), every, False, True)

    @pl.when((chunks > 1) & jnp.logical_not(all_same))
    def _():
        score(1, 1, leading, False, True)
        gather(0, 0, every, True, True)

        @pl.loop(2, chunks)
        def _(step):
            slot = lax.rem(step, 2)
            score(step, slot, leading, False, True)
            gather(step - 1, 1 - slot, leading, False, True)

        gather(chunks - 1, lax.rem(chunks - 1, 2), leading, False, True)

    for part in every:
        columns = pl.ds(part * rows, rows)
        span_rows = pl.ds(part * block_len, block_len)
        result = (total_ref[:, columns] / sum_ref[:, columns]).T.astype(out_ref.dtype)
        for source in range(sources):
            for at in range(heads):
                row = (source * heads + at) * block_len
                out_ref[span_rows, pl.ds(offsets[source] + at * HEAD_SIZE, HEAD_SIZE)] = result[
                    row : row + block_len
                ]
    for source in range(sources):
        for other in range(piece):
            columns = pl.ds((source * piece_count + other) * span, span)
            out_ref[:, columns] = done_ref[:, columns]


def attend(q_base, low, up_rows, kv, place, block_request, block_len, most_blocks, planes, piece, piece_count, done):
    tokens, width = q_base.shape
    devices, per_device, rank, span = up_rows.shape
    window = kv.shape[0]
    head_span = width // KEY_VALUE_HEADS
    sources = devices // KEY_VALUE_HEADS
    lanes = tokens * sources * span // HEAD_SIZE
    earlier = [] if done is None else [done]
    return pl.pallas_call(
        functools.partial(attend_kernel, block_len, most_blocks, planes, piece, piece_count),
        out_shape=jax.ShapeDtypeStruct((tokens, width), jnp.bfloat16),
        grid_spec=pltpu.PrefetchScalarGridSpec(
            num_scalar_prefetch=2,
            grid=(KEY_VALUE_HEADS,),
            in_specs=[
                pl.BlockSpec((tokens, head_span), lambda m, me, br: (0, m)),
                pl.BlockSpec((rank, tokens), lambda m, me, br: (0, 0)),
                pl.BlockSpec((sources, per_device, rank, span), lambda m, me, br: (m, 0, 0, 0)),
                pl.BlockSpec((window, HEAD_SIZE), lambda m, me, br: (0, m)),
                pl.BlockSpec((window, HEAD_SIZE), lambda m, me, br: (0, KEY_VALUE_HEADS + m)),
            ]
            + [pl.BlockSpec((tokens, head_span), lambda m, me, br: (0, m))] * len(earlier),
            out_specs=pl.BlockSpec((tokens, head_span), lambda m, me, br: (0, m)),
            scratch_shapes=[
                pltpu.VMEM((lanes, HEAD_SIZE), jnp.bfloat16),
                pltpu.VMEM((HEAD_SIZE, lanes), jnp.float32),
                pltpu.VMEM((2, KEY_CHUNK, lanes), jnp.float32),
                pltpu.VMEM((tokens, lanes), jnp.float32),
                pltpu.VMEM((2, 1, lanes), jnp.float32),
                pltpu.VMEM((2, 1, lanes), jnp.float32),
                pltpu.VMEM((1, lanes), jnp.float32),
            ],
        ),
        input_output_aliases={7: 0} if earlier else {},
        cost_estimate=pl.CostEstimate(
            flops=2 * tokens * width * window // piece_count,
            bytes_accessed=(16 << 20) // piece_count,
            transcendentals=(8 << 20) // piece_count,
        ),
        name="attend",
    )(place, block_request, q_base, low, up_rows, kv, kv, *earlier)


def body(
    hidden,
    q_base,
    base_key_weight,
    base_value_weight,
    shrink_a,
    expand_q,
    key_value_up_weight,
    block_request,
    request_adapter,
):
    tokens = hidden.shape[0]
    devices = lax.axis_size("seq")
    me = lax.axis_index("seq")
    place = me.astype(jnp.int32).reshape(1)
    block_count = block_request.shape[0]
    block_len = tokens * devices // block_count
    per_device = tokens // block_len
    most_blocks = min(MOST_BLOCKS_CAP, block_count // 2)
    hops = -(-(most_blocks - 1) // (PLANE * per_device))
    planes = hops + 1
    chips = devices // CORES
    same_core = [[chip * CORES + core for chip in range(chips)] for core in range(CORES)]
    forward = [(i, i + PLANE) for i in range(devices - PLANE)]
    swap_row = [(i, i ^ CORES) for i in range(devices)]
    swap_core = [(i, i ^ 1) for i in range(devices)]

    sent, kv = split(hidden, base_key_weight, base_value_weight, chips)
    rows = lax.all_to_all(
        sent, "seq", split_axis=0, concat_axis=0, axis_index_groups=same_core, tiled=True
    )
    down = jnp.swapaxes(shrink_a, 1, 2)
    other_down = lax.ppermute(down, "seq", swap_core)

    pieces = []
    own = kv
    for back in range(planes):
        if back > 0:
            own = lax.ppermute(own, "seq", forward)
        across = lax.ppermute(own, "seq", swap_row)
        flipped = lax.ppermute(own, "seq", swap_core)
        both = lax.ppermute(across, "seq", swap_core)
        pieces += [own, flipped, across, both]

    partials = shrink(rows, down, other_down, place, block_request, request_adapter, block_len)
    received = lax.all_to_all(
        partials, "seq", split_axis=0, concat_axis=0, axis_index_groups=same_core, tiled=True
    )

    piece_count = 1
    span = expand_q.shape[2] // piece_count
    adapter_of = jnp.sum(
        jnp.where(
            block_request[:, None] == jnp.arange(request_adapter.shape[0], dtype=jnp.int32)[None, :],
            request_adapter[None, :],
            0,
        ),
        axis=1,
    )
    up_pieces = []
    for piece in range(piece_count):
        picked = expand_q[:, :, piece * span : (piece + 1) * span][adapter_of]
        picked = picked.reshape(devices, per_device, ADAPTER_RANK, span)
        up_pieces.append(lax.all_to_all(picked, "seq", split_axis=0, concat_axis=0, tiled=True))

    low = jnp.sum(received.astype(jnp.float32), axis=0).astype(jnp.bfloat16)
    column = [low[ADAPTER_RANK:]]
    for back in range(1, planes):
        pairs = [(i, i + back * PLANE) for i in range(devices - back * PLANE)]
        column.append(lax.ppermute(column[0], "seq", pairs))
    column = join(column)
    across = lax.ppermute(column, "seq", swap_row)
    column_flipped = lax.ppermute(column, "seq", swap_core)
    across_flipped = lax.ppermute(across, "seq", swap_core)
    lows = [column, column_flipped, across, across_flipped]

    window = finish(
        pieces, lows, key_value_up_weight, place, block_request, request_adapter, block_len, planes
    )
    out = None
    for piece in range(piece_count):
        out = attend(
            q_base, low[:ADAPTER_RANK], up_pieces[piece], window, place, block_request,
            block_len, most_blocks, planes, piece, piece_count, out,
        )
    return out


def solution(mesh):
    return jax.shard_map(
        body,
        mesh=mesh,
        in_specs=(
            P(("groups", "seq"), None),
            P(("groups", "seq"), None),
            P(("groups", "seq"), None),
            P(("groups", "seq"), None),
            P("groups", "seq", None),
            P("groups", None, "seq"),
            P("groups", None, None),
            P("groups"),
            P("groups"),
        ),
        out_specs=P(("groups", "seq"), None),
        check_vma=False,
    )
```

```python
import functools
import math

import jax
import jax.numpy as jnp
from jax import lax
from jax.experimental import pallas as pl
from jax.experimental.pallas import tpu as pltpu
from jax.sharding import PartitionSpec as P

KEY_VALUE_HEADS = 8
HEAD_SIZE = 128
ADAPTER_RANK = 64
MOST_BLOCKS_CAP = 32
CORES = 2
PLANE = 4
KEY_CHUNK = 512
KEY_STEP = 512
NT = (((1,), (1,)), ((), ()))
TN = (((0,), (0,)), ((), ()))


def split_kernel(hidden_ref, key_ref, value_ref, sent_ref, kv_ref, rows_ref, both_ref, in_sems, out_sems):
    parts, _, span = rows_ref.shape
    width = key_ref.shape[1]
    fetches = [
        pltpu.make_async_copy(key_ref, both_ref.at[:, pl.ds(0, width)], in_sems.at[parts]),
        pltpu.make_async_copy(value_ref, both_ref.at[:, pl.ds(width, width)], in_sems.at[parts + 1]),
    ]
    fetches += [
        pltpu.make_async_copy(hidden_ref.at[:, pl.ds(i * span, span)], rows_ref.at[i], in_sems.at[i])
        for i in range(parts)
    ]
    for fetch in fetches:
        fetch.start()
    fetches[0].wait()
    fetches[1].wait()
    puts = [pltpu.make_async_copy(both_ref, kv_ref, out_sems.at[parts])]
    puts[0].start()
    for i in range(parts):
        fetches[2 + i].wait()
        put = pltpu.make_async_copy(rows_ref.at[i], sent_ref.at[i], out_sems.at[i])
        put.start()
        puts.append(put)
    for put in puts:
        put.wait()


def split(hidden, base_key, base_value, parts):
    tokens, width = hidden.shape
    span = width // parts
    kv_width = base_key.shape[1]
    return pl.pallas_call(
        split_kernel,
        out_shape=(
            jax.ShapeDtypeStruct((parts, tokens, span), hidden.dtype),
            jax.ShapeDtypeStruct((tokens, 2 * kv_width), hidden.dtype),
        ),
        in_specs=[pl.BlockSpec(memory_space=pl.ANY)] * 3,
        out_specs=(pl.BlockSpec(memory_space=pl.ANY),) * 2,
        scratch_shapes=[
            pltpu.VMEM((parts, tokens, span), hidden.dtype),
            pltpu.VMEM((tokens, 2 * kv_width), hidden.dtype),
            pltpu.SemaphoreType.DMA((parts + 2,)),
            pltpu.SemaphoreType.DMA((parts + 1,)),
        ],
        name="split",
    )(hidden, base_key, base_value)


def shrink_kernel(
    block_len, place_ref, request_ref, adapter_ref, rows_ref, own_hbm, other_hbm, out_ref,
    down_ref, down_sems,
):
    chips, tokens, features = rows_ref.shape
    requests = down_ref.shape[1]
    per_device = tokens // block_len
    half = features // CORES
    core = lax.rem(place_ref[0], CORES)
    downs = []
    for request in range(requests):
        adapter = adapter_ref[request]
        for which, source in enumerate((own_hbm, other_hbm)):
            downs.append(
                pltpu.make_async_copy(
                    source.at[adapter], down_ref.at[which, request], down_sems.at[which, request]
                )
            )
    for copy in downs:
        copy.start()
    for copy in downs:
        copy.wait()
    columns = [
        pl.ds(pl.multiple_of(core * half, half), half),
        pl.ds(pl.multiple_of((1 - core) * half, half), half),
    ]
    for chip in range(chips):
        device = chip * CORES + core
        picks = [request_ref[device * per_device + part] for part in range(per_device)]

        def put(request, span):
            total = None
            for which in range(CORES):
                term = lax.dot_general(
                    down_ref[which, request], rows_ref[chip, span, columns[which]], NT,
                    preferred_element_type=jnp.float32,
                )
                total = term if total is None else total + term
            out_ref[chip, :, span] = total.astype(out_ref.dtype)

        shared = picks[0] == picks[-1]

        @pl.when(shared)
        def _():
            put(picks[0], pl.ds(0, tokens))

        @pl.when(jnp.logical_not(shared))
        def _():
            for part in range(per_device):
                put(picks[part], pl.ds(part * block_len, block_len))


def shrink(rows, own, other, place, block_request, request_adapter, block_len):
    chips, tokens, features = rows.shape
    _, width, half = own.shape
    requests = request_adapter.shape[0]
    return pl.pallas_call(
        functools.partial(shrink_kernel, block_len),
        out_shape=jax.ShapeDtypeStruct((chips, width, tokens), jnp.bfloat16),
        grid_spec=pltpu.PrefetchScalarGridSpec(
            num_scalar_prefetch=3,
            grid=(1,),
            in_specs=[pl.BlockSpec(memory_space=pltpu.VMEM)] + [pl.BlockSpec(memory_space=pl.ANY)] * 2,
            out_specs=pl.BlockSpec((chips, width, tokens), lambda i, me, br, ra: (0, 0, 0)),
            scratch_shapes=[
                pltpu.VMEM((CORES, requests, width, half), jnp.bfloat16),
                pltpu.SemaphoreType.DMA((CORES, requests)),
            ],
        ),
        cost_estimate=pl.CostEstimate(
            flops=2 * chips * tokens * features * width,
            bytes_accessed=2 * (rows.size + own.size + other.size),
            transcendentals=0,
        ),
        name="shrink",
    )(place, block_request, request_adapter, rows, own, other)


def join_kernel(*refs):
    for index, ref in enumerate(refs[:-1]):
        refs[-1][index] = ref[...]


def join(parts):
    return pl.pallas_call(
        join_kernel,
        out_shape=jax.ShapeDtypeStruct((len(parts), *parts[0].shape), parts[0].dtype),
        name="join",
    )(*parts)


def finish_kernel(block_len, planes, place_ref, request_ref, adapter_ref, up_ref, *rest):
    pieces = planes * PLANE
    low_refs, rest = rest[:PLANE], rest[PLANE:]
    piece_refs = rest[:pieces]
    out_ref, base_ref, done_ref, in_sems, out_sems = rest[pieces:]
    tokens = piece_refs[0].shape[0]
    per_device = tokens // block_len
    rank = ADAPTER_RANK
    width = base_ref.shape[2] // 2
    me = place_ref[0]
    within = lax.rem(me, PLANE)
    for index in range(pieces):
        pltpu.make_async_copy(piece_refs[index], base_ref.at[index], in_sems.at[index]).start()
    for index in range(pieces):
        back, flip = index // PLANE, index % PLANE
        low_ref = low_refs[flip]
        place = within ^ flip
        pltpu.make_async_copy(piece_refs[index], base_ref.at[index], in_sems.at[index]).wait()
        spans = [(0, tokens)] if index else [(part * block_len, block_len) for part in range(per_device)]
        for part, (at, length) in enumerate(spans):
            adapter = adapter_ref[request_ref[me * per_device + part]]
            span = pl.ds(at, length)
            for which in range(2):
                columns = pl.ds(which * width, width)
                delta = lax.dot_general(
                    low_ref[back, pl.ds(which * rank, rank), span],
                    up_ref[adapter, :, columns],
                    TN,
                    preferred_element_type=jnp.float32,
                )
                done_ref[index, span, columns] = (
                    base_ref[index, span, columns].astype(jnp.float32) + delta
                ).astype(done_ref.dtype)
        slot = (planes - 1 - back) * PLANE + place
        pltpu.make_async_copy(
            done_ref.at[index], out_ref.at[pl.ds(pl.multiple_of(slot * tokens, tokens), tokens), :], out_sems.at[index]
        ).start()
    for index in range(pieces):
        pltpu.make_async_copy(done_ref.at[index], out_ref.at[pl.ds(0, tokens), :], out_sems.at[index]).wait()


def finish(pieces, lows, up_weight, place, block_request, request_adapter, block_len, planes):
    tokens, width = pieces[0].shape
    count = len(pieces)
    return pl.pallas_call(
        functools.partial(finish_kernel, block_len, planes),
        out_shape=jax.ShapeDtypeStruct((count * tokens, width), jnp.bfloat16),
        grid_spec=pltpu.PrefetchScalarGridSpec(
            num_scalar_prefetch=3,
            grid=(1,),
            in_specs=[
                pl.BlockSpec(up_weight.shape, lambda i, me, br, ra: (0, 0, 0)),
            ]
            + [pl.BlockSpec(lows[0].shape, lambda i, me, br, ra: (0, 0, 0))] * PLANE
            + [pl.BlockSpec(memory_space=pl.ANY)] * count,
            out_specs=pl.BlockSpec(memory_space=pl.ANY),
            scratch_shapes=[
                pltpu.VMEM((count, tokens, width), jnp.bfloat16),
                pltpu.VMEM((count, tokens, width), jnp.bfloat16),
                pltpu.SemaphoreType.DMA((count,)),
                pltpu.SemaphoreType.DMA((count,)),
            ],
        ),
        cost_estimate=pl.CostEstimate(
            flops=2 * count * tokens * width * ADAPTER_RANK, bytes_accessed=4 * count * tokens * width, transcendentals=0
        ),
        name="finish",
    )(place, block_request, request_adapter, up_weight, *lows, *pieces)


def attend_kernel(
    block_len, most_blocks, planes, piece, piece_count,
    place_ref, request_ref, q_ref, low_ref, up_ref, key_ref, value_ref, *rest,
):
    done_ref = rest[0] if piece > 0 else None
    out_ref, query_ref, total_ref, score_ref, bias_ref, top_ref, fade_ref, sum_ref = rest[-8:]
    tokens = q_ref.shape[0]
    per_device = tokens // block_len
    me = place_ref[0]
    within = lax.rem(me, PLANE)
    span = up_ref.shape[3]
    sources = up_ref.shape[0] // pl.num_programs(0)
    heads = span // HEAD_SIZE
    group = sources * heads
    rows = group * block_len
    offsets = [(source * piece_count + piece) * span for source in range(sources)]
    for part in range(per_device):
        own_rows = pl.ds(part * block_len, block_len)
        for source in range(sources):
            columns = pl.ds(offsets[source], span)
            delta = lax.dot_general(
                low_ref[:, own_rows], up_ref[pl.program_id(0) * sources + source, part], TN, preferred_element_type=jnp.float32
            )
            query = (q_ref[own_rows, columns].astype(jnp.float32) + delta).astype(jnp.bfloat16)
            for at in range(heads):
                row = part * rows + (source * heads + at) * block_len
                query_ref[pl.ds(row, block_len), :] = query[:, at * HEAD_SIZE : (at + 1) * HEAD_SIZE]

    first_block = me * per_device
    request = request_ref[first_block]
    count = jnp.int32(1)
    for back in range(1, most_blocks):
        earlier = request_ref[jnp.maximum(first_block - back, 0)]
        count = count + ((first_block >= back) & (earlier == request)).astype(jnp.int32)
    window_first = ((planes - 1) * PLANE + within) * per_device
    end = (window_first + per_device) * block_len
    starts = [(window_first - count + 1) * block_len]
    for part in range(1, per_device):
        same = request_ref[first_block + part] == request_ref[first_block + part - 1]
        starts.append(jnp.where(same, starts[-1], (window_first + part) * block_len))
    all_same = request_ref[first_block + per_device - 1] == request
    chunks = lax.div(end - starts[0] + (KEY_CHUNK - 1), KEY_CHUNK)
    factor = math.log2(math.e) / math.sqrt(HEAD_SIZE)

    @pl.when(pl.program_id(0) == 0)
    def _():
        key_at = lax.broadcasted_iota(jnp.int32, (tokens, rows), 0)
        offset = lax.rem(lax.broadcasted_iota(jnp.int32, (tokens, rows), 1), block_len)
        for part in range(per_device):
            bound = starts[part] - (end - tokens)
            allowed = (key_at >= bound) & (key_at <= offset + part * block_len)
            bias_ref[:, pl.ds(part * rows, rows)] = jnp.where(allowed, 0.0, -1e30)

    def score(step, slot, parts, first, masked):
        stop = end - step * KEY_CHUNK
        start = stop - KEY_CHUNK
        if masked:
            start = jnp.maximum(start, 0)
        start = pl.multiple_of(start, block_len)
        sections = [(0, KEY_CHUNK - tokens), (KEY_CHUNK - tokens, tokens)] if first else [(0, KEY_CHUNK)]
        for part in parts:
            columns = pl.ds(part * rows, rows)
            top = None
            for at, length in sections:
                keys = key_ref[pl.ds(start + at, length), :]
                scores = lax.dot_general(keys, query_ref[columns, :], NT, preferred_element_type=jnp.float32)
                if first and at > 0:
                    scores = scores + bias_ref[:, columns]
                elif masked:
                    key_at = start + at + lax.broadcasted_iota(jnp.int32, (length, 1), 0)
                    allowed = (key_at >= starts[part]) & (key_at < stop)
                    scores = jnp.where(allowed, scores, -1e30)
                score_ref[slot, pl.ds(at, length), columns] = scores
                high = jnp.max(scores, axis=0, keepdims=True)
                top = high if top is None else jnp.maximum(top, high)
            if first:
                top_ref[slot, :, columns] = top
            else:
                before = top_ref[1 - slot, :, columns]
                top = jnp.maximum(top, before)
                top_ref[slot, :, columns] = top
                fade_ref[slot, :, columns] = jnp.exp2((before - top) * factor)

    def gather(step, slot, parts, first, masked):
        stop = end - step * KEY_CHUNK
        start = stop - KEY_CHUNK
        if masked:
            start = jnp.maximum(start, 0)
        start = pl.multiple_of(start, block_len)
        for part in parts:
            columns = pl.ds(part * rows, rows)
            top = top_ref[slot, :, columns]
            sums = None
            product = None
            for at in range(0, KEY_CHUNK, KEY_STEP):
                weights = jnp.exp2((score_ref[slot, pl.ds(at, KEY_STEP), columns] - top) * factor)
                more = jnp.sum(weights, axis=0, keepdims=True)
                values = value_ref[pl.ds(start + at, KEY_STEP), :]
                extra = lax.dot_general(
                    values, weights.astype(jnp.bfloat16), TN, preferred_element_type=jnp.float32
                )
                sums = more if sums is None else sums + more
                product = extra if product is None else product + extra
            if not first:
                fade = fade_ref[slot, :, columns]
                sums = sums + sum_ref[:, columns] * fade
                product = product + total_ref[:, columns] * fade
            sum_ref[:, columns] = sums
            total_ref[:, columns] = product

    every = list(range(per_device))
    leading = every[: max(1, per_device - 1)]
    score(0, 0, every, True, True)

    @pl.when(chunks == 1)
    def _():
        gather(0, 0, every, True, True)

    @pl.when((chunks > 1) & all_same)
    def _():
        @pl.when(chunks == 2)
        def _():
            for part in every:
                score(1, 1, [part], False, True)
                gather(0, 0, [part], True, True)

        @pl.when(chunks > 2)
        def _():
            for part in every:
                score(1, 1, [part], False, False)
                gather(0, 0, [part], True, True)

            @pl.loop(2, chunks)
            def _(step):
                slot = lax.rem(step, 2)
                for part in every:
                    score(step, slot, [part], False, True)
                    gather(step - 1, 1 - slot, [part], False, False)

        gather(chunks - 1, lax.rem(chunks - 1, 2), every, False, True)

    @pl.when((chunks > 1) & jnp.logical_not(all_same))
    def _():
        score(1, 1, leading, False, True)
        gather(0, 0, every, True, True)

        @pl.loop(2, chunks)
        def _(step):
            slot = lax.rem(step, 2)
            score(step, slot, leading, False, True)
            gather(step - 1, 1 - slot, leading, False, True)

        gather(chunks - 1, lax.rem(chunks - 1, 2), leading, False, True)

    for part in every:
        columns = pl.ds(part * rows, rows)
        span_rows = pl.ds(part * block_len, block_len)
        result = (total_ref[:, columns] / sum_ref[:, columns]).T.astype(out_ref.dtype)
        for source in range(sources):
            for at in range(heads):
                row = (source * heads + at) * block_len
                out_ref[span_rows, pl.ds(offsets[source] + at * HEAD_SIZE, HEAD_SIZE)] = result[
                    row : row + block_len
                ]
    for source in range(sources):
        for other in range(piece):
            columns = pl.ds((source * piece_count + other) * span, span)
            out_ref[:, columns] = done_ref[:, columns]


def attend(q_base, low, up_rows, kv, place, block_request, block_len, most_blocks, planes, piece, piece_count, done):
    tokens, width = q_base.shape
    devices, _, rank, span = up_rows.shape
    window = kv.shape[0]
    head_span = width // KEY_VALUE_HEADS
    sources = devices // KEY_VALUE_HEADS
    lanes = tokens * sources * span // HEAD_SIZE
    earlier = [] if done is None else [done]
    return pl.pallas_call(
        functools.partial(attend_kernel, block_len, most_blocks, planes, piece, piece_count),
        out_shape=jax.ShapeDtypeStruct((tokens, width), jnp.bfloat16),
        grid_spec=pltpu.PrefetchScalarGridSpec(
            num_scalar_prefetch=2,
            grid=(KEY_VALUE_HEADS,),
            in_specs=[
                pl.BlockSpec((tokens, head_span), lambda m, me, br: (0, m)),
                pl.BlockSpec((rank, tokens), lambda m, me, br: (0, 0)),
                pl.BlockSpec(memory_space=pltpu.VMEM),
                pl.BlockSpec((window, HEAD_SIZE), lambda m, me, br: (0, m)),
                pl.BlockSpec((window, HEAD_SIZE), lambda m, me, br: (0, KEY_VALUE_HEADS + m)),
            ]
            + [pl.BlockSpec((tokens, head_span), lambda m, me, br: (0, m))] * len(earlier),
            out_specs=pl.BlockSpec((tokens, head_span), lambda m, me, br: (0, m)),
            scratch_shapes=[
                pltpu.VMEM((lanes, HEAD_SIZE), jnp.bfloat16),
                pltpu.VMEM((HEAD_SIZE, lanes), jnp.float32),
                pltpu.VMEM((2, KEY_CHUNK, lanes), jnp.float32),
                pltpu.VMEM((tokens, lanes), jnp.float32),
                pltpu.VMEM((2, 1, lanes), jnp.float32),
                pltpu.VMEM((2, 1, lanes), jnp.float32),
                pltpu.VMEM((1, lanes), jnp.float32),
            ],
        ),
        input_output_aliases={7: 0} if earlier else {},
        cost_estimate=pl.CostEstimate(
            flops=2 * tokens * width * window // piece_count,
            bytes_accessed=(16 << 20) // piece_count,
            transcendentals=(8 << 20) // piece_count,
        ),
        name="attend",
    )(place, block_request, q_base, low, up_rows, kv, kv, *earlier)


def body(
    hidden,
    q_base,
    base_key_weight,
    base_value_weight,
    shrink_a,
    expand_q,
    key_value_up_weight,
    block_request,
    request_adapter,
):
    tokens = hidden.shape[0]
    devices = lax.axis_size("seq")
    me = lax.axis_index("seq")
    place = me.astype(jnp.int32).reshape(1)
    block_count = block_request.shape[0]
    block_len = tokens * devices // block_count
    per_device = tokens // block_len
    most_blocks = min(MOST_BLOCKS_CAP, block_count // 2)
    hops = -(-(most_blocks - 1) // (PLANE * per_device))
    planes = hops + 1
    chips = devices // CORES
    same_core = [[chip * CORES + core for chip in range(chips)] for core in range(CORES)]
    forward = [(i, i + PLANE) for i in range(devices - PLANE)]
    swap_row = [(i, i ^ CORES) for i in range(devices)]
    swap_core = [(i, i ^ 1) for i in range(devices)]

    sent, kv = split(hidden, base_key_weight, base_value_weight, chips)
    rows = lax.all_to_all(
        sent, "seq", split_axis=0, concat_axis=0, axis_index_groups=same_core, tiled=True
    )
    rows = pltpu.with_memory_space_constraint(rows, pltpu.VMEM)
    down = jnp.swapaxes(shrink_a, 1, 2)
    other_down = lax.ppermute(down, "seq", swap_core)

    pieces = []
    own = kv
    for back in range(planes):
        if back > 0:
            own = lax.ppermute(own, "seq", forward)
        across = lax.ppermute(own, "seq", swap_row)
        flipped = lax.ppermute(own, "seq", swap_core)
        both = lax.ppermute(across, "seq", swap_core)
        pieces += [own, flipped, across, both]

    partials = shrink(rows, down, other_down, place, block_request, request_adapter, block_len)
    received = lax.all_to_all(
        partials, "seq", split_axis=0, concat_axis=0, axis_index_groups=same_core, tiled=True
    )

    piece_count = 1
    span = expand_q.shape[2] // piece_count
    adapter_of = jnp.sum(
        jnp.where(
            block_request[:, None] == jnp.arange(request_adapter.shape[0], dtype=jnp.int32)[None, :],
            request_adapter[None, :],
            0,
        ),
        axis=1,
    )
    up_pieces = []
    for piece in range(piece_count):
        picked = expand_q[:, :, piece * span : (piece + 1) * span][adapter_of]
        picked = picked.reshape(devices, per_device, ADAPTER_RANK, span)
        received_up = lax.all_to_all(picked, "seq", split_axis=0, concat_axis=0, tiled=True)
        up_pieces.append(pltpu.with_memory_space_constraint(received_up, pltpu.VMEM))

    low = jnp.sum(received.astype(jnp.float32), axis=0).astype(jnp.bfloat16)
    column = [low[ADAPTER_RANK:]]
    for back in range(1, planes):
        pairs = [(i, i + back * PLANE) for i in range(devices - back * PLANE)]
        column.append(lax.ppermute(column[0], "seq", pairs))
    column = join(column)
    across = lax.ppermute(column, "seq", swap_row)
    column_flipped = lax.ppermute(column, "seq", swap_core)
    across_flipped = lax.ppermute(across, "seq", swap_core)
    lows = [column, column_flipped, across, across_flipped]

    window = finish(
        pieces, lows, key_value_up_weight, place, block_request, request_adapter, block_len, planes
    )
    out = None
    for piece in range(piece_count):
        out = attend(
            q_base, low[:ADAPTER_RANK], up_pieces[piece], window, place, block_request,
            block_len, most_blocks, planes, piece, piece_count, out,
        )
    return out


def solution(mesh):
    return jax.shard_map(
        body,
        mesh=mesh,
        in_specs=(
            P(("groups", "seq"), None),
            P(("groups", "seq"), None),
            P(("groups", "seq"), None),
            P(("groups", "seq"), None),
            P("groups", "seq", None),
            P("groups", None, "seq"),
            P("groups", None, None),
            P("groups"),
            P("groups"),
        ),
        out_specs=P(("groups", "seq"), None),
        check_vma=False,
    )
```

```python
import functools
import math

import jax
import jax.numpy as jnp
from jax import lax
from jax.experimental import pallas as pl
from jax.experimental.pallas import tpu as pltpu
from jax.sharding import PartitionSpec as P

KEY_VALUE_HEADS = 8
HEAD_SIZE = 128
ADAPTER_RANK = 64
MOST_BLOCKS_CAP = 32
CORES = 2
PLANE = 4
KEY_CHUNK = 512
KEY_STEP = 512
NT = (((1,), (1,)), ((), ()))
TN = (((0,), (0,)), ((), ()))


def split_kernel(hidden_ref, key_ref, value_ref, sent_ref, kv_ref, rows_ref, both_ref, in_sems, out_sems):
    parts, _, span = rows_ref.shape
    width = key_ref.shape[1]
    fetches = [
        pltpu.make_async_copy(key_ref, both_ref.at[:, pl.ds(0, width)], in_sems.at[parts]),
        pltpu.make_async_copy(value_ref, both_ref.at[:, pl.ds(width, width)], in_sems.at[parts + 1]),
    ]
    fetches += [
        pltpu.make_async_copy(hidden_ref.at[:, pl.ds(i * span, span)], rows_ref.at[i], in_sems.at[i])
        for i in range(parts)
    ]
    for fetch in fetches:
        fetch.start()
    fetches[0].wait()
    fetches[1].wait()
    puts = [pltpu.make_async_copy(both_ref, kv_ref, out_sems.at[parts])]
    puts[0].start()
    for i in range(parts):
        fetches[2 + i].wait()
        put = pltpu.make_async_copy(rows_ref.at[i], sent_ref.at[i], out_sems.at[i])
        put.start()
        puts.append(put)
    for put in puts:
        put.wait()


def split(hidden, base_key, base_value, parts):
    tokens, width = hidden.shape
    span = width // parts
    kv_width = base_key.shape[1]
    return pl.pallas_call(
        split_kernel,
        out_shape=(
            jax.ShapeDtypeStruct((parts, tokens, span), hidden.dtype),
            jax.ShapeDtypeStruct((tokens, 2 * kv_width), hidden.dtype),
        ),
        in_specs=[pl.BlockSpec(memory_space=pl.ANY)] * 3,
        out_specs=(pl.BlockSpec(memory_space=pl.ANY),) * 2,
        scratch_shapes=[
            pltpu.VMEM((parts, tokens, span), hidden.dtype),
            pltpu.VMEM((tokens, 2 * kv_width), hidden.dtype),
            pltpu.SemaphoreType.DMA((parts + 2,)),
            pltpu.SemaphoreType.DMA((parts + 1,)),
        ],
        name="split",
    )(hidden, base_key, base_value)


def shrink_kernel(
    block_len, place_ref, request_ref, adapter_ref, rows_ref, own_hbm, other_hbm, out_ref,
    down_ref, down_sems,
):
    chips, tokens, features = rows_ref.shape
    requests = down_ref.shape[1]
    per_device = tokens // block_len
    half = features // CORES
    core = lax.rem(place_ref[0], CORES)
    downs = []
    for request in range(requests):
        adapter = adapter_ref[request]
        for which, source in enumerate((own_hbm, other_hbm)):
            downs.append(
                pltpu.make_async_copy(
                    source.at[adapter], down_ref.at[which, request], down_sems.at[which, request]
                )
            )
    for copy in downs:
        copy.start()
    for copy in downs:
        copy.wait()
    columns = [
        pl.ds(pl.multiple_of(core * half, half), half),
        pl.ds(pl.multiple_of((1 - core) * half, half), half),
    ]
    for chip in range(chips):
        device = chip * CORES + core
        picks = [request_ref[device * per_device + part] for part in range(per_device)]

        def put(request, span):
            total = None
            for which in range(CORES):
                term = lax.dot_general(
                    down_ref[which, request], rows_ref[chip, span, columns[which]], NT,
                    preferred_element_type=jnp.float32,
                )
                total = term if total is None else total + term
            out_ref[chip, :, span] = total.astype(out_ref.dtype)

        shared = picks[0] == picks[-1]

        @pl.when(shared)
        def _():
            put(picks[0], pl.ds(0, tokens))

        @pl.when(jnp.logical_not(shared))
        def _():
            for part in range(per_device):
                put(picks[part], pl.ds(part * block_len, block_len))


def shrink(rows, own, other, place, block_request, request_adapter, block_len):
    chips, tokens, features = rows.shape
    _, width, half = own.shape
    requests = request_adapter.shape[0]
    return pl.pallas_call(
        functools.partial(shrink_kernel, block_len),
        out_shape=jax.ShapeDtypeStruct((chips, width, tokens), jnp.bfloat16),
        grid_spec=pltpu.PrefetchScalarGridSpec(
            num_scalar_prefetch=3,
            grid=(1,),
            in_specs=[pl.BlockSpec(memory_space=pltpu.VMEM)] + [pl.BlockSpec(memory_space=pl.ANY)] * 2,
            out_specs=pl.BlockSpec((chips, width, tokens), lambda i, me, br, ra: (0, 0, 0)),
            scratch_shapes=[
                pltpu.VMEM((CORES, requests, width, half), jnp.bfloat16),
                pltpu.SemaphoreType.DMA((CORES, requests)),
            ],
        ),
        cost_estimate=pl.CostEstimate(
            flops=2 * chips * tokens * features * width,
            bytes_accessed=2 * (rows.size + own.size + other.size),
            transcendentals=0,
        ),
        name="shrink",
    )(place, block_request, request_adapter, rows, own, other)


def join_kernel(*refs):
    for index, ref in enumerate(refs[:-1]):
        refs[-1][index] = ref[...]


def join(parts):
    return pl.pallas_call(
        join_kernel,
        out_shape=jax.ShapeDtypeStruct((len(parts), *parts[0].shape), parts[0].dtype),
        name="join",
    )(*parts)


def finish_kernel(block_len, planes, per_device, place_ref, request_ref, adapter_ref, *rest):
    pieces = planes * PLANE
    up_refs, rest = rest[:per_device], rest[per_device:]
    low_refs, rest = rest[:PLANE], rest[PLANE:]
    piece_refs = rest[:pieces]
    out_ref, base_ref, done_ref, in_sems, out_sems = rest[pieces:]
    tokens = piece_refs[0].shape[0]
    rank = ADAPTER_RANK
    width = base_ref.shape[2] // 2
    me = place_ref[0]
    within = lax.rem(me, PLANE)
    for index in range(pieces):
        pltpu.make_async_copy(piece_refs[index], base_ref.at[index], in_sems.at[index]).start()
    for index in range(pieces):
        back, flip = index // PLANE, index % PLANE
        low_ref = low_refs[flip]
        place = within ^ flip
        pltpu.make_async_copy(piece_refs[index], base_ref.at[index], in_sems.at[index]).wait()
        spans = [(0, tokens)] if index else [(part * block_len, block_len) for part in range(per_device)]
        for part, (at, length) in enumerate(spans):
            span = pl.ds(at, length)
            for which in range(2):
                columns = pl.ds(which * width, width)
                delta = lax.dot_general(
                    low_ref[back, pl.ds(which * rank, rank), span],
                    up_refs[part][0, :, columns],
                    TN,
                    preferred_element_type=jnp.float32,
                )
                done_ref[index, span, columns] = (
                    base_ref[index, span, columns].astype(jnp.float32) + delta
                ).astype(done_ref.dtype)
        slot = (planes - 1 - back) * PLANE + place
        pltpu.make_async_copy(
            done_ref.at[index], out_ref.at[pl.ds(pl.multiple_of(slot * tokens, tokens), tokens), :], out_sems.at[index]
        ).start()
    for index in range(pieces):
        pltpu.make_async_copy(done_ref.at[index], out_ref.at[pl.ds(0, tokens), :], out_sems.at[index]).wait()


def finish(pieces, lows, up_weight, place, block_request, request_adapter, block_len, planes):
    tokens, width = pieces[0].shape
    count = len(pieces)
    return pl.pallas_call(
        functools.partial(finish_kernel, block_len, planes, tokens // block_len),
        out_shape=jax.ShapeDtypeStruct((count * tokens, width), jnp.bfloat16),
        grid_spec=pltpu.PrefetchScalarGridSpec(
            num_scalar_prefetch=3,
            grid=(1,),
            in_specs=[
                pl.BlockSpec(
                    (1, ADAPTER_RANK, width),
                    lambda i, me, br, ra, part=part: (ra[br[me[0] * (tokens // block_len) + part]], 0, 0),
                )
                for part in range(tokens // block_len)
            ]
            + [pl.BlockSpec(lows[0].shape, lambda i, me, br, ra: (0, 0, 0))] * PLANE
            + [pl.BlockSpec(memory_space=pl.ANY)] * count,
            out_specs=pl.BlockSpec(memory_space=pl.ANY),
            scratch_shapes=[
                pltpu.VMEM((count, tokens, width), jnp.bfloat16),
                pltpu.VMEM((count, tokens, width), jnp.bfloat16),
                pltpu.SemaphoreType.DMA((count,)),
                pltpu.SemaphoreType.DMA((count,)),
            ],
        ),
        cost_estimate=pl.CostEstimate(
            flops=2 * count * tokens * width * ADAPTER_RANK, bytes_accessed=4 * count * tokens * width, transcendentals=0
        ),
        name="finish",
    )(place, block_request, request_adapter, *[up_weight] * (tokens // block_len), *lows, *pieces)


def attend_kernel(
    block_len, most_blocks, planes, piece, piece_count,
    place_ref, request_ref, q_ref, low_ref, up_ref, key_ref, value_ref, *rest,
):
    done_ref = rest[0] if piece > 0 else None
    out_ref, query_ref, total_ref, score_ref, bias_ref, top_ref, fade_ref, sum_ref = rest[-8:]
    tokens = q_ref.shape[0]
    per_device = tokens // block_len
    me = place_ref[0]
    within = lax.rem(me, PLANE)
    span = up_ref.shape[3]
    sources = up_ref.shape[0] // pl.num_programs(0)
    heads = span // HEAD_SIZE
    group = sources * heads
    rows = group * block_len
    offsets = [(source * piece_count + piece) * span for source in range(sources)]
    for part in range(per_device):
        own_rows = pl.ds(part * block_len, block_len)
        for source in range(sources):
            columns = pl.ds(offsets[source], span)
            delta = lax.dot_general(
                low_ref[:, own_rows], up_ref[pl.program_id(0) * sources + source, part], TN, preferred_element_type=jnp.float32
            )
            query = (q_ref[own_rows, columns].astype(jnp.float32) + delta).astype(jnp.bfloat16)
            for at in range(heads):
                row = part * rows + (source * heads + at) * block_len
                query_ref[pl.ds(row, block_len), :] = query[:, at * HEAD_SIZE : (at + 1) * HEAD_SIZE]

    first_block = me * per_device
    request = request_ref[first_block]
    count = jnp.int32(1)
    for back in range(1, most_blocks):
        earlier = request_ref[jnp.maximum(first_block - back, 0)]
        count = count + ((first_block >= back) & (earlier == request)).astype(jnp.int32)
    window_first = ((planes - 1) * PLANE + within) * per_device
    end = (window_first + per_device) * block_len
    starts = [(window_first - count + 1) * block_len]
    for part in range(1, per_device):
        same = request_ref[first_block + part] == request_ref[first_block + part - 1]
        starts.append(jnp.where(same, starts[-1], (window_first + part) * block_len))
    all_same = request_ref[first_block + per_device - 1] == request
    chunks = lax.div(end - starts[0] + (KEY_CHUNK - 1), KEY_CHUNK)
    factor = math.log2(math.e) / math.sqrt(HEAD_SIZE)

    @pl.when(pl.program_id(0) == 0)
    def _():
        key_at = lax.broadcasted_iota(jnp.int32, (tokens, rows), 0)
        offset = lax.rem(lax.broadcasted_iota(jnp.int32, (tokens, rows), 1), block_len)
        for part in range(per_device):
            bound = starts[part] - (end - tokens)
            allowed = (key_at >= bound) & (key_at <= offset + part * block_len)
            bias_ref[:, pl.ds(part * rows, rows)] = jnp.where(allowed, 0.0, -1e30)

    def score(step, slot, parts, first, masked):
        stop = end - step * KEY_CHUNK
        start = stop - KEY_CHUNK
        if masked:
            start = jnp.maximum(start, 0)
        start = pl.multiple_of(start, block_len)
        sections = [(0, KEY_CHUNK - tokens), (KEY_CHUNK - tokens, tokens)] if first else [(0, KEY_CHUNK)]
        for part in parts:
            columns = pl.ds(part * rows, rows)
            top = None
            for at, length in sections:
                keys = key_ref[pl.ds(start + at, length), :]
                scores = lax.dot_general(keys, query_ref[columns, :], NT, preferred_element_type=jnp.float32)
                if first and at > 0:
                    scores = scores + bias_ref[:, columns]
                elif masked:
                    key_at = start + at + lax.broadcasted_iota(jnp.int32, (length, 1), 0)
                    allowed = (key_at >= starts[part]) & (key_at < stop)
                    scores = jnp.where(allowed, scores, -1e30)
                score_ref[slot, pl.ds(at, length), columns] = scores
                high = jnp.max(scores, axis=0, keepdims=True)
                top = high if top is None else jnp.maximum(top, high)
            if first:
                top_ref[slot, :, columns] = top
            else:
                before = top_ref[1 - slot, :, columns]
                top = jnp.maximum(top, before)
                top_ref[slot, :, columns] = top
                fade_ref[slot, :, columns] = jnp.exp2((before - top) * factor)

    def gather(step, slot, parts, first, masked):
        stop = end - step * KEY_CHUNK
        start = stop - KEY_CHUNK
        if masked:
            start = jnp.maximum(start, 0)
        start = pl.multiple_of(start, block_len)
        for part in parts:
            columns = pl.ds(part * rows, rows)
            top = top_ref[slot, :, columns]
            sums = None
            product = None
            for at in range(0, KEY_CHUNK, KEY_STEP):
                weights = jnp.exp2((score_ref[slot, pl.ds(at, KEY_STEP), columns] - top) * factor)
                more = jnp.sum(weights, axis=0, keepdims=True)
                values = value_ref[pl.ds(start + at, KEY_STEP), :]
                extra = lax.dot_general(
                    values, weights.astype(jnp.bfloat16), TN, preferred_element_type=jnp.float32
                )
                sums = more if sums is None else sums + more
                product = extra if product is None else product + extra
            if not first:
                fade = fade_ref[slot, :, columns]
                sums = sums + sum_ref[:, columns] * fade
                product = product + total_ref[:, columns] * fade
            sum_ref[:, columns] = sums
            total_ref[:, columns] = product

    every = list(range(per_device))
    leading = every[: max(1, per_device - 1)]
    score(0, 0, every, True, True)

    @pl.when(chunks == 1)
    def _():
        gather(0, 0, every, True, True)

    @pl.when((chunks > 1) & all_same)
    def _():
        @pl.when(chunks == 2)
        def _():
            for part in every:
                score(1, 1, [part], False, True)
                gather(0, 0, [part], True, True)

        @pl.when(chunks > 2)
        def _():
            for part in every:
                score(1, 1, [part], False, False)
                gather(0, 0, [part], True, True)

            @pl.loop(2, chunks)
            def _(step):
                slot = lax.rem(step, 2)
                for part in every:
                    score(step, slot, [part], False, True)
                    gather(step - 1, 1 - slot, [part], False, False)

        gather(chunks - 1, lax.rem(chunks - 1, 2), every, False, True)

    @pl.when((chunks > 1) & jnp.logical_not(all_same))
    def _():
        score(1, 1, leading, False, True)
        gather(0, 0, every, True, True)

        @pl.loop(2, chunks)
        def _(step):
            slot = lax.rem(step, 2)
            score(step, slot, leading, False, True)
            gather(step - 1, 1 - slot, leading, False, True)

        gather(chunks - 1, lax.rem(chunks - 1, 2), leading, False, True)

    for part in every:
        columns = pl.ds(part * rows, rows)
        span_rows = pl.ds(part * block_len, block_len)
        result = (total_ref[:, columns] / sum_ref[:, columns]).T.astype(out_ref.dtype)
        for source in range(sources):
            for at in range(heads):
                row = (source * heads + at) * block_len
                out_ref[span_rows, pl.ds(offsets[source] + at * HEAD_SIZE, HEAD_SIZE)] = result[
                    row : row + block_len
                ]
    for source in range(sources):
        for other in range(piece):
            columns = pl.ds((source * piece_count + other) * span, span)
            out_ref[:, columns] = done_ref[:, columns]


def attend(q_base, low, up_rows, kv, place, block_request, block_len, most_blocks, planes, piece, piece_count, done):
    tokens, width = q_base.shape
    devices, _, rank, span = up_rows.shape
    window = kv.shape[0]
    head_span = width // KEY_VALUE_HEADS
    sources = devices // KEY_VALUE_HEADS
    lanes = tokens * sources * span // HEAD_SIZE
    earlier = [] if done is None else [done]
    return pl.pallas_call(
        functools.partial(attend_kernel, block_len, most_blocks, planes, piece, piece_count),
        out_shape=jax.ShapeDtypeStruct((tokens, width), jnp.bfloat16),
        grid_spec=pltpu.PrefetchScalarGridSpec(
            num_scalar_prefetch=2,
            grid=(KEY_VALUE_HEADS,),
            in_specs=[
                pl.BlockSpec((tokens, head_span), lambda m, me, br: (0, m)),
                pl.BlockSpec((rank, tokens), lambda m, me, br: (0, 0)),
                pl.BlockSpec(memory_space=pltpu.VMEM),
                pl.BlockSpec((window, HEAD_SIZE), lambda m, me, br: (0, m)),
                pl.BlockSpec((window, HEAD_SIZE), lambda m, me, br: (0, KEY_VALUE_HEADS + m)),
            ]
            + [pl.BlockSpec((tokens, head_span), lambda m, me, br: (0, m))] * len(earlier),
            out_specs=pl.BlockSpec((tokens, head_span), lambda m, me, br: (0, m)),
            scratch_shapes=[
                pltpu.VMEM((lanes, HEAD_SIZE), jnp.bfloat16),
                pltpu.VMEM((HEAD_SIZE, lanes), jnp.float32),
                pltpu.VMEM((2, KEY_CHUNK, lanes), jnp.float32),
                pltpu.VMEM((tokens, lanes), jnp.float32),
                pltpu.VMEM((2, 1, lanes), jnp.float32),
                pltpu.VMEM((2, 1, lanes), jnp.float32),
                pltpu.VMEM((1, lanes), jnp.float32),
            ],
        ),
        input_output_aliases={7: 0} if earlier else {},
        cost_estimate=pl.CostEstimate(
            flops=2 * tokens * width * window // piece_count,
            bytes_accessed=(16 << 20) // piece_count,
            transcendentals=(8 << 20) // piece_count,
        ),
        name="attend",
    )(place, block_request, q_base, low, up_rows, kv, kv, *earlier)


def body(
    hidden,
    q_base,
    base_key_weight,
    base_value_weight,
    shrink_a,
    expand_q,
    key_value_up_weight,
    block_request,
    request_adapter,
):
    tokens = hidden.shape[0]
    devices = lax.axis_size("seq")
    me = lax.axis_index("seq")
    place = me.astype(jnp.int32).reshape(1)
    block_count = block_request.shape[0]
    block_len = tokens * devices // block_count
    per_device = tokens // block_len
    most_blocks = min(MOST_BLOCKS_CAP, block_count // 2)
    hops = -(-(most_blocks - 1) // (PLANE * per_device))
    planes = hops + 1
    chips = devices // CORES
    same_core = [[chip * CORES + core for chip in range(chips)] for core in range(CORES)]
    forward = [(i, i + PLANE) for i in range(devices - PLANE)]
    swap_row = [(i, i ^ CORES) for i in range(devices)]
    swap_core = [(i, i ^ 1) for i in range(devices)]

    sent, kv = split(hidden, base_key_weight, base_value_weight, chips)
    rows = lax.all_to_all(
        sent, "seq", split_axis=0, concat_axis=0, axis_index_groups=same_core, tiled=True
    )
    rows = pltpu.with_memory_space_constraint(rows, pltpu.VMEM)
    down = jnp.swapaxes(shrink_a, 1, 2)
    other_down = lax.ppermute(down, "seq", swap_core)

    pieces = []
    own = kv
    for back in range(planes):
        if back > 0:
            own = lax.ppermute(own, "seq", forward)
        across = lax.ppermute(own, "seq", swap_row)
        flipped = lax.ppermute(own, "seq", swap_core)
        both = lax.ppermute(across, "seq", swap_core)
        pieces += [own, flipped, across, both]

    partials = shrink(rows, down, other_down, place, block_request, request_adapter, block_len)
    received = lax.all_to_all(
        partials, "seq", split_axis=0, concat_axis=0, axis_index_groups=same_core, tiled=True
    )

    piece_count = 1
    span = expand_q.shape[2] // piece_count
    adapter_of = jnp.sum(
        jnp.where(
            block_request[:, None] == jnp.arange(request_adapter.shape[0], dtype=jnp.int32)[None, :],
            request_adapter[None, :],
            0,
        ),
        axis=1,
    )
    up_pieces = []
    for piece in range(piece_count):
        picked = expand_q[:, :, piece * span : (piece + 1) * span][adapter_of]
        picked = picked.reshape(devices, per_device, ADAPTER_RANK, span)
        received_up = lax.all_to_all(picked, "seq", split_axis=0, concat_axis=0, tiled=True)
        up_pieces.append(pltpu.with_memory_space_constraint(received_up, pltpu.VMEM))

    low = jnp.sum(received.astype(jnp.float32), axis=0).astype(jnp.bfloat16)
    column = [low[ADAPTER_RANK:]]
    for back in range(1, planes):
        pairs = [(i, i + back * PLANE) for i in range(devices - back * PLANE)]
        column.append(lax.ppermute(column[0], "seq", pairs))
    column = join(column)
    across = lax.ppermute(column, "seq", swap_row)
    column_flipped = lax.ppermute(column, "seq", swap_core)
    across_flipped = lax.ppermute(across, "seq", swap_core)
    lows = [column, column_flipped, across, across_flipped]

    window = finish(
        pieces, lows, key_value_up_weight, place, block_request, request_adapter, block_len, planes
    )
    out = None
    for piece in range(piece_count):
        out = attend(
            q_base, low[:ADAPTER_RANK], up_pieces[piece], window, place, block_request,
            block_len, most_blocks, planes, piece, piece_count, out,
        )
    return out


def solution(mesh):
    return jax.shard_map(
        body,
        mesh=mesh,
        in_specs=(
            P(("groups", "seq"), None),
            P(("groups", "seq"), None),
            P(("groups", "seq"), None),
            P(("groups", "seq"), None),
            P("groups", "seq", None),
            P("groups", None, "seq"),
            P("groups", None, None),
            P("groups"),
            P("groups"),
        ),
        out_specs=P(("groups", "seq"), None),
        check_vma=False,
    )
```
